32 devices in a mesh: rep: 2 (over x), ctx: 16 (over z, y, core).
Axes of the slice: x: 2, y: 2, z: 4, core: 2. Of those that a mesh axis runs over, the one named last changes fastest.
Arguments:
- queries: bfloat16 [4096, 12288], P(('rep', 'ctx')), parts along dimension 0, may hold values from -8 to 8
- latents: bfloat16 [512, 576], P(('rep', 'ctx')), parts along dimension 0, may hold values from -8 to 8
- w_key: bfloat16 [64, 512, 128], P('ctx'), may hold values from -0.25 to 0.25
- w_value: bfloat16 [64, 512, 128], P('ctx'), may hold values from -0.25 to 0.25
Outputs:
- attended: bfloat16 [4096, 8192], P(('rep', 'ctx')), parts along dimension 0
The draws below stay inside these ranges and needn't reach their ends.
There are 2 independent parts, one for each index of `rep`. The reference program is written for one: setup_inputs(seed, part) draws one part's arguments, and reference() takes and returns one part's arrays. A program takes and returns all parts, laid end to end along the dimension named above; an argument that names none is the same for every part. Nothing has to cross between parts.
All inputs are finite; a program needn't handle non-finite values.
Results may differ from the reference program's by a relative error of at most 0.0067.
Values may be sent and summed in bfloat16 or wider, within the bound.
A program may use at most 128 MiB of HBM per device.

```python
import jax
import jax.numpy as jnp
from jax import lax

DLAT = 512
DROPE = 64
DNOPE = 128
DV = 128
H = 64
QUERIES = 2048
CACHE = 256


def draw_queries(key, part):
    qk_width = DNOPE + DROPE
    value_key = jax.random.fold_in(key, 11)
    values_all = jnp.clip(2.5 * jax.random.normal(value_key, (QUERIES, H, qk_width), jnp.float32), -8.0, 8.0)
    return values_all.reshape(QUERIES, H * qk_width).astype(jnp.bfloat16)


def draw_latents(key, part):
    value_key = jax.random.fold_in(key, 12)
    values_all = jnp.clip(jax.random.normal(value_key, (CACHE, DLAT + DROPE), jnp.float32), -8.0, 8.0)
    return values_all.astype(jnp.bfloat16)


def block_levels(rng, dims, cuts, smallest, top_value):
    factor_of = 1.0
    for position, blocks in cuts:
        steps = jax.random.uniform(jax.random.fold_in(jax.random.fold_in(rng, 6), position), (blocks,), jnp.float32, smallest / len(cuts), top_value / len(cuts))
        factor_of = factor_of * jnp.repeat(jnp.exp(steps), dims[position] // blocks).reshape((-1,) + (1,) * (len(dims) - 1 - position))
    return factor_of


def scatter_about(own_key, shape, width, reach, pieces=(), held_as=jnp.bfloat16):
    entries = width * jax.random.normal(own_key, shape, jnp.float32)
    if pieces:
        entries = entries * block_levels(own_key, shape, pieces, -0.22, 0.18)
    return jnp.clip(entries, -reach, reach).astype(held_as)


def setup_inputs(seed: int = 0, part: int = 0) -> dict:
    arg_keys = jax.random.split(jax.random.key(seed), 5)
    own_keys = jax.random.split(jax.random.fold_in(arg_keys[4], part), 5)
    return {
        "queries": draw_queries(jax.random.fold_in(jax.random.fold_in(arg_keys[4], part), 71), part),
        "latents": draw_latents(jax.random.fold_in(jax.random.fold_in(arg_keys[4], part), 71), part),
        "w_key": scatter_about(arg_keys[2], (H, DLAT, DNOPE), DLAT ** -0.5, 0.25, ((0, 16),)),
        "w_value": scatter_about(arg_keys[3], (H, DLAT, DV), DLAT ** -0.5, 0.25, ((0, 16),)),
    }


def reference(queries, latents, w_key, w_value):
    query_count = queries.shape[0]
    qk_width = DNOPE + DROPE
    shaped = queries.reshape(query_count, H, qk_width)
    latent_part = latents[:, :DLAT].astype(jnp.float32)
    rope_part = latents[:, DLAT:]
    score_scale = 1.0 / (qk_width ** 0.5)

    def per_head(head_index):
        key_proj = w_key[head_index].astype(jnp.float32)
        value_proj = w_value[head_index].astype(jnp.float32)
        keys_nope = jnp.dot(latent_part, key_proj).astype(jnp.bfloat16)
        values_head = jnp.dot(latent_part, value_proj).astype(jnp.bfloat16)
        keys_nope = lax.optimization_barrier(keys_nope)
        values_head = lax.optimization_barrier(values_head)
        keys_full = jnp.concatenate([keys_nope, rope_part], axis=1).astype(jnp.float32)
        query_head = shaped[:, head_index, :].astype(jnp.float32)
        scores = jnp.dot(query_head, keys_full.T) * score_scale
        row_max = jnp.max(scores, axis=1)
        weights = jnp.exp(scores - row_max[:, None])
        total = jnp.sum(weights, axis=1)
        rounded = lax.optimization_barrier(weights.astype(jnp.bfloat16))
        mixed = jnp.dot(rounded.astype(jnp.float32), values_head.astype(jnp.float32))
        return (mixed / total[:, None]).astype(jnp.bfloat16)

    per_heads = lax.map(per_head, jnp.arange(H, dtype=jnp.int32))
    return jnp.transpose(per_heads, (1, 0, 2)).reshape(query_count, H * DV)
```

```python
import functools
import math

import jax
import jax.numpy as jnp
from jax import lax
from jax.experimental import pallas as pl
from jax.experimental.pallas import tpu as pltpu
from jax.sharding import PartitionSpec as P

MESH = pl.DeviceIdType.MESH


def kernel(
    grid_y,
    cores,
    early,
    q_hbm,
    lat_hbm,
    wk_hbm,
    wv_hbm,
    o,
    q,
    lat,
    wkv,
    ropes,
    kv,
    halves,
    load_sem,
    lat_recv,
    kv_recv,
    half_recv,
    send_sem,
):
    devices = lat.shape[0]
    heads = wkv.shape[0]
    rows = kv.shape[2]
    nope = kv.shape[3]
    width = wkv.shape[1]
    rope = lat.shape[2] - width
    qk = nope + rope
    chips = devices // cores
    grid_z = chips // grid_y
    half = chips // 2
    scale = math.log2(math.e) / math.sqrt(qk)

    half_right = (heads + 1) // 2
    late = list(range(early, heads))
    order_r = []
    for i in range(max(len(late), early)):
        order_r += late[i : i + 1]
        if i < early:
            order_r.append(i)
    order_l = order_r[half_right:] + order_r[:half_right]

    me = lax.axis_index("ctx")
    core = lax.rem(me, cores)
    my_chip = me // cores
    my_y = lax.rem(my_chip, grid_y)
    my_z = my_chip // grid_y
    place = (1 - my_y) * my_z + my_y * (2 * grid_z - 1 - my_z)

    def device_at(spot, which):
        spot = lax.rem(spot + 2 * chips, chips)
        y = spot // grid_z
        z = (1 - y) * spot + y * (2 * grid_z - 1 - spot)
        return (z * grid_y + y) * cores + which

    other_core = cores - 1 - core
    across = my_chip * cores + other_core
    right = device_at(place + 1, core)
    left = device_at(place - 1, core)
    rep = lax.axis_index("rep")

    q_copy = pltpu.make_async_copy(q_hbm, q, load_sem.at[0])
    lat_copy = pltpu.make_async_copy(lat_hbm, lat.at[me], load_sem.at[1])
    lat_copy.start()
    for j in range(heads):
        pltpu.make_async_copy(wk_hbm.at[j], wkv.at[j, :, pl.ds(0, nope)], load_sem.at[2]).start()
        pltpu.make_async_copy(wv_hbm.at[j], wkv.at[j, :, pl.ds(nope, nope)], load_sem.at[2]).start()
    q_copy.start()

    barrier = pltpu.get_barrier_semaphore()

    @pl.loop(1, chips)
    def _(d):
        pl.semaphore_signal(
            barrier, inc=1, device_id={"ctx": device_at(place + d, core)}, device_id_type=MESH
        )

    pl.semaphore_signal(barrier, inc=1, device_id={"ctx": across}, device_id_type=MESH)
    if early:
        pl.semaphore_signal(barrier, inc=1, device_id={"rep": 1 - rep}, device_id_type=MESH)
    pl.semaphore_wait(barrier, chips + (1 if early else 0))

    LAT_OUT, LAT_ON, RIGHT, LEFT, ACROSS, HALF_R, HALF_L, HALF_X = range(8)

    near = me // (devices // 2)
    chips_half = chips // 2

    def near_chip(i):
        return near * chips_half + lax.rem(my_chip - near * chips_half + i, chips_half)

    def far_chip(i):
        return (1 - near) * chips_half + lax.rem(my_chip - near * chips_half + i, chips_half)

    def lat_out(chip):
        return pltpu.make_async_remote_copy(
            src_ref=lat_hbm,
            dst_ref=lat.at[me],
            send_sem=send_sem.at[LAT_OUT],
            recv_sem=lat_recv.at[me],
            device_id={"ctx": chip * cores + core},
            device_id_type=MESH,
        )

    def lat_on(owner):
        return pltpu.make_async_remote_copy(
            src_ref=lat.at[owner],
            dst_ref=lat.at[owner],
            send_sem=send_sem.at[LAT_ON],
            recv_sem=lat_recv.at[owner],
            device_id={"ctx": across},
            device_id_type=MESH,
        )

    @pl.loop(1, chips_half)
    def _(i):
        lat_out(near_chip(i)).start()

    @pl.loop(0, chips_half)
    def _(i):
        lat_out(far_chip(i)).start()

    def half_out(src, j, way, target):
        return pltpu.make_async_remote_copy(
            src_ref=src,
            dst_ref=halves.at[way * early + j, rep],
            send_sem=send_sem.at[HALF_R + way],
            recv_sem=half_recv.at[way * early + j, rep],
            device_id={"ctx": target},
            device_id_type=MESH,
        )

    def half_over(j, way, which):
        return pltpu.make_async_remote_copy(
            src_ref=halves.at[way * early + j, which],
            dst_ref=halves.at[way * early + j, which],
            send_sem=send_sem.at[HALF_X],
            recv_sem=half_recv.at[way * early + j, which],
            device_id={"rep": 1 - rep},
            device_id_type=MESH,
        )

    early_r = [j for j in order_r if j < early]
    early_l = [j for j in order_l if j < early]

    if early:

        @pl.when(rep == 0)
        def _():
            for jr, jl in zip(early_r, early_l):
                half_out(wk_hbm.at[jr], jr, 0, right).start()
                half_out(wk_hbm.at[jl], jl, 1, left).start()

        @pl.when(rep == 1)
        def _():
            for jr, jl in zip(early_r, early_l):
                half_out(wv_hbm.at[jr], jr, 0, right).start()
                half_out(wv_hbm.at[jl], jl, 1, left).start()

    lat_copy.wait()
    lat_on(me).start()

    def relay(chip):
        owner = chip * cores + core
        lat_on(owner).wait_recv()
        lat_on(owner).start()

    @pl.loop(1, chips_half)
    def _(i):
        relay(near_chip(i))

    @pl.loop(0, chips_half)
    def _(i):
        lat_on(near_chip(i) * cores + other_core).wait_recv()

    pltpu.make_async_copy(wkv, wkv, load_sem.at[2]).wait()

    def parity(owner, j):
        if heads % 2 == 0:
            return j % 2
        return lax.rem(owner * heads + j, 2)

    def send(owner, j, stream, target):
        return pltpu.make_async_remote_copy(
            src_ref=kv.at[owner * heads + j],
            dst_ref=kv.at[owner * heads + j],
            send_sem=send_sem.at[stream],
            recv_sem=kv_recv.at[owner * heads + j],
            device_id={"ctx": target},
            device_id_type=MESH,
        )

    def go_right(owner, j):
        return send(owner, j, RIGHT, right)

    def go_left(owner, j):
        return send(owner, j, LEFT, left)

    def go_across(owner, j):
        return send(owner, j, ACROSS, across)

    def store(owner, j, keys, values):
        odd = parity(owner, j)
        turned = jnp.concatenate([keys[:, rope:], keys[:, :rope]], axis=1)
        if isinstance(odd, int):
            keys = turned if odd else keys
        else:
            keys = jnp.where(odd == 1, turned, keys)
        kv[owner * heads + j, 0] = keys.astype(jnp.bfloat16)
        kv[owner * heads + j, 1] = values.astype(jnp.bfloat16)

    def project(j):
        both = jnp.dot(
            lat[...].reshape(rows, lat.shape[2])[:, :width], wkv[j], preferred_element_type=jnp.float32
        )
        store(me, j, both[:, :nope], both[:, nope:])

    def project_arrived(owner, j, way):
        some = lat[...].reshape(rows, lat.shape[2])[:, :width]
        slot = way * early + j
        keys = jnp.dot(some, halves[slot, 0], preferred_element_type=jnp.float32)
        values = jnp.dot(some, halves[slot, 1], preferred_element_type=jnp.float32)
        store(owner, j, keys, values)

    @pl.loop(0, chips_half)
    def _(i):
        relay(far_chip(i))

    @pl.loop(0, chips_half)
    def _(i):
        lat_on(far_chip(i) * cores + other_core).wait_recv()

    for j in late:
        project(j)
        go_right(me, j).start()
        if early == 0:
            go_left(me, j).start()
    if early:
        for j in order_l:
            if j >= early:
                go_left(me, j).start()

    def hand_over(place_in):
        for j, way in ((early_r[place_in], 0), (early_l[place_in], 1)):
            half_over(j, way, rep).wait_recv()
            half_over(j, way, rep).start()

    if early:
        hand_over(0)
    for j in range(early):
        project(j)
    for j in range(heads):
        go_across(me, j).start()

    rope_part = lat[...].reshape(rows, lat.shape[2])[:, width:]
    blank = jnp.zeros_like(rope_part)
    ropes[0] = jnp.concatenate([rope_part, blank], axis=1)
    ropes[1] = jnp.concatenate([blank, rope_part], axis=1)

    q_copy.wait()

    lane = lax.broadcasted_iota(jnp.int32, (rows, nope), 1)
    upper = lane >= rope

    def attend(owner, j):
        odd = parity(owner, j)
        head = owner * heads + j
        pair = owner * (heads // 2) + j // 2 if heads % 2 == 0 else head // 2
        start = pl.multiple_of(pair * (2 * qk) + odd * nope, nope)
        queries = q[:, pl.ds(start, 2 * nope)]
        keys = kv[head, 0]
        values = kv[head, 1]

        def even_keys():
            return jnp.concatenate([keys, ropes[0]], axis=1)

        def odd_keys():
            return jnp.concatenate(
                [jnp.where(upper, keys, jnp.zeros_like(keys)), jnp.where(upper, ropes[1], keys)], axis=1
            )

        if isinstance(odd, int):
            keys_full = odd_keys() if odd else even_keys()
        else:
            keys_full = jnp.where(odd == 1, odd_keys(), even_keys())
        scores = lax.dot_general(
            queries, keys_full, (((1,), (1,)), ((), ())), preferred_element_type=jnp.float32
        )
        row_max = jnp.max(scores, axis=1, keepdims=True)
        weights = jnp.exp2((scores - row_max) * scale)
        total = jnp.sum(weights, axis=1, keepdims=True)
        mixed = jnp.dot(weights.astype(jnp.bfloat16), values, preferred_element_type=jnp.float32)
        o[:, pl.ds(pl.multiple_of(head * nope, nope), nope)] = (mixed * (1.0 / total)).astype(jnp.bfloat16)

    attend(me, 0)
    for i in range(1, early):
        hand_over(i)
        attend(me, i)
    for j in range(max(early, 1), heads):
        attend(me, j)

    def ring_step(s, first, last, before):
        from_left = device_at(place - s, core)
        from_right = device_at(place + s, core)
        for pos in range(heads):
            jr, jl = order_r[pos], order_l[pos]
            for j, way, owner, go in ((jr, 0, from_left, go_right), (jl, 1, from_right, go_left)):
                if first and j < early:
                    half_over(j, way, 1 - rep).wait_recv()
                    project_arrived(owner, j, way)
                else:
                    go(owner, j).wait_recv()
                if not last or pos < (half_right if way == 0 else heads - half_right):
                    go(owner, j).start()
                go_across(owner, j).start()
            for owner, js in zip(before, (order_r, order_l)):
                go_across(owner, js[pos]).wait_recv()
            attend(from_left, jr)
            attend(from_right, jl)
            for owner, js in zip(before, (order_r, order_l)):
                attend(owner, js[pos])

    def others(s):
        return (device_at(place - s, other_core), device_at(place + s, other_core))

    ring_step(1, True, half == 2, (across,))
    if half > 3:

        @pl.loop(2, half - 1)
        def _(s):
            ring_step(s, False, False, others(s - 1))

    if half > 2:
        ring_step(half - 1, False, True, others(half - 2))

    far = device_at(place + half, core)
    far_other = device_at(place + half, other_core)
    arrivals = []
    for pos in range(half_right):
        arrivals.append((order_r[pos], go_right))
        if pos < heads - half_right:
            arrivals.append((order_l[pos], go_left))
    before = others(half - 1)
    for pos in range(heads):
        for owner, js in zip(before, (order_r, order_l)):
            go_across(owner, js[pos]).wait_recv()
            attend(owner, js[pos])
    for j, go in arrivals:
        go(far, j).wait_recv()
        go_across(far, j).start()
        attend(far, j)
    for j, _ in arrivals:
        go_across(far_other, j).wait_recv()
        attend(far_other, j)

    def sent(stream, ref):
        pltpu.make_async_remote_copy(
            src_ref=ref,
            dst_ref=ref,
            send_sem=send_sem.at[stream],
            recv_sem=send_sem.at[stream],
            device_id={"ctx": across},
            device_id_type=MESH,
        ).wait_send()

    sent(LAT_OUT, lat.at[pl.ds(0, chips - 1)])
    sent(LAT_ON, lat.at[pl.ds(0, chips)])
    sent(RIGHT, kv.at[pl.ds(0, (half - 1) * heads + half_right - early)])
    sent(LEFT, kv.at[pl.ds(0, half * heads - half_right - early)])
    sent(ACROSS, kv.at[pl.ds(0, chips * heads)])
    if early:
        for stream in (HALF_R, HALF_L):
            sent(stream, halves.at[pl.ds(0, early), 0])
        sent(HALF_X, halves.at[pl.ds(0, early)])


def on_device(grid_y, cores, early, queries, latents, w_key, w_value):
    devices = lax.axis_size("ctx")
    heads, width, nope = w_key.shape
    query_rows = queries.shape[0]
    block = latents.shape[0]
    rows = block * devices
    anywhere = pl.BlockSpec(memory_space=pl.ANY)
    dma = pltpu.SemaphoreType.DMA
    return pl.pallas_call(
        functools.partial(kernel, grid_y, cores, early),
        out_shape=jax.ShapeDtypeStruct((query_rows, devices * heads * nope), jnp.bfloat16),
        in_specs=[anywhere] * 4,
        out_specs=pl.BlockSpec(memory_space=pltpu.VMEM),
        scratch_shapes=[
            pltpu.VMEM(queries.shape, jnp.bfloat16),
            pltpu.VMEM((devices, block, latents.shape[1]), jnp.bfloat16),
            pltpu.VMEM((heads, width, 2 * nope), jnp.bfloat16),
            pltpu.VMEM((2, rows, nope), jnp.bfloat16),
            pltpu.VMEM((devices * heads, 2, rows, nope), jnp.bfloat16),
            pltpu.VMEM((max(2 * early, 1), 2, width, nope), jnp.bfloat16),
            dma((3,)),
            dma((devices,)),
            dma((devices * heads,)),
            dma((max(2 * early, 1), 2)),
            dma((8,)),
        ],
        compiler_params=pltpu.CompilerParams(
            collective_id=0, has_side_effects=True, vmem_limit_bytes=50 * 1024 * 1024
        ),
    )(*(pltpu.with_memory_space_constraint(a, pltpu.HBM) for a in (queries, latents, w_key, w_value)))


def layout_of(mesh):
    group = list(mesh.devices.reshape(-1, mesh.shape["ctx"])[0])
    places = [tuple(d.coords) for d in group]
    chips = sorted(set(places))
    cores = len(group) // len(chips)
    varied = [axis for axis in range(3) if len({c[axis] for c in chips}) > 1]
    grid_y = 1
    if len(varied) == 2:
        fast = len({c[varied[0]] for c in chips})
        grid_y = 2 if fast == 2 else 1
    return grid_y, cores


def solution(mesh):
    grid_y, cores = layout_of(mesh)
    early = 2 if mesh.shape["rep"] == 2 else 0
    return jax.shard_map(
        functools.partial(on_device, grid_y, cores, early),
        mesh=mesh,
        in_specs=(
            P(("rep", "ctx"), None),
            P(("rep", "ctx"), None),
            P("ctx", None, None),
            P("ctx", None, None),
        ),
        out_specs=P(("rep", "ctx"), None),
        check_vma=False,
    )
```

```python
import functools
import math

import jax
import jax.numpy as jnp
from jax import lax
from jax.experimental import pallas as pl
from jax.experimental.pallas import tpu as pltpu
from jax.sharding import PartitionSpec as P

MESH = pl.DeviceIdType.MESH


def kernel(
    grid_y,
    cores,
    early,
    q_hbm,
    lat_hbm,
    wk_hbm,
    wv_hbm,
    o,
    q,
    lat,
    wkv,
    ropes,
    kv,
    halves,
    load_sem,
    lat_recv,
    kv_recv,
    half_recv,
    send_sem,
    part_recv,
    hello,
):
    devices = lat.shape[0]
    heads = wkv.shape[0]
    rows = kv.shape[2]
    nope = kv.shape[3]
    width = wkv.shape[1]
    rope = lat.shape[2] - width
    qk = nope + rope
    chips = devices // cores
    grid_z = chips // grid_y
    half = chips // 2
    scale = math.log2(math.e) / math.sqrt(qk)

    half_right = (heads + 1) // 2
    late = list(range(early, heads))
    order_r = []
    for i in range(max(len(late), early)):
        order_r += late[i : i + 1]
        if i < early:
            order_r.append(i)
    order_l = order_r[half_right:] + order_r[:half_right]

    me = lax.axis_index("ctx")
    core = lax.rem(me, cores)
    my_chip = me // cores
    my_y = lax.rem(my_chip, grid_y)
    my_z = my_chip // grid_y
    place = (1 - my_y) * my_z + my_y * (2 * grid_z - 1 - my_z)

    def device_at(spot, which):
        spot = lax.rem(spot + 2 * chips, chips)
        y = spot // grid_z
        z = (1 - y) * spot + y * (2 * grid_z - 1 - spot)
        return (z * grid_y + y) * cores + which

    other_core = cores - 1 - core
    across = my_chip * cores + other_core
    right = device_at(place + 1, core)
    left = device_at(place - 1, core)
    rep = lax.axis_index("rep")

    q_copy = pltpu.make_async_copy(q_hbm, q, load_sem.at[0])
    lat_copy = pltpu.make_async_copy(lat_hbm, lat.at[me], load_sem.at[1])
    lat_copy.start()
    for j in range(heads):
        pltpu.make_async_copy(wk_hbm.at[j], wkv.at[j, :, pl.ds(0, nope)], load_sem.at[2]).start()
        pltpu.make_async_copy(wv_hbm.at[j], wkv.at[j, :, pl.ds(nope, nope)], load_sem.at[2]).start()
    q_copy.start()

    barrier = pltpu.get_barrier_semaphore()

    def greet(sem):
        if grid_y == 2:
            beside = (my_z * grid_y + 1 - my_y) * cores + core
            pl.semaphore_signal(sem, inc=1, device_id={"ctx": beside}, device_id_type=MESH)

        @pl.when(my_z > 0)
        def _():
            pl.semaphore_signal(sem, inc=1, device_id={"ctx": me - grid_y * cores}, device_id_type=MESH)

        @pl.when(my_z < grid_z - 1)
        def _():
            pl.semaphore_signal(sem, inc=1, device_id={"ctx": me + grid_y * cores}, device_id_type=MESH)

    neighbours = (
        grid_y - 1 + lax.convert_element_type(my_z > 0, jnp.int32) + lax.convert_element_type(my_z < grid_z - 1, jnp.int32)
    )
    pl.semaphore_signal(barrier, inc=1, device_id={"ctx": across}, device_id_type=MESH)
    if early:
        greet(barrier)
        pl.semaphore_signal(barrier, inc=1, device_id={"rep": 1 - rep}, device_id_type=MESH)
        pl.semaphore_wait(barrier, neighbours + 2)
    else:

        @pl.loop(1, chips)
        def _(d):
            pl.semaphore_signal(
                barrier, inc=1, device_id={"ctx": device_at(place + d, core)}, device_id_type=MESH
            )

        pl.semaphore_wait(barrier, chips)

    LAT_OUT, LAT_ON, RIGHT, LEFT, ACROSS, HALF_R, HALF_L, HALF_X = range(8)

    near = me // (devices // 2)
    chips_half = chips // 2

    def near_chip(i):
        return near * chips_half + lax.rem(my_chip - near * chips_half + i, chips_half)

    def far_chip(i):
        return (1 - near) * chips_half + lax.rem(my_chip - near * chips_half + i, chips_half)

    def lat_out(chip):
        return pltpu.make_async_remote_copy(
            src_ref=lat_hbm,
            dst_ref=lat.at[me],
            send_sem=send_sem.at[LAT_OUT],
            recv_sem=lat_recv.at[me],
            device_id={"ctx": chip * cores + core},
            device_id_type=MESH,
        )

    def lat_on(owner):
        return pltpu.make_async_remote_copy(
            src_ref=lat.at[owner],
            dst_ref=lat.at[owner],
            send_sem=send_sem.at[LAT_ON],
            recv_sem=lat_recv.at[owner],
            device_id={"ctx": across},
            device_id_type=MESH,
        )

    def lat_near():
        @pl.loop(1, chips_half)
        def _(i):
            lat_out(near_chip(i)).start()

    def lat_far():
        @pl.loop(0, chips_half)
        def _(i):
            lat_out(far_chip(i)).start()

    pieces = 4
    deep = width // pieces

    def half_out(src, j, way, target, piece):
        return pltpu.make_async_remote_copy(
            src_ref=src.at[j, pl.ds(piece * deep, deep)],
            dst_ref=halves.at[way * early + j, rep, pl.ds(piece * deep, deep)],
            send_sem=send_sem.at[HALF_R + way],
            recv_sem=half_recv.at[way * early + j, rep],
            device_id={"ctx": target},
            device_id_type=MESH,
        )

    def half_over(j, way, which):
        return pltpu.make_async_remote_copy(
            src_ref=halves.at[way * early + j, which],
            dst_ref=halves.at[way * early + j, which],
            send_sem=send_sem.at[HALF_X],
            recv_sem=half_recv.at[way * early + j, which],
            device_id={"rep": 1 - rep},
            device_id_type=MESH,
        )

    early_r = [j for j in order_r if j < early]
    early_l = [j for j in order_l if j < early]

    def weights_out(first, last):
        for which, src in ((0, wk_hbm), (1, wv_hbm)):

            @pl.when(rep == which)
            def _():
                for i in range(first, last):
                    jr, jl, piece = early_r[i // pieces], early_l[i // pieces], i % pieces
                    half_out(src, jr, 0, right, piece).start()
                    half_out(src, jl, 1, left, piece).start()

    if early:
        rounds = grid_y + grid_z - 3
        near_rounds = grid_y + grid_z // 2 - 3
        sent_out = 2
        weights_out(0, sent_out)
        for r in range(rounds):
            greet(hello.at[r])
            pl.semaphore_wait(hello.at[r], neighbours)
            if r == near_rounds:
                lat_near()
            if r == rounds - 1:
                lat_far()
            more = early * pieces if r == rounds - 1 else min(sent_out + 1, early * pieces)
            weights_out(sent_out, more)
            sent_out = more
    else:
        lat_near()
        lat_far()

    lat_copy.wait()
    lat_on(me).start()

    def relay(chip):
        owner = chip * cores + core
        lat_on(owner).wait_recv()
        lat_on(owner).start()

    @pl.loop(1, chips_half)
    def _(i):
        relay(near_chip(i))

    @pl.loop(0, chips_half)
    def _(i):
        lat_on(near_chip(i) * cores + other_core).wait_recv()

    pltpu.make_async_copy(wkv, wkv, load_sem.at[2]).wait()

    def parity(owner, j):
        if heads % 2 == 0:
            return j % 2
        return lax.rem(owner * heads + j, 2)

    def send(owner, j, stream, target):
        return pltpu.make_async_remote_copy(
            src_ref=kv.at[owner * heads + j],
            dst_ref=kv.at[owner * heads + j],
            send_sem=send_sem.at[stream],
            recv_sem=kv_recv.at[owner * heads + j],
            device_id={"ctx": target},
            device_id_type=MESH,
        )

    def go_right(owner, j):
        return send(owner, j, RIGHT, right)

    def go_left(owner, j):
        return send(owner, j, LEFT, left)

    def go_across(owner, j):
        return send(owner, j, ACROSS, across)

    def part_of(item, part):
        return kv.at[item, :, pl.ds(pl.multiple_of(part * (rows // 2), rows // 2), rows // 2)]

    def half_hop(owner, j, part, way, is_first):
        ref = part_of(owner * heads + j, part)
        sem = part_recv.at[way, j] if is_first else kv_recv.at[owner * heads + j]
        return pltpu.make_async_remote_copy(
            src_ref=ref,
            dst_ref=ref,
            send_sem=send_sem.at[RIGHT + way],
            recv_sem=sem,
            device_id={"ctx": right if way == 0 else left},
            device_id_type=MESH,
        )

    def project_part(j, part):
        some = lat[pl.ds(part * (devices // 2), devices // 2)].reshape(rows // 2, lat.shape[2])[:, :width]
        both = jnp.dot(some, wkv[j], preferred_element_type=jnp.float32)
        keys = both[:, :nope]
        if parity(me, j) == 1:
            keys = jnp.concatenate([keys[:, rope:], keys[:, :rope]], axis=1)
        at = pl.ds(pl.multiple_of(part * (rows // 2), rows // 2), rows // 2)
        kv[me * heads + j, 0, at] = keys.astype(jnp.bfloat16)
        kv[me * heads + j, 1, at] = both[:, nope:].astype(jnp.bfloat16)

    def late_out(part, is_first):
        for j in late:
            project_part(j, part)
        for jr, jl in zip([j for j in order_r if j >= early], [j for j in order_l if j >= early]):
            half_hop(me, jr, part, 0, is_first).start()
            half_hop(me, jl, part, 1, is_first).start()

    def store(owner, j, keys, values):
        odd = parity(owner, j)
        turned = jnp.concatenate([keys[:, rope:], keys[:, :rope]], axis=1)
        if isinstance(odd, int):
            keys = turned if odd else keys
        else:
            keys = jnp.where(odd == 1, turned, keys)
        kv[owner * heads + j, 0] = keys.astype(jnp.bfloat16)
        kv[owner * heads + j, 1] = values.astype(jnp.bfloat16)

    def project(j):
        both = jnp.dot(
            lat[...].reshape(rows, lat.shape[2])[:, :width], wkv[j], preferred_element_type=jnp.float32
        )
        store(me, j, both[:, :nope], both[:, nope:])

    def project_arrived(owner, j, way):
        some = lat[...].reshape(rows, lat.shape[2])[:, :width]
        slot = way * early + j
        keys = jnp.dot(some, halves[slot, 0], preferred_element_type=jnp.float32)
        values = jnp.dot(some, halves[slot, 1], preferred_element_type=jnp.float32)
        store(owner, j, keys, values)

    def hand_over(place_in):
        for j, way in ((early_r[place_in], 0), (early_l[place_in], 1)):
            half_over(j, way, rep).wait_recv()
            half_over(j, way, rep).start()

    if early:
        late_out(near, True)
        hand_over(0)

    @pl.loop(0, chips_half)
    def _(i):
        relay(far_chip(i))

    @pl.loop(0, chips_half)
    def _(i):
        lat_on(far_chip(i) * cores + other_core).wait_recv()

    if early:
        late_out(1 - near, False)
    else:
        for j in late:
            project(j)
            go_right(me, j).start()
            go_left(me, j).start()
    for j in range(early):
        project(j)
    for j in range(heads):
        go_across(me, j).start()

    rope_part = lat[...].reshape(rows, lat.shape[2])[:, width:]
    blank = jnp.zeros_like(rope_part)
    ropes[0] = jnp.concatenate([rope_part, blank], axis=1)
    ropes[1] = jnp.concatenate([blank, rope_part], axis=1)

    q_copy.wait()

    lane = lax.broadcasted_iota(jnp.int32, (rows, nope), 1)
    upper = lane >= rope

    def attend(owner, j):
        odd = parity(owner, j)
        head = owner * heads + j
        pair = owner * (heads // 2) + j // 2 if heads % 2 == 0 else head // 2
        start = pl.multiple_of(pair * (2 * qk) + odd * nope, nope)
        queries = q[:, pl.ds(start, 2 * nope)]
        keys = kv[head, 0]
        values = kv[head, 1]

        def even_keys():
            return jnp.concatenate([keys, ropes[0]], axis=1)

        def odd_keys():
            return jnp.concatenate(
                [jnp.where(upper, keys, jnp.zeros_like(keys)), jnp.where(upper, ropes[1], keys)], axis=1
            )

        if isinstance(odd, int):
            keys_full = odd_keys() if odd else even_keys()
        else:
            keys_full = jnp.where(odd == 1, odd_keys(), even_keys())
        scores = lax.dot_general(
            queries, keys_full, (((1,), (1,)), ((), ())), preferred_element_type=jnp.float32
        )
        row_max = jnp.max(scores, axis=1, keepdims=True)
        weights = jnp.exp2((scores - row_max) * scale)
        total = jnp.sum(weights, axis=1, keepdims=True)
        mixed = jnp.dot(weights.astype(jnp.bfloat16), values, preferred_element_type=jnp.float32)
        o[:, pl.ds(pl.multiple_of(head * nope, nope), nope)] = (mixed * (1.0 / total)).astype(jnp.bfloat16)

    attend(me, 0)
    for i in range(1, early):
        hand_over(i)
        attend(me, i)
    for j in range(max(early, 1), heads):
        attend(me, j)

    def others(s):
        return (device_at(place - s, other_core), device_at(place + s, other_core))

    def attend_others(s, pos):
        pair = list(zip(others(s), (order_r, order_l)))
        for owner, js in pair:
            go_across(owner, js[pos]).wait_recv()
        return [(owner, js[pos]) for owner, js in pair]

    def ring_step(s, first, last):
        from_left = device_at(place - s, core)
        from_right = device_at(place + s, core)
        for pos in range(heads):
            jr, jl = order_r[pos], order_l[pos]
            for j, way, owner, go in ((jr, 0, from_left, go_right), (jl, 1, from_right, go_left)):
                if first and j < early:
                    half_over(j, way, 1 - rep).wait_recv()
                    project_arrived(owner, j, way)
                elif first and early:
                    half_hop(owner, j, owner // (devices // 2), way, True).wait_recv()
                    half_hop(owner, j, 1 - owner // (devices // 2), way, False).wait_recv()
                else:
                    go(owner, j).wait_recv()
                if not last or pos < (half_right if way == 0 else heads - half_right):
                    go(owner, j).start()
                go_across(owner, j).start()
            todo = [(from_left, jr), (from_right, jl)]
            if first:
                go_across(across, pos).wait_recv()
                todo.append((across, pos))
            if pos > 0:
                todo += attend_others(s, pos - 1)
            elif not first:
                todo += attend_others(s - 1, heads - 1)
            for owner, j in todo:
                attend(owner, j)

    ring_step(1, True, half == 2)
    if half > 3:

        @pl.loop(2, half - 1)
        def _(s):
            ring_step(s, False, False)

    if half > 2:
        ring_step(half - 1, False, True)

    far = device_at(place + half, core)
    far_other = device_at(place + half, other_core)
    todo = attend_others(half - 1, heads - 1)
    for pos in range(half_right):
        arrivals = [(order_r[pos], go_right)]
        if pos < heads - half_right:
            arrivals.append((order_l[pos], go_left))
        for j, go in arrivals:
            go(far, j).wait_recv()
            go_across(far, j).start()
            todo.append((far, j))
        for owner, j in todo:
            attend(owner, j)
        for j, _ in arrivals:
            go_across(far_other, j).wait_recv()
        for j, _ in arrivals:
            attend(far_other, j)
        todo = []

    def sent(stream, ref):
        pltpu.make_async_remote_copy(
            src_ref=ref,
            dst_ref=ref,
            send_sem=send_sem.at[stream],
            recv_sem=send_sem.at[stream],
            device_id={"ctx": across},
            device_id_type=MESH,
        ).wait_send()

    sent(LAT_OUT, lat.at[pl.ds(0, chips - 1)])
    sent(LAT_ON, lat.at[pl.ds(0, chips)])
    sent(RIGHT, kv.at[pl.ds(0, (half - 1) * heads + half_right - early)])
    sent(LEFT, kv.at[pl.ds(0, half * heads - half_right - early)])
    sent(ACROSS, kv.at[pl.ds(0, chips * heads)])
    if early:
        for stream in (HALF_R, HALF_L):
            sent(stream, halves.at[pl.ds(0, early), 0])
        sent(HALF_X, halves.at[pl.ds(0, early)])


def on_device(grid_y, cores, early, queries, latents, w_key, w_value):
    devices = lax.axis_size("ctx")
    heads, width, nope = w_key.shape
    query_rows = queries.shape[0]
    block = latents.shape[0]
    rows = block * devices
    anywhere = pl.BlockSpec(memory_space=pl.ANY)
    dma = pltpu.SemaphoreType.DMA
    return pl.pallas_call(
        functools.partial(kernel, grid_y, cores, early),
        out_shape=jax.ShapeDtypeStruct((query_rows, devices * heads * nope), jnp.bfloat16),
        in_specs=[anywhere] * 4,
        out_specs=pl.BlockSpec(memory_space=pltpu.VMEM),
        scratch_shapes=[
            pltpu.VMEM(queries.shape, jnp.bfloat16),
            pltpu.VMEM((devices, block, latents.shape[1]), jnp.bfloat16),
            pltpu.VMEM((heads, width, 2 * nope), jnp.bfloat16),
            pltpu.VMEM((2, rows, nope), jnp.bfloat16),
            pltpu.VMEM((devices * heads, 2, rows, nope), jnp.bfloat16),
            pltpu.VMEM((max(2 * early, 1), 2, width, nope), jnp.bfloat16),
            dma((3,)),
            dma((devices,)),
            dma((devices * heads,)),
            dma((max(2 * early, 1), 2)),
            dma((8,)),
            dma((2, heads)),
            pltpu.SemaphoreType.REGULAR((max(devices // cores - 2, 1) if early else 1,)),
        ],
        compiler_params=pltpu.CompilerParams(
            collective_id=0, has_side_effects=True, vmem_limit_bytes=50 * 1024 * 1024
        ),
    )(*(pltpu.with_memory_space_constraint(a, pltpu.HBM) for a in (queries, latents, w_key, w_value)))


def layout_of(mesh):
    group = list(mesh.devices.reshape(-1, mesh.shape["ctx"])[0])
    places = [tuple(d.coords) for d in group]
    chips = sorted(set(places))
    cores = len(group) // len(chips)
    varied = [axis for axis in range(3) if len({c[axis] for c in chips}) > 1]
    grid_y = 1
    if len(varied) == 2:
        fast = len({c[varied[0]] for c in chips})
        grid_y = 2 if fast == 2 else 1
    return grid_y, cores


def solution(mesh):
    grid_y, cores = layout_of(mesh)
    early = 2 if mesh.shape["rep"] == 2 and grid_y == 2 else 0
    return jax.shard_map(
        functools.partial(on_device, grid_y, cores, early),
        mesh=mesh,
        in_specs=(
            P(("rep", "ctx"), None),
            P(("rep", "ctx"), None),
            P("ctx", None, None),
            P("ctx", None, None),
        ),
        out_specs=P(("rep", "ctx"), None),
        check_vma=False,
    )
```

```python
import functools
import math

import jax
import jax.numpy as jnp
from jax import lax
from jax.experimental import pallas as pl
from jax.experimental.pallas import tpu as pltpu
from jax.sharding import PartitionSpec as P

MESH = pl.DeviceIdType.MESH


def kernel(
    grid_y,
    cores,
    early,
    q_hbm,
    lat_hbm,
    wk_hbm,
    wv_hbm,
    o,
    q,
    lat,
    wkv,
    ropes,
    kv,
    halves,
    load_sem,
    lat_recv,
    kv_recv,
    half_recv,
    send_sem,
    part_recv,
):
    devices = lat.shape[0]
    heads = wkv.shape[0]
    rows = kv.shape[2]
    nope = kv.shape[3]
    width = wkv.shape[1]
    rope = lat.shape[2] - width
    qk = nope + rope
    chips = devices // cores
    grid_z = chips // grid_y
    half = chips // 2
    scale = math.log2(math.e) / math.sqrt(qk)

    half_right = (heads + 1) // 2
    late = list(range(early, heads))
    order_r = []
    for i in range(max(len(late), early)):
        order_r += late[i : i + 1]
        if i < early:
            order_r.append(i)
    order_l = order_r[half_right:] + order_r[:half_right]

    me = lax.axis_index("ctx")
    core = lax.rem(me, cores)
    my_chip = me // cores
    my_y = lax.rem(my_chip, grid_y)
    my_z = my_chip // grid_y
    place = (1 - my_y) * my_z + my_y * (2 * grid_z - 1 - my_z)

    def device_at(spot, which):
        spot = lax.rem(spot + 2 * chips, chips)
        y = spot // grid_z
        z = (1 - y) * spot + y * (2 * grid_z - 1 - spot)
        return (z * grid_y + y) * cores + which

    other_core = cores - 1 - core
    across = my_chip * cores + other_core
    right = device_at(place + 1, core)
    left = device_at(place - 1, core)
    rep = lax.axis_index("rep")

    q_copy = pltpu.make_async_copy(q_hbm, q, load_sem.at[0])
    lat_copy = pltpu.make_async_copy(lat_hbm, lat.at[me], load_sem.at[1])
    lat_copy.start()
    for j in range(heads):
        pltpu.make_async_copy(wk_hbm.at[j], wkv.at[j, :, pl.ds(0, nope)], load_sem.at[2]).start()
        pltpu.make_async_copy(wv_hbm.at[j], wkv.at[j, :, pl.ds(nope, nope)], load_sem.at[2]).start()
    q_copy.start()

    barrier = pltpu.get_barrier_semaphore()

    plane = grid_y * cores
    beside = (my_z * grid_y + 1 - my_y) * cores + core
    steps = [(0, 1, True), (-1, 1, my_z > 0), (1, 1, my_z < grid_z - 1)]
    steps += [(-1, 0, my_z > 0), (1, 0, my_z < grid_z - 1), (-2, 0, my_z > 1), (2, 0, my_z < grid_z - 2)]

    def greet(sem):
        for dz, dy, there in steps:
            to = (beside if dy else me) + dz * plane

            def tell():
                pl.semaphore_signal(sem, inc=1, device_id={"ctx": to}, device_id_type=MESH)

            if there is True:
                tell()
            else:
                pl.when(there)(tell)

    greeted = 1
    for _, _, there in steps[1:]:
        greeted = greeted + lax.convert_element_type(there, jnp.int32)
    pl.semaphore_signal(barrier, inc=1, device_id={"ctx": across}, device_id_type=MESH)
    if early:
        greet(barrier)
        pl.semaphore_signal(barrier, inc=1, device_id={"rep": 1 - rep}, device_id_type=MESH)
        pl.semaphore_wait(barrier, greeted + 2)
    else:

        @pl.loop(1, chips)
        def _(d):
            pl.semaphore_signal(
                barrier, inc=1, device_id={"ctx": device_at(place + d, core)}, device_id_type=MESH
            )

        pl.semaphore_wait(barrier, chips)

    LAT_OUT, LAT_ON, RIGHT, LEFT, ACROSS, HALF_R, HALF_L, HALF_X = range(8)

    near = me // (devices // 2)
    chips_half = chips // 2

    def near_chip(i):
        return near * chips_half + lax.rem(my_chip - near * chips_half + i, chips_half)

    def far_chip(i):
        return (1 - near) * chips_half + lax.rem(my_chip - near * chips_half + i, chips_half)

    def lat_out(owner, chip):
        return pltpu.make_async_remote_copy(
            src_ref=lat.at[owner],
            dst_ref=lat.at[owner],
            send_sem=send_sem.at[LAT_OUT],
            recv_sem=lat_recv.at[owner],
            device_id={"ctx": chip * cores + core},
            device_id_type=MESH,
        )

    def lat_on(owner):
        return pltpu.make_async_remote_copy(
            src_ref=lat.at[owner],
            dst_ref=lat.at[owner],
            send_sem=send_sem.at[LAT_ON],
            recv_sem=lat_recv.at[owner],
            device_id={"ctx": across},
            device_id_type=MESH,
        )

    lat_copy.wait()

    def lat_near(owner):
        @pl.loop(1, chips_half)
        def _(i):
            lat_out(owner, near_chip(i)).start()

    pieces = 4
    deep = width // pieces

    def half_out(src, j, way, target, piece):
        return pltpu.make_async_remote_copy(
            src_ref=src.at[j, pl.ds(piece * deep, deep)],
            dst_ref=halves.at[way * early + j, rep, pl.ds(piece * deep, deep)],
            send_sem=send_sem.at[HALF_R + way],
            recv_sem=half_recv.at[way * early + j, rep],
            device_id={"ctx": target},
            device_id_type=MESH,
        )

    def half_over(j, way, which):
        return pltpu.make_async_remote_copy(
            src_ref=halves.at[way * early + j, which],
            dst_ref=halves.at[way * early + j, which],
            send_sem=send_sem.at[HALF_X],
            recv_sem=half_recv.at[way * early + j, which],
            device_id={"rep": 1 - rep},
            device_id_type=MESH,
        )

    early_r = [j for j in order_r if j < early]
    early_l = [j for j in order_l if j < early]

    def relay(chip):
        owner = chip * cores + core
        lat_on(owner).wait_recv()
        lat_on(owner).start()

    def weights_out(first, last):
        for which, src in ((0, wk_hbm), (1, wv_hbm)):

            @pl.when(rep == which)
            def _():
                for i in range(first, last):
                    jr, jl, piece = early_r[i // pieces], early_l[i // pieces], i % pieces
                    half_out(src, jr, 0, right, piece).start()
                    half_out(src, jl, 1, left, piece).start()

    if early:
        partner = lax.rem(my_chip + chips_half, chips)
        lat_near(me)
        lat_out(me, partner).start()
        lat_on(me).start()
        weights_out(0, pieces)
        relay(partner)
        lat_near(partner * cores + core)
        weights_out(pieces, early * pieces)
    else:
        lat_near(me)

        @pl.loop(0, chips_half)
        def _(i):
            lat_out(me, far_chip(i)).start()

        lat_on(me).start()

    @pl.loop(1, chips_half)
    def _(i):
        relay(near_chip(i))

    @pl.loop(0, chips_half)
    def _(i):
        lat_on(near_chip(i) * cores + other_core).wait_recv()

    pltpu.make_async_copy(wkv, wkv, load_sem.at[2]).wait()

    def parity(owner, j):
        if heads % 2 == 0:
            return j % 2
        return lax.rem(owner * heads + j, 2)

    def send(owner, j, stream, target):
        return pltpu.make_async_remote_copy(
            src_ref=kv.at[owner * heads + j],
            dst_ref=kv.at[owner * heads + j],
            send_sem=send_sem.at[stream],
            recv_sem=kv_recv.at[owner * heads + j],
            device_id={"ctx": target},
            device_id_type=MESH,
        )

    def go_right(owner, j):
        return send(owner, j, RIGHT, right)

    def go_left(owner, j):
        return send(owner, j, LEFT, left)

    def go_across(owner, j):
        return send(owner, j, ACROSS, across)

    def part_of(item, part):
        return kv.at[item, :, pl.ds(pl.multiple_of(part * (rows // 2), rows // 2), rows // 2)]

    def half_hop(owner, j, part, way, is_first):
        ref = part_of(owner * heads + j, part)
        sem = part_recv.at[way, j] if is_first else kv_recv.at[owner * heads + j]
        return pltpu.make_async_remote_copy(
            src_ref=ref,
            dst_ref=ref,
            send_sem=send_sem.at[RIGHT + way],
            recv_sem=sem,
            device_id={"ctx": right if way == 0 else left},
            device_id_type=MESH,
        )

    def project_part(j, part):
        some = lat[pl.ds(part * (devices // 2), devices // 2)].reshape(rows // 2, lat.shape[2])[:, :width]
        both = jnp.dot(some, wkv[j], preferred_element_type=jnp.float32)
        keys = both[:, :nope]
        if parity(me, j) == 1:
            keys = jnp.concatenate([keys[:, rope:], keys[:, :rope]], axis=1)
        at = pl.ds(pl.multiple_of(part * (rows // 2), rows // 2), rows // 2)
        kv[me * heads + j, 0, at] = keys.astype(jnp.bfloat16)
        kv[me * heads + j, 1, at] = both[:, nope:].astype(jnp.bfloat16)

    def late_out(part, is_first):
        for j in late:
            project_part(j, part)
        for jr, jl in zip([j for j in order_r if j >= early], [j for j in order_l if j >= early]):
            half_hop(me, jr, part, 0, is_first).start()
            half_hop(me, jl, part, 1, is_first).start()

    def store(owner, j, keys, values):
        odd = parity(owner, j)
        turned = jnp.concatenate([keys[:, rope:], keys[:, :rope]], axis=1)
        if isinstance(odd, int):
            keys = turned if odd else keys
        else:
            keys = jnp.where(odd == 1, turned, keys)
        kv[owner * heads + j, 0] = keys.astype(jnp.bfloat16)
        kv[owner * heads + j, 1] = values.astype(jnp.bfloat16)

    def project(j):
        both = jnp.dot(
            lat[...].reshape(rows, lat.shape[2])[:, :width], wkv[j], preferred_element_type=jnp.float32
        )
        store(me, j, both[:, :nope], both[:, nope:])

    def project_arrived(owner, j, way):
        some = lat[...].reshape(rows, lat.shape[2])[:, :width]
        slot = way * early + j
        keys = jnp.dot(some, halves[slot, 0], preferred_element_type=jnp.float32)
        values = jnp.dot(some, halves[slot, 1], preferred_element_type=jnp.float32)
        store(owner, j, keys, values)

    def hand_over(place_in):
        for j, way in ((early_r[place_in], 0), (early_l[place_in], 1)):
            half_over(j, way, rep).wait_recv()
            half_over(j, way, rep).start()

    if early:
        late_out(near, True)
        hand_over(0)

    @pl.loop(1 if early else 0, chips_half)
    def _(i):
        relay(far_chip(i))

    @pl.loop(0, chips_half)
    def _(i):
        lat_on(far_chip(i) * cores + other_core).wait_recv()

    if early:
        late_out(1 - near, False)
    else:
        for j in late:
            project(j)
            go_right(me, j).start()
            go_left(me, j).start()
    for j in range(early):
        project(j)
    for j in range(heads):
        go_across(me, j).start()

    rope_part = lat[...].reshape(rows, lat.shape[2])[:, width:]
    blank = jnp.zeros_like(rope_part)
    ropes[0] = jnp.concatenate([rope_part, blank], axis=1)
    ropes[1] = jnp.concatenate([blank, rope_part], axis=1)

    q_copy.wait()

    lane = lax.broadcasted_iota(jnp.int32, (rows, nope), 1)
    upper = lane >= rope

    def attend(owner, j):
        odd = parity(owner, j)
        head = owner * heads + j
        pair = owner * (heads // 2) + j // 2 if heads % 2 == 0 else head // 2
        start = pl.multiple_of(pair * (2 * qk) + odd * nope, nope)
        queries = q[:, pl.ds(start, 2 * nope)]
        keys = kv[head, 0]
        values = kv[head, 1]

        def even_keys():
            return jnp.concatenate([keys, ropes[0]], axis=1)

        def odd_keys():
            return jnp.concatenate(
                [jnp.where(upper, keys, jnp.zeros_like(keys)), jnp.where(upper, ropes[1], keys)], axis=1
            )

        if isinstance(odd, int):
            keys_full = odd_keys() if odd else even_keys()
        else:
            keys_full = jnp.where(odd == 1, odd_keys(), even_keys())
        scores = lax.dot_general(
            queries, keys_full, (((1,), (1,)), ((), ())), preferred_element_type=jnp.float32
        )
        row_max = jnp.max(scores, axis=1, keepdims=True)
        weights = jnp.exp2((scores - row_max) * scale)
        total = jnp.sum(weights, axis=1, keepdims=True)
        mixed = jnp.dot(weights.astype(jnp.bfloat16), values, preferred_element_type=jnp.float32)
        o[:, pl.ds(pl.multiple_of(head * nope, nope), nope)] = (mixed * (1.0 / total)).astype(jnp.bfloat16)

    attend(me, 0)
    for i in range(1, early):
        hand_over(i)
        attend(me, i)
    for j in range(max(early, 1), heads):
        attend(me, j)

    def others(s):
        return (device_at(place - s, other_core), device_at(place + s, other_core))

    def attend_others(s, pos):
        pair = list(zip(others(s), (order_r, order_l)))
        for owner, js in pair:
            go_across(owner, js[pos]).wait_recv()
        return [(owner, js[pos]) for owner, js in pair]

    def ring_step(s, first, last):
        from_left = device_at(place - s, core)
        from_right = device_at(place + s, core)
        for pos in range(heads):
            jr, jl = order_r[pos], order_l[pos]
            for j, way, owner, go in ((jr, 0, from_left, go_right), (jl, 1, from_right, go_left)):
                if first and j < early:
                    half_over(j, way, 1 - rep).wait_recv()
                    project_arrived(owner, j, way)
                elif first and early:
                    half_hop(owner, j, owner // (devices // 2), way, True).wait_recv()
                    half_hop(owner, j, 1 - owner // (devices // 2), way, False).wait_recv()
                else:
                    go(owner, j).wait_recv()
                if not last or pos < (half_right if way == 0 else heads - half_right):
                    go(owner, j).start()
                go_across(owner, j).start()
            todo = [(from_left, jr), (from_right, jl)]
            if first:
                go_across(across, pos).wait_recv()
                todo.append((across, pos))
            if pos > 0:
                todo += attend_others(s, pos - 1)
            elif not first:
                todo += attend_others(s - 1, heads - 1)
            for owner, j in todo:
                attend(owner, j)

    ring_step(1, True, half == 2)
    if half > 3:

        @pl.loop(2, half - 1)
        def _(s):
            ring_step(s, False, False)

    if half > 2:
        ring_step(half - 1, False, True)

    far = device_at(place + half, core)
    far_other = device_at(place + half, other_core)
    todo = attend_others(half - 1, heads - 1)
    for pos in range(half_right):
        arrivals = [(order_r[pos], go_right)]
        if pos < heads - half_right:
            arrivals.append((order_l[pos], go_left))
        for j, go in arrivals:
            go(far, j).wait_recv()
            go_across(far, j).start()
            todo.append((far, j))
        for owner, j in todo:
            attend(owner, j)
        for j, _ in arrivals:
            go_across(far_other, j).wait_recv()
        for j, _ in arrivals:
            attend(far_other, j)
        todo = []

    def sent(stream, ref):
        pltpu.make_async_remote_copy(
            src_ref=ref,
            dst_ref=ref,
            send_sem=send_sem.at[stream],
            recv_sem=send_sem.at[stream],
            device_id={"ctx": across},
            device_id_type=MESH,
        ).wait_send()

    sent(LAT_OUT, lat.at[pl.ds(0, chips - 1)])
    sent(LAT_ON, lat.at[pl.ds(0, chips)])
    sent(RIGHT, kv.at[pl.ds(0, (half - 1) * heads + half_right - early)])
    sent(LEFT, kv.at[pl.ds(0, half * heads - half_right - early)])
    sent(ACROSS, kv.at[pl.ds(0, chips * heads)])
    if early:
        for stream in (HALF_R, HALF_L):
            sent(stream, halves.at[pl.ds(0, early), 0])
        sent(HALF_X, halves.at[pl.ds(0, early)])


def on_device(grid_y, cores, early, queries, latents, w_key, w_value):
    devices = lax.axis_size("ctx")
    heads, width, nope = w_key.shape
    query_rows = queries.shape[0]
    block = latents.shape[0]
    rows = block * devices
    anywhere = pl.BlockSpec(memory_space=pl.ANY)
    dma = pltpu.SemaphoreType.DMA
    return pl.pallas_call(
        functools.partial(kernel, grid_y, cores, early),
        out_shape=jax.ShapeDtypeStruct((query_rows, devices * heads * nope), jnp.bfloat16),
        in_specs=[anywhere] * 4,
        out_specs=pl.BlockSpec(memory_space=pltpu.VMEM),
        scratch_shapes=[
            pltpu.VMEM(queries.shape, jnp.bfloat16),
            pltpu.VMEM((devices, block, latents.shape[1]), jnp.bfloat16),
            pltpu.VMEM((heads, width, 2 * nope), jnp.bfloat16),
            pltpu.VMEM((2, rows, nope), jnp.bfloat16),
            pltpu.VMEM((devices * heads, 2, rows, nope), jnp.bfloat16),
            pltpu.VMEM((max(2 * early, 1), 2, width, nope), jnp.bfloat16),
            dma((3,)),
            dma((devices,)),
            dma((devices * heads,)),
            dma((max(2 * early, 1), 2)),
            dma((8,)),
            dma((2, heads)),
        ],
        compiler_params=pltpu.CompilerParams(
            collective_id=0, has_side_effects=True, vmem_limit_bytes=50 * 1024 * 1024
        ),
    )(*(pltpu.with_memory_space_constraint(a, pltpu.HBM) for a in (queries, latents, w_key, w_value)))


def layout_of(mesh):
    group = list(mesh.devices.reshape(-1, mesh.shape["ctx"])[0])
    places = [tuple(d.coords) for d in group]
    chips = sorted(set(places))
    cores = len(group) // len(chips)
    varied = [axis for axis in range(3) if len({c[axis] for c in chips}) > 1]
    grid_y = 1
    if len(varied) == 2:
        fast = len({c[varied[0]] for c in chips})
        grid_y = 2 if fast == 2 else 1
    return grid_y, cores


def solution(mesh):
    grid_y, cores = layout_of(mesh)
    chips = mesh.shape["ctx"] // cores
    early = 2 if mesh.shape["rep"] == 2 and grid_y == 2 and chips // grid_y <= 4 else 0
    return jax.shard_map(
        functools.partial(on_device, grid_y, cores, early),
        mesh=mesh,
        in_specs=(
            P(("rep", "ctx"), None),
            P(("rep", "ctx"), None),
            P("ctx", None, None),
            P("ctx", None, None),
        ),
        out_specs=P(("rep", "ctx"), None),
        check_vma=False,
    )
```

```python
import functools
import math

import jax
import jax.numpy as jnp
from jax import lax
from jax.experimental import pallas as pl
from jax.experimental.pallas import tpu as pltpu
from jax.sharding import PartitionSpec as P

MESH = pl.DeviceIdType.MESH


def kernel(
    grid_y,
    cores,
    early,
    q_hbm,
    lat_hbm,
    wk_hbm,
    wv_hbm,
    o,
    q,
    lat,
    wkv,
    ropes,
    kv,
    halves,
    load_sem,
    lat_recv,
    kv_recv,
    half_recv,
    send_sem,
    part_recv,
    lent,
    mixed_out,
    lend_sem,
):
    devices = lat.shape[0]
    heads = wkv.shape[0]
    rows = kv.shape[2]
    nope = kv.shape[3]
    width = wkv.shape[1]
    rope = lat.shape[2] - width
    qk = nope + rope
    chips = devices // cores
    grid_z = chips // grid_y
    half = chips // 2
    scale = math.log2(math.e) / math.sqrt(qk)

    half_right = (heads + 1) // 2
    late = list(range(early, heads))
    order_r = []
    for i in range(max(len(late), early)):
        order_r += late[i : i + 1]
        if i < early:
            order_r.append(i)
    order_l = order_r[half_right:] + order_r[:half_right]
    order_a = late + list(range(early))
    keep = order_a[:2] + order_a[3:]
    ship = order_a[:3]

    me = lax.axis_index("ctx")
    core = lax.rem(me, cores)
    my_chip = me // cores
    my_y = lax.rem(my_chip, grid_y)
    my_z = my_chip // grid_y
    place = (1 - my_y) * my_z + my_y * (2 * grid_z - 1 - my_z)

    def device_at(spot, which):
        spot = lax.rem(spot + 2 * chips, chips)
        y = spot // grid_z
        z = (1 - y) * spot + y * (2 * grid_z - 1 - spot)
        return (z * grid_y + y) * cores + which

    other_core = cores - 1 - core
    across = my_chip * cores + other_core
    right = device_at(place + 1, core)
    left = device_at(place - 1, core)
    rep = lax.axis_index("rep")
    top = my_z // (grid_z // 2)
    inward = 1 - 2 * top
    z_a = top * (grid_z - 1)
    z_g = (1 - top) * (grid_z - 1)
    corner = my_z == z_a
    inner = my_z != z_a

    def chip_of(name, which):
        z = {"A": z_a, "C": z_a + inward, "E": z_g - inward, "G": z_g}
        z |= {"B": z["A"], "D": z["C"], "F": z["E"], "H": z["G"]}
        y = my_y if name in "ACEG" else 1 - my_y
        return (z[name] * grid_y + y) * cores + which

    def mine(name):
        return chip_of(name, core)

    q_copy = pltpu.make_async_copy(q_hbm, q, load_sem.at[0])
    lat_copy = pltpu.make_async_copy(lat_hbm, lat.at[me], load_sem.at[1])
    lat_copy.start()
    for j in range(heads):
        pltpu.make_async_copy(wk_hbm.at[j], wkv.at[j, :, pl.ds(0, nope)], load_sem.at[2]).start()
        pltpu.make_async_copy(wv_hbm.at[j], wkv.at[j, :, pl.ds(nope, nope)], load_sem.at[2]).start()
    q_copy.start()

    barrier = pltpu.get_barrier_semaphore()

    plane = grid_y * cores
    beside = (my_z * grid_y + 1 - my_y) * cores + core
    steps = [(0, 1, True), (-1, 1, my_z > 0), (1, 1, my_z < grid_z - 1)]
    steps += [(-1, 0, my_z > 0), (1, 0, my_z < grid_z - 1), (-2, 0, my_z > 1), (2, 0, my_z < grid_z - 2)]

    def greet(sem):
        for dz, dy, there in steps:
            to = (beside if dy else me) + dz * plane

            def tell():
                pl.semaphore_signal(sem, inc=1, device_id={"ctx": to}, device_id_type=MESH)

            if there is True:
                tell()
            else:
                pl.when(there)(tell)

    greeted = 1
    for _, _, there in steps[1:]:
        greeted = greeted + lax.convert_element_type(there, jnp.int32)
    pl.semaphore_signal(barrier, inc=1, device_id={"ctx": across}, device_id_type=MESH)
    if early:
        greet(barrier)
        pl.semaphore_signal(barrier, inc=1, device_id={"rep": 1 - rep}, device_id_type=MESH)
        pl.semaphore_wait(barrier, greeted + 2)
    else:

        @pl.loop(1, chips)
        def _(d):
            pl.semaphore_signal(
                barrier, inc=1, device_id={"ctx": device_at(place + d, core)}, device_id_type=MESH
            )

        pl.semaphore_wait(barrier, chips)

    LAT_OUT, LAT_ON, RIGHT, LEFT, MID, ACROSS, HALF_R, HALF_L, HALF_X, LEND = range(10)

    near = me // (devices // 2)
    chips_half = chips // 2

    def near_chip(i):
        return near * chips_half + lax.rem(my_chip - near * chips_half + i, chips_half)

    def far_chip(i):
        return (1 - near) * chips_half + lax.rem(my_chip - near * chips_half + i, chips_half)

    def lat_out(owner, chip):
        return pltpu.make_async_remote_copy(
            src_ref=lat.at[owner],
            dst_ref=lat.at[owner],
            send_sem=send_sem.at[LAT_OUT],
            recv_sem=lat_recv.at[owner],
            device_id={"ctx": chip * cores + core},
            device_id_type=MESH,
        )

    def lat_on(owner):
        return pltpu.make_async_remote_copy(
            src_ref=lat.at[owner],
            dst_ref=lat.at[owner],
            send_sem=send_sem.at[LAT_ON],
            recv_sem=lat_recv.at[owner],
            device_id={"ctx": across},
            device_id_type=MESH,
        )

    lat_copy.wait()

    def lat_near(owner):
        @pl.loop(1, chips_half)
        def _(i):
            lat_out(owner, near_chip(i)).start()

    pieces = 4
    deep = width // pieces

    def half_out(src, j, way, target, piece):
        return pltpu.make_async_remote_copy(
            src_ref=src.at[j, pl.ds(piece * deep, deep)],
            dst_ref=halves.at[way * early + j, rep, pl.ds(piece * deep, deep)],
            send_sem=send_sem.at[HALF_R + way],
            recv_sem=half_recv.at[way * early + j, rep],
            device_id={"ctx": target},
            device_id_type=MESH,
        )

    def half_over(j, way, which):
        return pltpu.make_async_remote_copy(
            src_ref=halves.at[way * early + j, which],
            dst_ref=halves.at[way * early + j, which],
            send_sem=send_sem.at[HALF_X],
            recv_sem=half_recv.at[way * early + j, which],
            device_id={"rep": 1 - rep},
            device_id_type=MESH,
        )

    early_r = [j for j in order_r if j < early]
    early_l = [j for j in order_l if j < early]

    def relay(chip):
        owner = chip * cores + core
        lat_on(owner).wait_recv()
        lat_on(owner).start()

    def parity(owner, j):
        if heads % 2 == 0:
            return j % 2
        return lax.rem(owner * heads + j, 2)

    def weights_out(first, last):
        for which, src in ((0, wk_hbm), (1, wv_hbm)):

            @pl.when(rep == which)
            def _():
                for i in range(first, last):
                    half_out(src, early_r[i // pieces], 0, beside, i % pieces).start()

            @pl.when(jnp.logical_and(rep == which, inner))
            def _():
                for i in range(first, last):
                    for target in (mine("A"), mine("E")):
                        half_out(src, early_l[i // pieces], 1, target, i % pieces).start()

    lends = [("G", c, j) for j in order_a[2:3] for c in range(cores)]
    lends += [("H", c, j) for j in ship for c in range(cores)]

    def query_start(owner, j):
        odd = parity(owner, j)
        pair = owner * (heads // 2) + j // 2 if heads % 2 == 0 else (owner * heads + j) // 2
        return pl.multiple_of(pair * (2 * qk) + odd * nope, nope)

    def lend(i):
        name, which, j = lends[i]
        return pltpu.make_async_remote_copy(
            src_ref=q.at[:, pl.ds(query_start(chip_of(name, which), j), 2 * nope)],
            dst_ref=lent.at[i],
            send_sem=send_sem.at[LEND],
            recv_sem=lend_sem.at[0],
            device_id={"ctx": mine("C")},
            device_id_type=MESH,
        )

    def give_back(i):
        name, which, j = lends[i]
        at = pl.multiple_of((chip_of(name, which) * heads + j) * nope, nope)
        return pltpu.make_async_remote_copy(
            src_ref=mixed_out.at[i],
            dst_ref=o.at[:, pl.ds(at, nope)],
            send_sem=send_sem.at[LEND],
            recv_sem=lend_sem.at[1],
            device_id={"ctx": mine("A")},
            device_id_type=MESH,
        )

    def lend_out(first, last):
        @pl.when(corner)
        def _():
            for i in range(first, last):
                lend(i).start()

    if early:
        partner = lax.rem(my_chip + chips_half, chips)
        lat_out(me, partner).start()
        lat_near(me)
        lat_on(me).start()
        weights_out(0, pieces)
        q_copy.wait()
        lend_out(0, len(lends) // 2)
        lat_on(partner * cores + core).wait_recv()
        lat_near(partner * cores + core)
        lat_on(partner * cores + core).start()
        weights_out(pieces, early * pieces)
    else:
        lat_near(me)

        @pl.loop(0, chips_half)
        def _(i):
            lat_out(me, far_chip(i)).start()

        lat_on(me).start()

    @pl.loop(1, chips_half)
    def _(i):
        relay(near_chip(i))

    @pl.loop(0, chips_half)
    def _(i):
        lat_on(near_chip(i) * cores + other_core).wait_recv()

    pltpu.make_async_copy(wkv, wkv, load_sem.at[2]).wait()

    def send(owner, j, stream, target):
        return pltpu.make_async_remote_copy(
            src_ref=kv.at[owner * heads + j],
            dst_ref=kv.at[owner * heads + j],
            send_sem=send_sem.at[stream],
            recv_sem=kv_recv.at[owner * heads + j],
            device_id={"ctx": target},
            device_id_type=MESH,
        )

    def go_right(owner, j):
        return send(owner, j, RIGHT, right)

    def go_left(owner, j):
        return send(owner, j, LEFT, left)

    def go_across(owner, j):
        return send(owner, j, ACROSS, across)

    def part_of(item, part):
        return kv.at[item, :, pl.ds(pl.multiple_of(part * (rows // 2), rows // 2), rows // 2)]

    def half_hop(owner, j, part, is_first, way, stream, target):
        ref = part_of(owner * heads + j, part)
        sem = part_recv.at[way, j] if is_first else kv_recv.at[owner * heads + j]
        return pltpu.make_async_remote_copy(
            src_ref=ref,
            dst_ref=ref,
            send_sem=send_sem.at[stream],
            recv_sem=sem,
            device_id={"ctx": target},
            device_id_type=MESH,
        )

    def project_part(j, part):
        some = lat[pl.ds(part * (devices // 2), devices // 2)].reshape(rows // 2, lat.shape[2])[:, :width]
        both = jnp.dot(some, wkv[j], preferred_element_type=jnp.float32)
        keys = both[:, :nope]
        if parity(me, j) == 1:
            keys = jnp.concatenate([keys[:, rope:], keys[:, :rope]], axis=1)
        at = pl.ds(pl.multiple_of(part * (rows // 2), rows // 2), rows // 2)
        kv[me * heads + j, 0, at] = keys.astype(jnp.bfloat16)
        kv[me * heads + j, 1, at] = both[:, nope:].astype(jnp.bfloat16)

    late_r = [j for j in order_r if j >= early]
    late_l = [j for j in order_l if j >= early]

    def late_out(part, is_first):
        for j in late:
            project_part(j, part)
        for j in late_r:
            half_hop(me, j, part, is_first, 0, RIGHT, beside).start()

        @pl.when(corner)
        def _():
            for j in late:
                half_hop(me, j, part, is_first, 2, LEFT, mine("C")).start()

        @pl.when(inner)
        def _():
            for j in late_l:
                half_hop(me, j, part, is_first, 1, LEFT, mine("A")).start()
                half_hop(me, j, part, is_first, 1, MID, mine("E")).start()

    def store(owner, j, keys, values):
        odd = parity(owner, j)
        turned = jnp.concatenate([keys[:, rope:], keys[:, :rope]], axis=1)
        if isinstance(odd, int):
            keys = turned if odd else keys
        else:
            keys = jnp.where(odd == 1, turned, keys)
        kv[owner * heads + j, 0] = keys.astype(jnp.bfloat16)
        kv[owner * heads + j, 1] = values.astype(jnp.bfloat16)

    def project(j):
        both = jnp.dot(
            lat[...].reshape(rows, lat.shape[2])[:, :width], wkv[j], preferred_element_type=jnp.float32
        )
        store(me, j, both[:, :nope], both[:, nope:])

    def project_arrived(owner, j, way):
        some = lat[...].reshape(rows, lat.shape[2])[:, :width]
        slot = way * early + j
        keys = jnp.dot(some, halves[slot, 0], preferred_element_type=jnp.float32)
        values = jnp.dot(some, halves[slot, 1], preferred_element_type=jnp.float32)
        store(owner, j, keys, values)

    def hand_over(place_in):
        for j, way in ((early_r[place_in], 0), (early_l[place_in], 1)):
            half_over(j, way, rep).wait_recv()
            half_over(j, way, rep).start()

    if early:
        late_out(near, True)
        hand_over(0)

    @pl.loop(1 if early else 0, chips_half)
    def _(i):
        relay(far_chip(i))

    @pl.loop(0, chips_half)
    def _(i):
        lat_on(far_chip(i) * cores + other_core).wait_recv()

    if early:
        late_out(1 - near, False)
    else:
        for j in late:
            project(j)
            go_right(me, j).start()
            go_left(me, j).start()
    for j in range(early):
        project(j)
    if early:

        @pl.when(corner)
        def _():
            for j in range(early):
                send(me, j, LEFT, mine("C")).start()

        lend_out(len(lends) // 2, len(lends))
    for j in range(heads):
        go_across(me, j).start()

    rope_part = lat[...].reshape(rows, lat.shape[2])[:, width:]
    blank = jnp.zeros_like(rope_part)
    ropes[0] = jnp.concatenate([rope_part, blank], axis=1)
    ropes[1] = jnp.concatenate([blank, rope_part], axis=1)

    if not early:
        q_copy.wait()

    lane = lax.broadcasted_iota(jnp.int32, (rows, nope), 1)
    upper = lane >= rope

    def attended(queries, owner, j):
        odd = parity(owner, j)
        head = owner * heads + j
        keys = kv[head, 0]
        values = kv[head, 1]

        def even_keys():
            return jnp.concatenate([keys, ropes[0]], axis=1)

        def odd_keys():
            return jnp.concatenate(
                [jnp.where(upper, keys, jnp.zeros_like(keys)), jnp.where(upper, ropes[1], keys)], axis=1
            )

        if isinstance(odd, int):
            keys_full = odd_keys() if odd else even_keys()
        else:
            keys_full = jnp.where(odd == 1, odd_keys(), even_keys())
        scores = lax.dot_general(
            queries, keys_full, (((1,), (1,)), ((), ())), preferred_element_type=jnp.float32
        )
        row_max = jnp.max(scores, axis=1, keepdims=True)
        weights = jnp.exp2((scores - row_max) * scale)
        total = jnp.sum(weights, axis=1, keepdims=True)
        mixed = jnp.dot(weights.astype(jnp.bfloat16), values, preferred_element_type=jnp.float32)
        return (mixed * (1.0 / total)).astype(jnp.bfloat16)

    def attend(owner, j):
        at = pl.multiple_of((owner * heads + j) * nope, nope)
        o[:, pl.ds(at, nope)] = attended(q[:, pl.ds(query_start(owner, j), 2 * nope)], owner, j)

    attend(me, 0)
    for i in range(1, early):
        hand_over(i)
        attend(me, i)
    for j in range(max(early, 1), heads):
        attend(me, j)

    def sent(stream, ref):
        pltpu.make_async_remote_copy(
            src_ref=ref,
            dst_ref=ref,
            send_sem=send_sem.at[stream],
            recv_sem=send_sem.at[stream],
            device_id={"ctx": across},
            device_id_type=MESH,
        ).wait_send()

    def around():
        def others(s):
            return (device_at(place - s, other_core), device_at(place + s, other_core))

        def attend_others(s, pos):
            pair = list(zip(others(s), (order_r, order_l)))
            for owner, js in pair:
                go_across(owner, js[pos]).wait_recv()
            return [(owner, js[pos]) for owner, js in pair]

        def ring_step(s, first, last):
            from_left = device_at(place - s, core)
            from_right = device_at(place + s, core)
            for pos in range(heads):
                jr, jl = order_r[pos], order_l[pos]
                for j, way, owner, go in ((jr, 0, from_left, go_right), (jl, 1, from_right, go_left)):
                    go(owner, j).wait_recv()
                    if not last or pos < (half_right if way == 0 else heads - half_right):
                        go(owner, j).start()
                    go_across(owner, j).start()
                todo = [(from_left, jr), (from_right, jl)]
                if first:
                    go_across(across, pos).wait_recv()
                    todo.append((across, pos))
                if pos > 0:
                    todo += attend_others(s, pos - 1)
                elif not first:
                    todo += attend_others(s - 1, heads - 1)
                for owner, j in todo:
                    attend(owner, j)

        ring_step(1, True, half == 2)
        if half > 3:

            @pl.loop(2, half - 1)
            def _(s):
                ring_step(s, False, False)

        if half > 2:
            ring_step(half - 1, False, True)

        far = device_at(place + half, core)
        far_other = device_at(place + half, other_core)
        todo = attend_others(half - 1, heads - 1)
        for pos in range(half_right):
            arrivals = [(order_r[pos], go_right)]
            if pos < heads - half_right:
                arrivals.append((order_l[pos], go_left))
            for j, go in arrivals:
                go(far, j).wait_recv()
                go_across(far, j).start()
                todo.append((far, j))
            for owner, j in todo:
                attend(owner, j)
            for j, _ in arrivals:
                go_across(far_other, j).wait_recv()
            for j, _ in arrivals:
                attend(far_other, j)
            todo = []

        sent(RIGHT, kv.at[pl.ds(0, (half - 1) * heads + half_right)])
        sent(LEFT, kv.at[pl.ds(0, half * heads - half_right)])
        sent(ACROSS, kv.at[pl.ds(0, chips * heads)])

    def arrived(name, j, way):
        owner = mine(name)
        direct = {0: "B" if name == "B" else "D", 1: "C" if name == "C" else "E", 2: "A"}
        if way is None or name != direct[way]:
            go_across(owner, j).wait_recv()
        elif way < 2 and j < early:
            half_over(j, way, 1 - rep).wait_recv()
            project_arrived(owner, j, way)
        elif j >= early:
            near_part = owner // (devices // 2)
            half_hop(owner, j, near_part, True, way, RIGHT, across).wait_recv()
            half_hop(owner, j, 1 - near_part, False, way, RIGHT, across).wait_recv()
        else:
            go_across(owner, j).wait_recv()

    def follow(name, j):
        owner = chip_of(name, other_core)
        go_across(owner, j).wait_recv()
        return owner, j

    def at_corner():
        from_z = [("C", j, 1) for j in order_l] + [("E", j, None) for j in order_l] + [("G", j, None) for j in keep]
        from_y = [("B", j, 0) for j in order_r] + [("D", j, None) for j in order_l] + [("F", j, None) for j in order_l]
        from_y += [("H", order_a[3], None)]
        lag = []
        for k in range(len(from_y)):
            now = from_z[k : k + 1] + from_y[k : k + 1]
            for name, j, way in now:
                arrived(name, j, way)
                if name in "CE" or (name == "G" and j == order_a[3]):
                    send(mine(name), j, RIGHT, beside).start()
                go_across(mine(name), j).start()
            todo = [(mine(name), j) for name, j, _ in now]
            if k < heads:
                go_across(across, k).wait_recv()
                todo.append((across, k))
            todo += [follow(name, j) for name, j in lag]
            for owner, j in todo:
                attend(owner, j)
            lag = [(name, j) for name, j, _ in now]
        for name, j in lag:
            attend(*follow(name, j))
        pltpu.make_async_copy(mixed_out, mixed_out, lend_sem.at[1]).wait()
        sent(RIGHT, kv.at[pl.ds(0, heads - early + 2 * heads + 1)])
        sent(LEFT, kv.at[pl.ds(0, heads)])
        sent(ACROSS, kv.at[pl.ds(0, 7 * heads)])
        sent(LEND, lent)

    def at_inner():
        events = []
        for k in range(heads):
            events.append([("D", order_r[k], 0), ("E", order_l[k], 1), ("A", order_a[k], 2)])
        events[heads - 1].append(("F", order_l[0], None))
        for k in range(heads):
            events.append([("B", order_a[k], None), ("G", order_a[k], None)])
        for k in range(heads):
            events.append([("H", order_a[k], None)])
            if k > 0:
                events[-1].append(("F", order_l[k], None))
            if k == heads - 2:
                events.append([])
        lag = []
        ready = False

        for k, now in enumerate(events):
            for name, j, way in now:
                arrived(name, j, way)
                if name == "A":
                    send(mine("A"), j, MID, mine("E")).start()
                    send(mine("A"), j, RIGHT, beside).start()
                elif name == "B":
                    send(mine("B"), j, MID, mine("E")).start()
                elif name == "E":
                    send(mine("E"), j, LEFT, mine("A")).start()
                    if j == order_l[0]:
                        send(mine("E"), j, RIGHT, beside).start()
                elif name == "G" and j in keep:
                    send(mine("G"), j, LEFT, mine("A")).start()
                go_across(mine(name), j).start()
            if k == heads - 1:
                for j in order_l[1:]:
                    send(mine("E"), j, RIGHT, beside).start()
            todo = [(mine(name), j) for name, j, _ in now]
            if k < heads:
                go_across(across, k).wait_recv()
                todo.append((across, k))
            todo += [follow(name, j) for name, j in lag]
            give = [(name, j) for name, j in lag if (name == "G" and j not in keep) or (name == "H" and j in ship)]
            if give and not ready:
                ready = True
                pltpu.make_async_copy(lent, lent, lend_sem.at[0]).wait()
            back = []
            for name, j in give:
                for i, (n, c, jj) in enumerate(lends):
                    if n == name and jj == j:
                        mixed_out[i] = attended(lent[i], chip_of(n, c), jj)
                        back.append(i)
            for i in back:
                give_back(i).start()
            for owner, j in todo:
                attend(owner, j)
            lag = [(name, j) for name, j, _ in now]
        for name, j in lag:
            attend(*follow(name, j))
        sent(RIGHT, kv.at[pl.ds(0, heads - early + 2 * heads)])
        sent(LEFT, kv.at[pl.ds(0, heads - early + heads + len(keep))])
        sent(MID, kv.at[pl.ds(0, heads - early + 2 * heads)])
        sent(ACROSS, kv.at[pl.ds(0, 8 * heads)])
        sent(HALF_L, halves.at[pl.ds(0, 2 * early), 0])
        sent(LEND, mixed_out)

    if early:
        pl.when(corner)(at_corner)
        pl.when(inner)(at_inner)
        sent(HALF_R, halves.at[pl.ds(0, early), 0])
        sent(HALF_X, halves.at[pl.ds(0, early)])
    else:
        around()
    sent(LAT_OUT, lat.at[pl.ds(0, chips - 1)])
    sent(LAT_ON, lat.at[pl.ds(0, chips)])


def on_device(grid_y, cores, early, queries, latents, w_key, w_value):
    devices = lax.axis_size("ctx")
    heads, width, nope = w_key.shape
    query_rows = queries.shape[0]
    block = latents.shape[0]
    rows = block * devices
    anywhere = pl.BlockSpec(memory_space=pl.ANY)
    dma = pltpu.SemaphoreType.DMA
    return pl.pallas_call(
        functools.partial(kernel, grid_y, cores, early),
        out_shape=jax.ShapeDtypeStruct((query_rows, devices * heads * nope), jnp.bfloat16),
        in_specs=[anywhere] * 4,
        out_specs=pl.BlockSpec(memory_space=pltpu.VMEM),
        scratch_shapes=[
            pltpu.VMEM(queries.shape, jnp.bfloat16),
            pltpu.VMEM((devices, block, latents.shape[1]), jnp.bfloat16),
            pltpu.VMEM((heads, width, 2 * nope), jnp.bfloat16),
            pltpu.VMEM((2, rows, nope), jnp.bfloat16),
            pltpu.VMEM((devices * heads, 2, rows, nope), jnp.bfloat16),
            pltpu.VMEM((max(2 * early, 1), 2, width, nope), jnp.bfloat16),
            dma((3,)),
            dma((devices,)),
            dma((devices * heads,)),
            dma((max(2 * early, 1), 2)),
            dma((10,)),
            dma((3, heads)),
            pltpu.VMEM((8 if early else 1, query_rows, 2 * nope), jnp.bfloat16),
            pltpu.VMEM((8 if early else 1, query_rows, nope), jnp.bfloat16),
            dma((2,)),
        ],
        compiler_params=pltpu.CompilerParams(
            collective_id=0, has_side_effects=True, vmem_limit_bytes=50 * 1024 * 1024
        ),
    )(*(pltpu.with_memory_space_constraint(a, pltpu.HBM) for a in (queries, latents, w_key, w_value)))


def layout_of(mesh):
    group = list(mesh.devices.reshape(-1, mesh.shape["ctx"])[0])
    places = [tuple(d.coords) for d in group]
    chips = sorted(set(places))
    cores = len(group) // len(chips)
    varied = [axis for axis in range(3) if len({c[axis] for c in chips}) > 1]
    grid_y = 1
    if len(varied) == 2:
        fast = len({c[varied[0]] for c in chips})
        grid_y = 2 if fast == 2 else 1
    return grid_y, cores


def solution(mesh):
    grid_y, cores = layout_of(mesh)
    chips = mesh.shape["ctx"] // cores
    early = 2 if mesh.shape["rep"] == 2 and grid_y == 2 and chips // grid_y == 4 and cores == 2 else 0
    return jax.shard_map(
        functools.partial(on_device, grid_y, cores, early),
        mesh=mesh,
        in_specs=(
            P(("rep", "ctx"), None),
            P(("rep", "ctx"), None),
            P("ctx", None, None),
            P("ctx", None, None),
        ),
        out_specs=P(("rep", "ctx"), None),
        check_vma=False,
    )
```

```python
import functools
import math

import jax
import jax.numpy as jnp
from jax import lax
from jax.experimental import pallas as pl
from jax.experimental.pallas import tpu as pltpu
from jax.sharding import PartitionSpec as P

MESH = pl.DeviceIdType.MESH


def kernel(
    grid_y,
    cores,
    early,
    q_hbm,
    lat_hbm,
    wk_hbm,
    wv_hbm,
    o,
    q,
    lat,
    wkv,
    ropes,
    kv,
    halves,
    load_sem,
    lat_recv,
    kv_recv,
    half_recv,
    send_sem,
    part_recv,
    lent,
    mixed_out,
    lend_sem,
):
    devices = lat.shape[0]
    heads = wkv.shape[0]
    rows = kv.shape[2]
    nope = kv.shape[3]
    width = wkv.shape[1]
    rope = lat.shape[2] - width
    qk = nope + rope
    chips = devices // cores
    grid_z = chips // grid_y
    half = chips // 2
    scale = math.log2(math.e) / math.sqrt(qk)

    half_right = (heads + 1) // 2
    late = list(range(early, heads))
    order_r = late + list(range(early))
    order_l = order_r[half_right:] + order_r[:half_right]
    if early:
        order_l = [early - 1] + late[::-1] + list(range(early - 1))
    order_a = late + list(range(early))
    keep = order_a[:2] + order_a[3:]
    ship = order_a[:3]

    me = lax.axis_index("ctx")
    core = lax.rem(me, cores)
    my_chip = me // cores
    my_y = lax.rem(my_chip, grid_y)
    my_z = my_chip // grid_y
    place = (1 - my_y) * my_z + my_y * (2 * grid_z - 1 - my_z)

    def device_at(spot, which):
        spot = lax.rem(spot + 2 * chips, chips)
        y = spot // grid_z
        z = (1 - y) * spot + y * (2 * grid_z - 1 - spot)
        return (z * grid_y + y) * cores + which

    other_core = cores - 1 - core
    across = my_chip * cores + other_core
    right = device_at(place + 1, core)
    left = device_at(place - 1, core)
    rep = lax.axis_index("rep")
    top = my_z // (grid_z // 2)
    inward = 1 - 2 * top
    z_a = top * (grid_z - 1)
    z_g = (1 - top) * (grid_z - 1)
    corner = my_z == z_a
    inner = my_z != z_a

    def chip_of(name, which):
        z = {"A": z_a, "C": z_a + inward, "E": z_g - inward, "G": z_g}
        z |= {"B": z["A"], "D": z["C"], "F": z["E"], "H": z["G"]}
        y = my_y if name in "ACEG" else 1 - my_y
        return (z[name] * grid_y + y) * cores + which

    def mine(name):
        return chip_of(name, core)

    q_copy = pltpu.make_async_copy(q_hbm, q, load_sem.at[0])
    lat_copy = pltpu.make_async_copy(lat_hbm, lat.at[me], load_sem.at[1])
    lat_copy.start()
    for j in range(heads):
        pltpu.make_async_copy(wk_hbm.at[j], wkv.at[j, :, pl.ds(0, nope)], load_sem.at[2]).start()
        pltpu.make_async_copy(wv_hbm.at[j], wkv.at[j, :, pl.ds(nope, nope)], load_sem.at[2]).start()
    q_copy.start()

    barrier = pltpu.get_barrier_semaphore()

    plane = grid_y * cores
    beside = (my_z * grid_y + 1 - my_y) * cores + core
    steps = [(0, 1, True), (-1, 1, my_z > 0), (1, 1, my_z < grid_z - 1)]
    steps += [(-1, 0, my_z > 0), (1, 0, my_z < grid_z - 1), (-2, 0, my_z > 1), (2, 0, my_z < grid_z - 2)]

    def greet(sem):
        for dz, dy, there in steps:
            to = (beside if dy else me) + dz * plane

            def tell():
                pl.semaphore_signal(sem, inc=1, device_id={"ctx": to}, device_id_type=MESH)

            if there is True:
                tell()
            else:
                pl.when(there)(tell)

    greeted = 1
    for _, _, there in steps[1:]:
        greeted = greeted + lax.convert_element_type(there, jnp.int32)
    pl.semaphore_signal(barrier, inc=1, device_id={"ctx": across}, device_id_type=MESH)
    if early:
        greet(barrier)
        pl.semaphore_signal(barrier, inc=1, device_id={"rep": 1 - rep}, device_id_type=MESH)
        pl.semaphore_wait(barrier, greeted + 2)
    else:

        @pl.loop(1, chips)
        def _(d):
            pl.semaphore_signal(
                barrier, inc=1, device_id={"ctx": device_at(place + d, core)}, device_id_type=MESH
            )

        pl.semaphore_wait(barrier, chips)

    LAT_OUT, LAT_ON, RIGHT, LEFT, MID, ACROSS, HALF_R, HALF_L, HALF_X, LEND = range(10)

    near = me // (devices // 2)
    chips_half = chips // 2

    def near_chip(i):
        return near * chips_half + lax.rem(my_chip - near * chips_half + i, chips_half)

    def far_chip(i):
        return (1 - near) * chips_half + lax.rem(my_chip - near * chips_half + i, chips_half)

    def lat_out(owner, chip):
        return pltpu.make_async_remote_copy(
            src_ref=lat.at[owner],
            dst_ref=lat.at[owner],
            send_sem=send_sem.at[LAT_OUT],
            recv_sem=lat_recv.at[owner],
            device_id={"ctx": chip * cores + core},
            device_id_type=MESH,
        )

    def lat_on(owner):
        return pltpu.make_async_remote_copy(
            src_ref=lat.at[owner],
            dst_ref=lat.at[owner],
            send_sem=send_sem.at[LAT_ON],
            recv_sem=lat_recv.at[owner],
            device_id={"ctx": across},
            device_id_type=MESH,
        )

    lat_copy.wait()

    def lat_near(owner):
        @pl.loop(1, chips_half)
        def _(i):
            lat_out(owner, near_chip(i)).start()

    pieces = 4
    deep = width // pieces

    def half_out(src, j, way, target, piece):
        return pltpu.make_async_remote_copy(
            src_ref=src.at[j, pl.ds(piece * deep, deep)],
            dst_ref=halves.at[way * early + j, rep, pl.ds(piece * deep, deep)],
            send_sem=send_sem.at[HALF_R + way],
            recv_sem=half_recv.at[way * early + j, rep],
            device_id={"ctx": target},
            device_id_type=MESH,
        )

    def half_over(j, way, which):
        return pltpu.make_async_remote_copy(
            src_ref=halves.at[way * early + j, which],
            dst_ref=halves.at[way * early + j, which],
            send_sem=send_sem.at[HALF_X],
            recv_sem=half_recv.at[way * early + j, which],
            device_id={"rep": 1 - rep},
            device_id_type=MESH,
        )

    early_r = [j for j in order_r if j < early]
    early_l = [j for j in order_l if j < early]

    def relay(chip):
        owner = chip * cores + core
        lat_on(owner).wait_recv()
        lat_on(owner).start()

    def parity(owner, j):
        if heads % 2 == 0:
            return j % 2
        return lax.rem(owner * heads + j, 2)

    def weights_out(first, last):
        for which, src in ((0, wk_hbm), (1, wv_hbm)):

            @pl.when(rep == which)
            def _():
                for i in range(first, last):
                    half_out(src, early_r[i // pieces], 0, beside, i % pieces).start()

            @pl.when(jnp.logical_and(rep == which, inner))
            def _():
                for i in range(first, last):
                    for target in (mine("A"), mine("E")):
                        half_out(src, early_l[i // pieces], 1, target, i % pieces).start()

    lends = [("G", c, j) for j in order_a[2:3] for c in range(cores)]
    lends += [("H", c, j) for j in ship for c in range(cores)]

    def query_start(owner, j):
        odd = parity(owner, j)
        pair = owner * (heads // 2) + j // 2 if heads % 2 == 0 else (owner * heads + j) // 2
        return pl.multiple_of(pair * (2 * qk) + odd * nope, nope)

    def lend(i):
        name, which, j = lends[i]
        return pltpu.make_async_remote_copy(
            src_ref=q.at[:, pl.ds(query_start(chip_of(name, which), j), 2 * nope)],
            dst_ref=lent.at[i],
            send_sem=send_sem.at[LEND],
            recv_sem=lend_sem.at[0],
            device_id={"ctx": mine("C")},
            device_id_type=MESH,
        )

    def give_back(i):
        name, which, j = lends[i]
        at = pl.multiple_of((chip_of(name, which) * heads + j) * nope, nope)
        return pltpu.make_async_remote_copy(
            src_ref=mixed_out.at[i],
            dst_ref=o.at[:, pl.ds(at, nope)],
            send_sem=send_sem.at[LEND],
            recv_sem=lend_sem.at[1],
            device_id={"ctx": mine("A")},
            device_id_type=MESH,
        )

    def lend_out(first, last):
        @pl.when(corner)
        def _():
            for i in range(first, last):
                lend(i).start()

    if early:
        partner = lax.rem(my_chip + chips_half, chips)
        lat_out(me, partner).start()
        lat_near(me)
        lat_on(me).start()
        weights_out(0, pieces)
        q_copy.wait()
        lend_out(0, len(lends) // 2)
        lat_on(partner * cores + core).wait_recv()
        lat_near(partner * cores + core)
        lat_on(partner * cores + core).start()
        weights_out(pieces, early * pieces)
    else:
        lat_near(me)

        @pl.loop(0, chips_half)
        def _(i):
            lat_out(me, far_chip(i)).start()

        lat_on(me).start()

    @pl.loop(1, chips_half)
    def _(i):
        relay(near_chip(i))

    @pl.loop(0, chips_half)
    def _(i):
        lat_on(near_chip(i) * cores + other_core).wait_recv()

    pltpu.make_async_copy(wkv, wkv, load_sem.at[2]).wait()

    def send(owner, j, stream, target):
        return pltpu.make_async_remote_copy(
            src_ref=kv.at[owner * heads + j],
            dst_ref=kv.at[owner * heads + j],
            send_sem=send_sem.at[stream],
            recv_sem=kv_recv.at[owner * heads + j],
            device_id={"ctx": target},
            device_id_type=MESH,
        )

    def go_right(owner, j):
        return send(owner, j, RIGHT, right)

    def go_left(owner, j):
        return send(owner, j, LEFT, left)

    def go_across(owner, j):
        return send(owner, j, ACROSS, across)

    def part_of(item, part):
        return kv.at[item, :, pl.ds(pl.multiple_of(part * (rows // 2), rows // 2), rows // 2)]

    def half_hop(owner, j, part, is_first, way, stream, target):
        ref = part_of(owner * heads + j, part)
        sem = part_recv.at[way, j] if is_first else kv_recv.at[owner * heads + j]
        return pltpu.make_async_remote_copy(
            src_ref=ref,
            dst_ref=ref,
            send_sem=send_sem.at[stream],
            recv_sem=sem,
            device_id={"ctx": target},
            device_id_type=MESH,
        )

    def project_part(j, part):
        some = lat[pl.ds(part * (devices // 2), devices // 2)].reshape(rows // 2, lat.shape[2])[:, :width]
        both = jnp.dot(some, wkv[j], preferred_element_type=jnp.float32)
        keys = both[:, :nope]
        if parity(me, j) == 1:
            keys = jnp.concatenate([keys[:, rope:], keys[:, :rope]], axis=1)
        at = pl.ds(pl.multiple_of(part * (rows // 2), rows // 2), rows // 2)
        kv[me * heads + j, 0, at] = keys.astype(jnp.bfloat16)
        kv[me * heads + j, 1, at] = both[:, nope:].astype(jnp.bfloat16)

    late_r = [j for j in order_r if j >= early]
    late_l = [j for j in order_l if j >= early]

    def late_out(part, is_first):
        for j in late:
            project_part(j, part)
        for j in late_r:
            half_hop(me, j, part, is_first, 0, RIGHT, beside).start()

        @pl.when(corner)
        def _():
            for j in late:
                half_hop(me, j, part, is_first, 2, LEFT, mine("C")).start()

        @pl.when(inner)
        def _():
            for j in late_l:
                half_hop(me, j, part, is_first, 1, LEFT, mine("A")).start()
                half_hop(me, j, part, is_first, 1, MID, mine("E")).start()

    def store(owner, j, keys, values):
        odd = parity(owner, j)
        turned = jnp.concatenate([keys[:, rope:], keys[:, :rope]], axis=1)
        if isinstance(odd, int):
            keys = turned if odd else keys
        else:
            keys = jnp.where(odd == 1, turned, keys)
        kv[owner * heads + j, 0] = keys.astype(jnp.bfloat16)
        kv[owner * heads + j, 1] = values.astype(jnp.bfloat16)

    def project(j):
        both = jnp.dot(
            lat[...].reshape(rows, lat.shape[2])[:, :width], wkv[j], preferred_element_type=jnp.float32
        )
        store(me, j, both[:, :nope], both[:, nope:])

    def project_arrived(owner, j, way):
        some = lat[...].reshape(rows, lat.shape[2])[:, :width]
        slot = way * early + j
        keys = jnp.dot(some, halves[slot, 0], preferred_element_type=jnp.float32)
        values = jnp.dot(some, halves[slot, 1], preferred_element_type=jnp.float32)
        store(owner, j, keys, values)

    def hand_over(*slots):
        for way, place_in in slots:
            j = (early_r, early_l)[way][place_in]
            half_over(j, way, rep).wait_recv()
            half_over(j, way, rep).start()

    if early:
        late_out(near, True)
        hand_over((1, 0))

    @pl.loop(1 if early else 0, chips_half)
    def _(i):
        relay(far_chip(i))

    @pl.loop(0, chips_half)
    def _(i):
        lat_on(far_chip(i) * cores + other_core).wait_recv()

    if early:
        late_out(1 - near, False)
    else:
        for j in late:
            project(j)
            go_right(me, j).start()
            go_left(me, j).start()
    for j in range(early):
        project(j)
    if early:

        @pl.when(corner)
        def _():
            for j in range(early):
                send(me, j, LEFT, mine("C")).start()

        lend_out(len(lends) // 2, len(lends))
    for j in range(heads):
        go_across(me, j).start()

    rope_part = lat[...].reshape(rows, lat.shape[2])[:, width:]
    blank = jnp.zeros_like(rope_part)
    ropes[0] = jnp.concatenate([rope_part, blank], axis=1)
    ropes[1] = jnp.concatenate([blank, rope_part], axis=1)

    if not early:
        q_copy.wait()

    lane = lax.broadcasted_iota(jnp.int32, (rows, nope), 1)
    upper = lane >= rope

    def attended(queries, owner, j):
        odd = parity(owner, j)
        head = owner * heads + j
        keys = kv[head, 0]
        values = kv[head, 1]

        def even_keys():
            return jnp.concatenate([keys, ropes[0]], axis=1)

        def odd_keys():
            return jnp.concatenate(
                [jnp.where(upper, keys, jnp.zeros_like(keys)), jnp.where(upper, ropes[1], keys)], axis=1
            )

        if isinstance(odd, int):
            keys_full = odd_keys() if odd else even_keys()
        else:
            keys_full = jnp.where(odd == 1, odd_keys(), even_keys())
        scores = lax.dot_general(
            queries, keys_full, (((1,), (1,)), ((), ())), preferred_element_type=jnp.float32
        )
        row_max = jnp.max(scores, axis=1, keepdims=True)
        weights = jnp.exp2((scores - row_max) * scale)
        total = jnp.sum(weights, axis=1, keepdims=True)
        mixed = jnp.dot(weights.astype(jnp.bfloat16), values, preferred_element_type=jnp.float32)
        return (mixed * (1.0 / total)).astype(jnp.bfloat16)

    def attend(owner, j):
        at = pl.multiple_of((owner * heads + j) * nope, nope)
        o[:, pl.ds(at, nope)] = attended(q[:, pl.ds(query_start(owner, j), 2 * nope)], owner, j)

    attend(me, 0)
    if early:
        hand_over(*[(1, i) for i in range(1, early)], *[(0, i) for i in range(early)])
    for i in range(1, early):
        attend(me, i)
    for j in range(max(early, 1), heads):
        attend(me, j)

    def sent(stream, ref):
        pltpu.make_async_remote_copy(
            src_ref=ref,
            dst_ref=ref,
            send_sem=send_sem.at[stream],
            recv_sem=send_sem.at[stream],
            device_id={"ctx": across},
            device_id_type=MESH,
        ).wait_send()

    def around():
        def others(s):
            return (device_at(place - s, other_core), device_at(place + s, other_core))

        def attend_others(s, pos):
            pair = list(zip(others(s), (order_r, order_l)))
            for owner, js in pair:
                go_across(owner, js[pos]).wait_recv()
            return [(owner, js[pos]) for owner, js in pair]

        def ring_step(s, first, last):
            from_left = device_at(place - s, core)
            from_right = device_at(place + s, core)
            for pos in range(heads):
                jr, jl = order_r[pos], order_l[pos]
                for j, way, owner, go in ((jr, 0, from_left, go_right), (jl, 1, from_right, go_left)):
                    go(owner, j).wait_recv()
                    if not last or pos < (half_right if way == 0 else heads - half_right):
                        go(owner, j).start()
                    go_across(owner, j).start()
                todo = [(from_left, jr), (from_right, jl)]
                if first:
                    go_across(across, pos).wait_recv()
                    todo.append((across, pos))
                if pos > 0:
                    todo += attend_others(s, pos - 1)
                elif not first:
                    todo += attend_others(s - 1, heads - 1)
                for owner, j in todo:
                    attend(owner, j)

        ring_step(1, True, half == 2)
        if half > 3:

            @pl.loop(2, half - 1)
            def _(s):
                ring_step(s, False, False)

        if half > 2:
            ring_step(half - 1, False, True)

        far = device_at(place + half, core)
        far_other = device_at(place + half, other_core)
        todo = attend_others(half - 1, heads - 1)
        for pos in range(half_right):
            arrivals = [(order_r[pos], go_right)]
            if pos < heads - half_right:
                arrivals.append((order_l[pos], go_left))
            for j, go in arrivals:
                go(far, j).wait_recv()
                go_across(far, j).start()
                todo.append((far, j))
            for owner, j in todo:
                attend(owner, j)
            for j, _ in arrivals:
                go_across(far_other, j).wait_recv()
            for j, _ in arrivals:
                attend(far_other, j)
            todo = []

        sent(RIGHT, kv.at[pl.ds(0, (half - 1) * heads + half_right)])
        sent(LEFT, kv.at[pl.ds(0, half * heads - half_right)])
        sent(ACROSS, kv.at[pl.ds(0, chips * heads)])

    def arrived(name, j, way):
        owner = mine(name)
        direct = {0: "B" if name == "B" else "D", 1: "C" if name == "C" else "E", 2: "A"}
        if way is None or name != direct[way]:
            go_across(owner, j).wait_recv()
        elif way < 2 and j < early:
            half_over(j, way, 1 - rep).wait_recv()
            project_arrived(owner, j, way)
        elif j >= early:
            near_part = owner // (devices // 2)
            half_hop(owner, j, near_part, True, way, RIGHT, across).wait_recv()
            half_hop(owner, j, 1 - near_part, False, way, RIGHT, across).wait_recv()
        else:
            go_across(owner, j).wait_recv()

    def follow(name, j):
        owner = chip_of(name, other_core)
        go_across(owner, j).wait_recv()
        return owner, j

    def at_corner():
        from_z = [("C", j, 1) for j in order_l] + [("E", j, None) for j in order_l] + [("G", j, None) for j in keep]
        from_y = [("B", j, 0) for j in order_r] + [("D", j, None) for j in order_l] + [("F", j, None) for j in order_l]
        from_y += [("H", order_a[3], None)]
        lag = []
        for k in range(len(from_y)):
            now = from_z[k : k + 1] + from_y[k : k + 1]
            for name, j, way in now:
                arrived(name, j, way)
                if name in "CE" or (name == "G" and j == order_a[3]):
                    send(mine(name), j, RIGHT, beside).start()
                go_across(mine(name), j).start()
            todo = [(mine(name), j) for name, j, _ in now]
            if k < heads:
                go_across(across, k).wait_recv()
                todo.append((across, k))
            todo += [follow(name, j) for name, j in lag]
            for owner, j in todo:
                attend(owner, j)
            lag = [(name, j) for name, j, _ in now]
        for name, j in lag:
            attend(*follow(name, j))
        pltpu.make_async_copy(mixed_out, mixed_out, lend_sem.at[1]).wait()
        sent(RIGHT, kv.at[pl.ds(0, heads - early + 2 * heads + 1)])
        sent(LEFT, kv.at[pl.ds(0, heads)])
        sent(ACROSS, kv.at[pl.ds(0, 7 * heads)])
        sent(LEND, lent)

    def at_inner():
        events = []
        for k in range(heads):
            events.append([("E", order_l[k], 1), ("A", order_a[k], 2), ("D", order_r[k], 0)])
        events[heads - 1].append(("F", order_l[0], None))
        for k in range(heads):
            events.append([("B", order_a[k], None), ("G", order_a[k], None)])
        for k in range(heads):
            events.append([("H", order_a[k], None)])
            if k > 0:
                events[-1].append(("F", order_l[k], None))
            if k == heads - 2:
                events.append([])
        lag = []
        ready = False

        for k, now in enumerate(events):
            for name, j, way in now:
                arrived(name, j, way)
                if name == "A":
                    send(mine("A"), j, MID, mine("E")).start()
                    send(mine("A"), j, RIGHT, beside).start()
                elif name == "B":
                    send(mine("B"), j, MID, mine("E")).start()
                elif name == "E":
                    send(mine("E"), j, LEFT, mine("A")).start()
                    if j == order_l[0]:
                        send(mine("E"), j, RIGHT, beside).start()
                elif name == "G" and j in keep:
                    send(mine("G"), j, LEFT, mine("A")).start()
                go_across(mine(name), j).start()
            if k == heads - 1:
                for j in order_l[1:]:
                    send(mine("E"), j, RIGHT, beside).start()
            todo = [(mine(name), j) for name, j, _ in now]
            if k < heads:
                go_across(across, k).wait_recv()
                todo.append((across, k))
            todo += [follow(name, j) for name, j in lag]
            give = [(name, j) for name, j in lag if (name == "G" and j not in keep) or (name == "H" and j in ship)]
            if give and not ready:
                ready = True
                pltpu.make_async_copy(lent, lent, lend_sem.at[0]).wait()
            back = []
            for name, j in give:
                for i, (n, c, jj) in enumerate(lends):
                    if n == name and jj == j:
                        mixed_out[i] = attended(lent[i], chip_of(n, c), jj)
                        back.append(i)
            for i in back:
                give_back(i).start()
            for owner, j in todo:
                attend(owner, j)
            lag = [(name, j) for name, j, _ in now]
        for name, j in lag:
            attend(*follow(name, j))
        sent(RIGHT, kv.at[pl.ds(0, heads - early + 2 * heads)])
        sent(LEFT, kv.at[pl.ds(0, heads - early + heads + len(keep))])
        sent(MID, kv.at[pl.ds(0, heads - early + 2 * heads)])
        sent(ACROSS, kv.at[pl.ds(0, 8 * heads)])
        sent(HALF_L, halves.at[pl.ds(0, 2 * early), 0])
        sent(LEND, mixed_out)

    if early:
        pl.when(corner)(at_corner)
        pl.when(inner)(at_inner)
        sent(HALF_R, halves.at[pl.ds(0, early), 0])
        sent(HALF_X, halves.at[pl.ds(0, early)])
    else:
        around()
    sent(LAT_OUT, lat.at[pl.ds(0, chips - 1)])
    sent(LAT_ON, lat.at[pl.ds(0, chips)])


def on_device(grid_y, cores, early, queries, latents, w_key, w_value):
    devices = lax.axis_size("ctx")
    heads, width, nope = w_key.shape
    query_rows = queries.shape[0]
    block = latents.shape[0]
    rows = block * devices
    anywhere = pl.BlockSpec(memory_space=pl.ANY)
    dma = pltpu.SemaphoreType.DMA
    return pl.pallas_call(
        functools.partial(kernel, grid_y, cores, early),
        out_shape=jax.ShapeDtypeStruct((query_rows, devices * heads * nope), jnp.bfloat16),
        in_specs=[anywhere] * 4,
        out_specs=pl.BlockSpec(memory_space=pltpu.VMEM),
        scratch_shapes=[
            pltpu.VMEM(queries.shape, jnp.bfloat16),
            pltpu.VMEM((devices, block, latents.shape[1]), jnp.bfloat16),
            pltpu.VMEM((heads, width, 2 * nope), jnp.bfloat16),
            pltpu.VMEM((2, rows, nope), jnp.bfloat16),
            pltpu.VMEM((devices * heads, 2, rows, nope), jnp.bfloat16),
            pltpu.VMEM((max(2 * early, 1), 2, width, nope), jnp.bfloat16),
            dma((3,)),
            dma((devices,)),
            dma((devices * heads,)),
            dma((max(2 * early, 1), 2)),
            dma((10,)),
            dma((3, heads)),
            pltpu.VMEM((8 if early else 1, query_rows, 2 * nope), jnp.bfloat16),
            pltpu.VMEM((8 if early else 1, query_rows, nope), jnp.bfloat16),
            dma((2,)),
        ],
        compiler_params=pltpu.CompilerParams(
            collective_id=0, has_side_effects=True, vmem_limit_bytes=50 * 1024 * 1024
        ),
    )(*(pltpu.with_memory_space_constraint(a, pltpu.HBM) for a in (queries, latents, w_key, w_value)))


def layout_of(mesh):
    group = list(mesh.devices.reshape(-1, mesh.shape["ctx"])[0])
    places = [tuple(d.coords) for d in group]
    chips = sorted(set(places))
    cores = len(group) // len(chips)
    varied = [axis for axis in range(3) if len({c[axis] for c in chips}) > 1]
    grid_y = 1
    if len(varied) == 2:
        fast = len({c[varied[0]] for c in chips})
        grid_y = 2 if fast == 2 else 1
    return grid_y, cores


def solution(mesh):
    grid_y, cores = layout_of(mesh)
    chips = mesh.shape["ctx"] // cores
    early = 2 if mesh.shape["rep"] == 2 and grid_y == 2 and chips // grid_y == 4 and cores == 2 else 0
    return jax.shard_map(
        functools.partial(on_device, grid_y, cores, early),
        mesh=mesh,
        in_specs=(
            P(("rep", "ctx"), None),
            P(("rep", "ctx"), None),
            P("ctx", None, None),
            P("ctx", None, None),
        ),
        out_specs=P(("rep", "ctx"), None),
        check_vma=False,
    )
```

```python
import functools
import math

import jax
import jax.numpy as jnp
from jax import lax
from jax.experimental import pallas as pl
from jax.experimental.pallas import tpu as pltpu
from jax.sharding import PartitionSpec as P

MESH = pl.DeviceIdType.MESH


def kernel(
    grid_y,
    cores,
    early,
    q_hbm,
    lat_hbm,
    wk_hbm,
    wv_hbm,
    o,
    q,
    lat,
    wkv,
    ropes,
    kv,
    halves,
    load_sem,
    lat_recv,
    kv_recv,
    half_recv,
    send_sem,
    part_recv,
    lent,
    mixed_out,
    lend_sem,
):
    devices = lat.shape[0]
    heads = wkv.shape[0]
    rows = kv.shape[2]
    nope = kv.shape[3]
    width = wkv.shape[1]
    rope = lat.shape[2] - width
    qk = nope + rope
    chips = devices // cores
    grid_z = chips // grid_y
    half = chips // 2
    scale = math.log2(math.e) / math.sqrt(qk)

    half_right = (heads + 1) // 2
    late = list(range(early, heads))
    order_r = late + list(range(early))
    order_l = order_r[half_right:] + order_r[:half_right]
    if early:
        order_l = [early - 1] + late[::-1] + list(range(early - 1))
        order_r = list(range(heads))
    order_a = late + list(range(early))
    keep = order_a[:2] + order_a[3:]
    ship = order_a[:3]

    me = lax.axis_index("ctx")
    core = lax.rem(me, cores)
    my_chip = me // cores
    my_y = lax.rem(my_chip, grid_y)
    my_z = my_chip // grid_y
    place = (1 - my_y) * my_z + my_y * (2 * grid_z - 1 - my_z)

    def device_at(spot, which):
        spot = lax.rem(spot + 2 * chips, chips)
        y = spot // grid_z
        z = (1 - y) * spot + y * (2 * grid_z - 1 - spot)
        return (z * grid_y + y) * cores + which

    other_core = cores - 1 - core
    across = my_chip * cores + other_core
    right = device_at(place + 1, core)
    left = device_at(place - 1, core)
    rep = lax.axis_index("rep")
    top = my_z // (grid_z // 2)
    inward = 1 - 2 * top
    z_a = top * (grid_z - 1)
    z_g = (1 - top) * (grid_z - 1)
    corner = my_z == z_a
    inner = my_z != z_a

    def chip_of(name, which):
        z = {"A": z_a, "C": z_a + inward, "E": z_g - inward, "G": z_g}
        z |= {"B": z["A"], "D": z["C"], "F": z["E"], "H": z["G"]}
        y = my_y if name in "ACEG" else 1 - my_y
        return (z[name] * grid_y + y) * cores + which

    def mine(name):
        return chip_of(name, core)

    barrier = pltpu.get_barrier_semaphore()

    plane = grid_y * cores
    beside = (my_z * grid_y + 1 - my_y) * cores + core
    steps = [(0, 1, True), (-1, 1, my_z > 0), (1, 1, my_z < grid_z - 1)]
    steps += [(-1, 0, my_z > 0), (1, 0, my_z < grid_z - 1), (-2, 0, my_z > 1), (2, 0, my_z < grid_z - 2)]

    def greet(sem):
        for dz, dy, there in steps:
            to = (beside if dy else me) + dz * plane

            def tell():
                pl.semaphore_signal(sem, inc=1, device_id={"ctx": to}, device_id_type=MESH)

            if there is True:
                tell()
            else:
                pl.when(there)(tell)

    greeted = 1
    for _, _, there in steps[1:]:
        greeted = greeted + lax.convert_element_type(there, jnp.int32)
    if early:
        greet(barrier)
        pl.semaphore_signal(barrier, inc=1, device_id={"rep": 1 - rep}, device_id_type=MESH)
    else:

        @pl.loop(1, chips)
        def _(d):
            pl.semaphore_signal(
                barrier, inc=1, device_id={"ctx": device_at(place + d, core)}, device_id_type=MESH
            )

    pl.semaphore_signal(barrier, inc=1, device_id={"ctx": across}, device_id_type=MESH)

    q_copy = pltpu.make_async_copy(q_hbm, q, load_sem.at[0])
    lat_copy = pltpu.make_async_copy(lat_hbm, lat.at[me], load_sem.at[1])
    lat_copy.start()
    for j in range(heads):
        pltpu.make_async_copy(wk_hbm.at[j], wkv.at[j, :, pl.ds(0, nope)], load_sem.at[2]).start()
        pltpu.make_async_copy(wv_hbm.at[j], wkv.at[j, :, pl.ds(nope, nope)], load_sem.at[2]).start()
    q_copy.start()

    pl.semaphore_wait(barrier, greeted + 2 if early else chips)

    LAT_OUT, LAT_ON, RIGHT, LEFT, MID, ACROSS, HALF_R, HALF_L, HALF_X, LEND = range(10)

    near = me // (devices // 2)
    chips_half = chips // 2

    def near_chip(i):
        return near * chips_half + lax.rem(my_chip - near * chips_half + i, chips_half)

    def far_chip(i):
        return (1 - near) * chips_half + lax.rem(my_chip - near * chips_half + i, chips_half)

    def lat_out(owner, chip):
        return pltpu.make_async_remote_copy(
            src_ref=lat.at[owner],
            dst_ref=lat.at[owner],
            send_sem=send_sem.at[LAT_OUT],
            recv_sem=lat_recv.at[owner],
            device_id={"ctx": chip * cores + core},
            device_id_type=MESH,
        )

    def lat_on(owner):
        return pltpu.make_async_remote_copy(
            src_ref=lat.at[owner],
            dst_ref=lat.at[owner],
            send_sem=send_sem.at[LAT_ON],
            recv_sem=lat_recv.at[owner],
            device_id={"ctx": across},
            device_id_type=MESH,
        )

    lat_copy.wait()

    def lat_near(owner):
        @pl.loop(1, chips_half)
        def _(i):
            lat_out(owner, near_chip(i)).start()

    pieces = 4
    deep = width // pieces

    def half_out(src, j, way, target, piece):
        return pltpu.make_async_remote_copy(
            src_ref=src.at[j, pl.ds(piece * deep, deep)],
            dst_ref=halves.at[way * heads + j, rep, pl.ds(piece * deep, deep)],
            send_sem=send_sem.at[HALF_R + way],
            recv_sem=half_recv.at[way * heads + j, rep],
            device_id={"ctx": target},
            device_id_type=MESH,
        )

    def half_over(j, way, which):
        return pltpu.make_async_remote_copy(
            src_ref=halves.at[way * heads + j, which],
            dst_ref=halves.at[way * heads + j, which],
            send_sem=send_sem.at[HALF_X],
            recv_sem=half_recv.at[way * heads + j, which],
            device_id={"rep": 1 - rep},
            device_id_type=MESH,
        )

    early_r = order_r
    early_l = [j for j in order_l if j < early]

    def relay(chip):
        owner = chip * cores + core
        lat_on(owner).wait_recv()
        lat_on(owner).start()

    def parity(owner, j):
        if heads % 2 == 0:
            return j % 2
        return lax.rem(owner * heads + j, 2)

    def weights_out(first, last):
        for which, src in ((0, wk_hbm), (1, wv_hbm)):

            @pl.when(rep == which)
            def _():
                for i in range(first, last):
                    half_out(src, early_r[i // pieces], 0, beside, i % pieces).start()

            @pl.when(jnp.logical_and(rep == which, inner))
            def _():
                for i in range(first, min(last, early * pieces)):
                    for target in (mine("A"), mine("E")):
                        half_out(src, early_l[i // pieces], 1, target, i % pieces).start()

    lends = [("G", c, j) for j in order_a[2:3] for c in range(cores)]
    lends += [("H", c, j) for j in ship for c in range(cores)]

    def query_start(owner, j):
        odd = parity(owner, j)
        pair = owner * (heads // 2) + j // 2 if heads % 2 == 0 else (owner * heads + j) // 2
        return pl.multiple_of(pair * (2 * qk) + odd * nope, nope)

    def lend(i):
        name, which, j = lends[i]
        return pltpu.make_async_remote_copy(
            src_ref=q.at[:, pl.ds(query_start(chip_of(name, which), j), 2 * nope)],
            dst_ref=lent.at[i],
            send_sem=send_sem.at[LEND],
            recv_sem=lend_sem.at[0],
            device_id={"ctx": mine("C")},
            device_id_type=MESH,
        )

    def give_back(i):
        name, which, j = lends[i]
        at = pl.multiple_of((chip_of(name, which) * heads + j) * nope, nope)
        return pltpu.make_async_remote_copy(
            src_ref=mixed_out.at[i],
            dst_ref=o.at[:, pl.ds(at, nope)],
            send_sem=send_sem.at[LEND],
            recv_sem=lend_sem.at[1],
            device_id={"ctx": mine("A")},
            device_id_type=MESH,
        )

    def lend_out(first, last):
        @pl.when(corner)
        def _():
            for i in range(first, last):
                lend(i).start()

    if early:

        def lat_to(owner, names):
            for name in names:
                lat_out(owner, mine(name) // cores).start()

        def lat_take(names):
            for name in names:
                lat_on(mine(name)).wait_recv()
                lat_on(mine(name)).start()

        def lat_meet(names):
            for name in names:
                lat_on(chip_of(name, other_core)).wait_recv()

        pl.when(corner)(lambda: lat_to(me, "EDCB"))
        pl.when(inner)(lambda: lat_to(me, "GFBEAD"))
        lat_on(me).start()
        weights_out(0, pieces)
        q_copy.wait()
        lend_out(0, len(lends) // 2)

        @pl.when(inner)
        def _():
            lat_take("G")
            lat_to(mine("G"), "BAD")
            lat_take("F")
            lat_to(mine("F"), "A")

        weights_out(pieces, heads * pieces)

        @pl.when(corner)
        def _():
            lat_take("BCD")
            lat_meet("ABCD")

        @pl.when(inner)
        def _():
            lat_take("ABDE")
            lat_meet("ABCDEF")

    else:
        lat_near(me)

        @pl.loop(0, chips_half)
        def _(i):
            lat_out(me, far_chip(i)).start()

        lat_on(me).start()

        @pl.loop(1, chips_half)
        def _(i):
            relay(near_chip(i))

        @pl.loop(0, chips_half)
        def _(i):
            lat_on(near_chip(i) * cores + other_core).wait_recv()

    pltpu.make_async_copy(wkv, wkv, load_sem.at[2]).wait()

    def send(owner, j, stream, target):
        return pltpu.make_async_remote_copy(
            src_ref=kv.at[owner * heads + j],
            dst_ref=kv.at[owner * heads + j],
            send_sem=send_sem.at[stream],
            recv_sem=kv_recv.at[owner * heads + j],
            device_id={"ctx": target},
            device_id_type=MESH,
        )

    def go_right(owner, j):
        return send(owner, j, RIGHT, right)

    def go_left(owner, j):
        return send(owner, j, LEFT, left)

    def go_across(owner, j):
        return send(owner, j, ACROSS, across)

    def piece_of(side, quarters, is_first):
        size = quarters if is_first else 4 - quarters
        return (side if is_first else 1 - side) * (4 - size), size

    def half_hop(owner, j, piece, is_first, way, stream, target):
        begin, size = piece
        quarter = rows // 4
        ref = kv.at[owner * heads + j, :, pl.ds(pl.multiple_of(begin * quarter, quarter), size * quarter)]
        sem = part_recv.at[way, j] if is_first else kv_recv.at[owner * heads + j]
        return pltpu.make_async_remote_copy(
            src_ref=ref,
            dst_ref=ref,
            send_sem=send_sem.at[stream],
            recv_sem=sem,
            device_id={"ctx": target},
            device_id_type=MESH,
        )

    def project_part(j, piece):
        begin, size = piece
        some = lat[pl.ds(begin * (devices // 4), size * (devices // 4))]
        some = some.reshape(size * rows // 4, lat.shape[2])[:, :width]
        both = jnp.dot(some, wkv[j], preferred_element_type=jnp.float32)
        keys = both[:, :nope]
        if parity(me, j) == 1:
            keys = jnp.concatenate([keys[:, rope:], keys[:, :rope]], axis=1)
        at = pl.ds(pl.multiple_of(begin * (rows // 4), rows // 4), size * (rows // 4))
        kv[me * heads + j, 0, at] = keys.astype(jnp.bfloat16)
        kv[me * heads + j, 1, at] = both[:, nope:].astype(jnp.bfloat16)

    late_l = [j for j in order_l if j >= early]

    def late_out(is_first):
        @pl.when(corner)
        def _():
            piece = piece_of(top, 2, is_first)
            for j in late:
                project_part(j, piece)
            for j in late:
                half_hop(me, j, piece, is_first, 2, LEFT, mine("C")).start()

        @pl.when(inner)
        def _():
            piece = piece_of(top, 3, is_first)
            for j in late:
                project_part(j, piece)
            for j in late_l:
                half_hop(me, j, piece, is_first, 1, LEFT, mine("A")).start()
                half_hop(me, j, piece, is_first, 1, MID, mine("E")).start()

    def store(owner, j, keys, values):
        odd = parity(owner, j)
        turned = jnp.concatenate([keys[:, rope:], keys[:, :rope]], axis=1)
        if isinstance(odd, int):
            keys = turned if odd else keys
        else:
            keys = jnp.where(odd == 1, turned, keys)
        kv[owner * heads + j, 0] = keys.astype(jnp.bfloat16)
        kv[owner * heads + j, 1] = values.astype(jnp.bfloat16)

    def project(j):
        both = jnp.dot(
            lat[...].reshape(rows, lat.shape[2])[:, :width], wkv[j], preferred_element_type=jnp.float32
        )
        store(me, j, both[:, :nope], both[:, nope:])

    def project_arrived(owner, j, way):
        some = lat[...].reshape(rows, lat.shape[2])[:, :width]
        slot = way * heads + j
        keys = jnp.dot(some, halves[slot, 0], preferred_element_type=jnp.float32)
        values = jnp.dot(some, halves[slot, 1], preferred_element_type=jnp.float32)
        store(owner, j, keys, values)

    def hand_over(*slots):
        for way, place_in in slots:
            j = (early_r, early_l)[way][place_in]
            half_over(j, way, rep).wait_recv()
            half_over(j, way, rep).start()

    if early:
        late_out(True)
        hand_over((1, 0))

        @pl.when(corner)
        def _():
            lat_take("EGFH")
            lat_meet("EGFH")

        @pl.when(inner)
        def _():
            lat_take("H")
            lat_meet("GH")

        late_out(False)
    else:
        @pl.loop(0, chips_half)
        def _(i):
            relay(far_chip(i))

        @pl.loop(0, chips_half)
        def _(i):
            lat_on(far_chip(i) * cores + other_core).wait_recv()
        for j in late:
            project(j)
            go_right(me, j).start()
            go_left(me, j).start()

    for j in range(early):
        project(j)
    if early:

        @pl.when(corner)
        def _():
            for j in range(early):
                send(me, j, LEFT, mine("C")).start()

        lend_out(len(lends) // 2, len(lends))
    for j in range(heads):
        go_across(me, j).start()

    rope_part = lat[...].reshape(rows, lat.shape[2])[:, width:]
    blank = jnp.zeros_like(rope_part)
    ropes[0] = jnp.concatenate([rope_part, blank], axis=1)
    ropes[1] = jnp.concatenate([blank, rope_part], axis=1)

    if not early:
        q_copy.wait()

    lane = lax.broadcasted_iota(jnp.int32, (rows, nope), 1)
    upper = lane >= rope

    def attended(queries, owner, j):
        odd = parity(owner, j)
        head = owner * heads + j
        keys = kv[head, 0]
        values = kv[head, 1]

        def even_keys():
            return jnp.concatenate([keys, ropes[0]], axis=1)

        def odd_keys():
            return jnp.concatenate(
                [jnp.where(upper, keys, jnp.zeros_like(keys)), jnp.where(upper, ropes[1], keys)], axis=1
            )

        if isinstance(odd, int):
            keys_full = odd_keys() if odd else even_keys()
        else:
            keys_full = jnp.where(odd == 1, odd_keys(), even_keys())
        scores = lax.dot_general(
            queries, keys_full, (((1,), (1,)), ((), ())), preferred_element_type=jnp.float32
        )
        row_max = jnp.max(scores, axis=1, keepdims=True)
        weights = jnp.exp2((scores - row_max) * scale)
        total = jnp.sum(weights, axis=1, keepdims=True)
        mixed = jnp.dot(weights.astype(jnp.bfloat16), values, preferred_element_type=jnp.float32)
        return (mixed * (1.0 / total)).astype(jnp.bfloat16)

    def attend(owner, j):
        at = pl.multiple_of((owner * heads + j) * nope, nope)
        o[:, pl.ds(at, nope)] = attended(q[:, pl.ds(query_start(owner, j), 2 * nope)], owner, j)

    attend(me, 0)
    if early:
        hand_over(*[(1, i) for i in range(1, early)], *[(0, i) for i in range(early)])
    for i in range(1, early):
        attend(me, i)
    for j in range(max(early, 1), heads):
        attend(me, j)

    def sent(stream, ref):
        pltpu.make_async_remote_copy(
            src_ref=ref,
            dst_ref=ref,
            send_sem=send_sem.at[stream],
            recv_sem=send_sem.at[stream],
            device_id={"ctx": across},
            device_id_type=MESH,
        ).wait_send()

    def around():
        def others(s):
            return (device_at(place - s, other_core), device_at(place + s, other_core))

        def attend_others(s, pos):
            pair = list(zip(others(s), (order_r, order_l)))
            for owner, js in pair:
                go_across(owner, js[pos]).wait_recv()
            return [(owner, js[pos]) for owner, js in pair]

        def ring_step(s, first, last):
            from_left = device_at(place - s, core)
            from_right = device_at(place + s, core)
            for pos in range(heads):
                jr, jl = order_r[pos], order_l[pos]
                for j, way, owner, go in ((jr, 0, from_left, go_right), (jl, 1, from_right, go_left)):
                    go(owner, j).wait_recv()
                    if not last or pos < (half_right if way == 0 else heads - half_right):
                        go(owner, j).start()
                    go_across(owner, j).start()
                todo = [(from_left, jr), (from_right, jl)]
                if first:
                    go_across(across, pos).wait_recv()
                    todo.append((across, pos))
                if pos > 0:
                    todo += attend_others(s, pos - 1)
                elif not first:
                    todo += attend_others(s - 1, heads - 1)
                for owner, j in todo:
                    attend(owner, j)

        ring_step(1, True, half == 2)
        if half > 3:

            @pl.loop(2, half - 1)
            def _(s):
                ring_step(s, False, False)

        if half > 2:
            ring_step(half - 1, False, True)

        far = device_at(place + half, core)
        far_other = device_at(place + half, other_core)
        todo = attend_others(half - 1, heads - 1)
        for pos in range(half_right):
            arrivals = [(order_r[pos], go_right)]
            if pos < heads - half_right:
                arrivals.append((order_l[pos], go_left))
            for j, go in arrivals:
                go(far, j).wait_recv()
                go_across(far, j).start()
                todo.append((far, j))
            for owner, j in todo:
                attend(owner, j)
            for j, _ in arrivals:
                go_across(far_other, j).wait_recv()
            for j, _ in arrivals:
                attend(far_other, j)
            todo = []

        sent(RIGHT, kv.at[pl.ds(0, (half - 1) * heads + half_right)])
        sent(LEFT, kv.at[pl.ds(0, half * heads - half_right)])
        sent(ACROSS, kv.at[pl.ds(0, chips * heads)])

    def arrived(name, j, way):
        owner = mine(name)
        direct = {0: "B" if name == "B" else "D", 1: "C" if name == "C" else "E", 2: "A"}
        if way is None or name != direct[way]:
            go_across(owner, j).wait_recv()
        elif way == 0 or (way == 1 and j < early):
            half_over(j, way, 1 - rep).wait_recv()
            project_arrived(owner, j, way)
        elif j >= early:
            side = owner // (devices // 2)
            quarters = 3 if way == 1 else 2
            half_hop(owner, j, piece_of(side, quarters, True), True, way, RIGHT, across).wait_recv()
            half_hop(owner, j, piece_of(side, quarters, False), False, way, RIGHT, across).wait_recv()
        else:
            go_across(owner, j).wait_recv()

    def later_hands(k):
        if k in (0, 2):
            hand_over((0, early + k // 2))

    def follow(name, j):
        owner = chip_of(name, other_core)
        go_across(owner, j).wait_recv()
        return owner, j

    def at_corner():
        events = [[("C", j, 1)] for j in order_l]
        for jz, jy in zip(order_l, order_r):
            events.append([("E", jz, None), ("D", jz, None), ("B", jy, 0)])
        for k in range(heads):
            events.append([("G", j, None) for j in keep[k : k + 1]] + [("F", order_l[k], None)])
        events.append([("H", order_a[3], None)])
        lag = []
        for k, now in enumerate(events):
            for name, j, way in now:
                arrived(name, j, way)
                if name in "CE" or (name == "G" and j == order_a[3]):
                    send(mine(name), j, RIGHT, beside).start()
                go_across(mine(name), j).start()
            later_hands(k)
            todo = [(mine(name), j) for name, j, _ in now]
            if k < heads:
                go_across(across, k).wait_recv()
                todo.append((across, k))
            todo += [follow(name, j) for name, j in lag]
            for owner, j in todo:
                attend(owner, j)
            lag = [(name, j) for name, j, _ in now]
        for name, j in lag:
            attend(*follow(name, j))
        pltpu.make_async_copy(mixed_out, mixed_out, lend_sem.at[1]).wait()
        sent(RIGHT, kv.at[pl.ds(0, 2 * heads + 1)])
        sent(LAT_OUT, lat.at[pl.ds(0, 4)])
        sent(LEFT, kv.at[pl.ds(0, heads)])
        sent(ACROSS, kv.at[pl.ds(0, 7 * heads)])
        sent(LEND, lent)

    def at_inner():
        events = []
        for k in range(heads):
            events.append([("E", order_l[k], 1), ("A", order_a[k], 2)])
        events[heads - 1].append(("F", order_l[0], None))
        for k in range(heads):
            events.append([("B", order_a[k], None), ("G", order_a[k], None), ("D", order_r[k], 0)])
        for k in range(heads):
            events.append([("H", order_a[k], None)])
            if k > 0:
                events[-1].append(("F", order_l[k], None))
            if k == heads - 2:
                events.append([])
        lag = []
        ready = False

        for k, now in enumerate(events):
            for name, j, way in now:
                arrived(name, j, way)
                if name == "A":
                    send(mine("A"), j, MID, mine("E")).start()
                    send(mine("A"), j, RIGHT, beside).start()
                elif name == "B":
                    send(mine("B"), j, MID, mine("E")).start()
                elif name == "E":
                    send(mine("E"), j, LEFT, mine("A")).start()
                    if j == order_l[0]:
                        send(mine("E"), j, RIGHT, beside).start()
                elif name == "G" and j in keep:
                    send(mine("G"), j, LEFT, mine("A")).start()
                go_across(mine(name), j).start()
            later_hands(k)
            if k == heads - 1:
                for j in order_l[1:]:
                    send(mine("E"), j, RIGHT, beside).start()
            todo = [(mine(name), j) for name, j, _ in now]
            if k < heads:
                go_across(across, k).wait_recv()
                todo.append((across, k))
            todo += [follow(name, j) for name, j in lag]
            give = [(name, j) for name, j in lag if (name == "G" and j not in keep) or (name == "H" and j in ship)]
            if give and not ready:
                ready = True
                pltpu.make_async_copy(lent, lent, lend_sem.at[0]).wait()
            back = []
            for name, j in give:
                for i, (n, c, jj) in enumerate(lends):
                    if n == name and jj == j:
                        mixed_out[i] = attended(lent[i], chip_of(n, c), jj)
                        back.append(i)
            for i in back:
                give_back(i).start()
            for owner, j in todo:
                attend(owner, j)
            lag = [(name, j) for name, j, _ in now]
        for name, j in lag:
            attend(*follow(name, j))
        sent(RIGHT, kv.at[pl.ds(0, 2 * heads)])
        sent(LAT_OUT, lat.at[pl.ds(0, 10)])
        sent(LEFT, kv.at[pl.ds(0, heads - early + heads + len(keep))])
        sent(MID, kv.at[pl.ds(0, heads - early + 2 * heads)])
        sent(ACROSS, kv.at[pl.ds(0, 8 * heads)])
        sent(HALF_L, halves.at[pl.ds(0, 2 * early), 0])
        sent(LEND, mixed_out)

    if early:
        pl.when(corner)(at_corner)
        pl.when(inner)(at_inner)
        sent(HALF_R, halves.at[pl.ds(0, heads), 0])
        sent(HALF_X, halves.at[pl.ds(0, heads + early), 0])
    else:
        around()
        sent(LAT_OUT, lat.at[pl.ds(0, chips - 1)])
    sent(LAT_ON, lat.at[pl.ds(0, chips)])


def on_device(grid_y, cores, early, queries, latents, w_key, w_value):
    devices = lax.axis_size("ctx")
    heads, width, nope = w_key.shape
    query_rows = queries.shape[0]
    block = latents.shape[0]
    rows = block * devices
    anywhere = pl.BlockSpec(memory_space=pl.ANY)
    dma = pltpu.SemaphoreType.DMA
    return pl.pallas_call(
        functools.partial(kernel, grid_y, cores, early),
        out_shape=jax.ShapeDtypeStruct((query_rows, devices * heads * nope), jnp.bfloat16),
        in_specs=[anywhere] * 4,
        out_specs=pl.BlockSpec(memory_space=pltpu.VMEM),
        scratch_shapes=[
            pltpu.VMEM(queries.shape, jnp.bfloat16),
            pltpu.VMEM((devices, block, latents.shape[1]), jnp.bfloat16),
            pltpu.VMEM((heads, width, 2 * nope), jnp.bfloat16),
            pltpu.VMEM((2, rows, nope), jnp.bfloat16),
            pltpu.VMEM((devices * heads, 2, rows, nope), jnp.bfloat16),
            pltpu.VMEM((heads + early if early else 1, 2, width, nope), jnp.bfloat16),
            dma((3,)),
            dma((devices,)),
            dma((devices * heads,)),
            dma((heads + early if early else 1, 2)),
            dma((10,)),
            dma((3, heads)),
            pltpu.VMEM((8 if early else 1, query_rows, 2 * nope), jnp.bfloat16),
            pltpu.VMEM((8 if early else 1, query_rows, nope), jnp.bfloat16),
            dma((2,)),
        ],
        compiler_params=pltpu.CompilerParams(
            collective_id=0, has_side_effects=True, vmem_limit_bytes=50 * 1024 * 1024
        ),
    )(*(pltpu.with_memory_space_constraint(a, pltpu.HBM) for a in (queries, latents, w_key, w_value)))


def layout_of(mesh):
    group = list(mesh.devices.reshape(-1, mesh.shape["ctx"])[0])
    places = [tuple(d.coords) for d in group]
    chips = sorted(set(places))
    cores = len(group) // len(chips)
    varied = [axis for axis in range(3) if len({c[axis] for c in chips}) > 1]
    grid_y = 1
    if len(varied) == 2:
        fast = len({c[varied[0]] for c in chips})
        grid_y = 2 if fast == 2 else 1
    return grid_y, cores


def solution(mesh):
    grid_y, cores = layout_of(mesh)
    chips = mesh.shape["ctx"] // cores
    early = 2 if mesh.shape["rep"] == 2 and grid_y == 2 and chips // grid_y == 4 and cores == 2 else 0
    return jax.shard_map(
        functools.partial(on_device, grid_y, cores, early),
        mesh=mesh,
        in_specs=(
            P(("rep", "ctx"), None),
            P(("rep", "ctx"), None),
            P("ctx", None, None),
            P("ctx", None, None),
        ),
        out_specs=P(("rep", "ctx"), None),
        check_vma=False,
    )
```

```python
import functools
import math

import jax
import jax.numpy as jnp
from jax import lax
from jax.experimental import pallas as pl
from jax.experimental.pallas import tpu as pltpu
from jax.sharding import PartitionSpec as P

MESH = pl.DeviceIdType.MESH


def kernel(
    grid_y,
    cores,
    early,
    q_hbm,
    lat_hbm,
    wk_hbm,
    wv_hbm,
    o,
    q,
    lat,
    wkv,
    ropes,
    kv,
    halves,
    load_sem,
    lat_recv,
    kv_recv,
    half_recv,
    send_sem,
    part_recv,
    lent,
    mixed_out,
    lend_sem,
):
    devices = lat.shape[0]
    heads = wkv.shape[0]
    rows = kv.shape[2]
    nope = kv.shape[3]
    width = wkv.shape[1]
    rope = lat.shape[2] - width
    qk = nope + rope
    chips = devices // cores
    grid_z = chips // grid_y
    half = chips // 2
    scale = math.log2(math.e) / math.sqrt(qk)

    half_right = (heads + 1) // 2
    late = list(range(early, heads))
    order_r = late + list(range(early))
    order_l = order_r[half_right:] + order_r[:half_right]
    if early:
        order_l = [early - 1] + late[::-1] + list(range(early - 1))
        order_r = list(range(heads))
    order_a = late + list(range(early))
    keep = order_a[:1] + order_a[3:]
    ship = order_a[:3]

    me = lax.axis_index("ctx")
    core = lax.rem(me, cores)
    my_chip = me // cores
    my_y = lax.rem(my_chip, grid_y)
    my_z = my_chip // grid_y
    place = (1 - my_y) * my_z + my_y * (2 * grid_z - 1 - my_z)

    def device_at(spot, which):
        spot = lax.rem(spot + 2 * chips, chips)
        y = spot // grid_z
        z = (1 - y) * spot + y * (2 * grid_z - 1 - spot)
        return (z * grid_y + y) * cores + which

    other_core = cores - 1 - core
    across = my_chip * cores + other_core
    right = device_at(place + 1, core)
    left = device_at(place - 1, core)
    rep = lax.axis_index("rep")
    top = my_z // (grid_z // 2)
    inward = 1 - 2 * top
    z_a = top * (grid_z - 1)
    z_g = (1 - top) * (grid_z - 1)
    corner = my_z == z_a
    inner = my_z != z_a

    def chip_of(name, which):
        z = {"A": z_a, "C": z_a + inward, "E": z_g - inward, "G": z_g}
        z |= {"B": z["A"], "D": z["C"], "F": z["E"], "H": z["G"]}
        y = my_y if name in "ACEG" else 1 - my_y
        return (z[name] * grid_y + y) * cores + which

    def mine(name):
        return chip_of(name, core)

    barrier = pltpu.get_barrier_semaphore()

    plane = grid_y * cores
    beside = (my_z * grid_y + 1 - my_y) * cores + core
    steps = [(0, 1, True), (-1, 1, my_z > 0), (1, 1, my_z < grid_z - 1)]
    steps += [(-1, 0, my_z > 0), (1, 0, my_z < grid_z - 1), (-2, 0, my_z > 1), (2, 0, my_z < grid_z - 2)]

    def greet(sem):
        for dz, dy, there in steps:
            to = (beside if dy else me) + dz * plane

            def tell():
                pl.semaphore_signal(sem, inc=1, device_id={"ctx": to}, device_id_type=MESH)

            if there is True:
                tell()
            else:
                pl.when(there)(tell)

    greeted = 1
    for _, _, there in steps[1:]:
        greeted = greeted + lax.convert_element_type(there, jnp.int32)
    if early:
        greet(barrier)
        pl.semaphore_signal(barrier, inc=1, device_id={"rep": 1 - rep}, device_id_type=MESH)
    else:

        @pl.loop(1, chips)
        def _(d):
            pl.semaphore_signal(
                barrier, inc=1, device_id={"ctx": device_at(place + d, core)}, device_id_type=MESH
            )

    pl.semaphore_signal(barrier, inc=1, device_id={"ctx": across}, device_id_type=MESH)

    q_copy = pltpu.make_async_copy(q_hbm, q, load_sem.at[0])
    lat_copy = pltpu.make_async_copy(lat_hbm, lat.at[me], load_sem.at[1])
    lat_copy.start()
    for j in range(heads):
        pltpu.make_async_copy(wk_hbm.at[j], wkv.at[j, :, pl.ds(0, nope)], load_sem.at[2]).start()
        pltpu.make_async_copy(wv_hbm.at[j], wkv.at[j, :, pl.ds(nope, nope)], load_sem.at[2]).start()
    q_copy.start()

    pl.semaphore_wait(barrier, greeted + 2 if early else chips)

    LAT_OUT, LAT_ON, RIGHT, LEFT, MID, ACROSS, HALF_R, HALF_L, HALF_X, LEND = range(10)

    near = me // (devices // 2)
    chips_half = chips // 2

    def near_chip(i):
        return near * chips_half + lax.rem(my_chip - near * chips_half + i, chips_half)

    def far_chip(i):
        return (1 - near) * chips_half + lax.rem(my_chip - near * chips_half + i, chips_half)

    def lat_out(owner, chip):
        return pltpu.make_async_remote_copy(
            src_ref=lat.at[owner],
            dst_ref=lat.at[owner],
            send_sem=send_sem.at[LAT_OUT],
            recv_sem=lat_recv.at[owner],
            device_id={"ctx": chip * cores + core},
            device_id_type=MESH,
        )

    def lat_on(owner):
        return pltpu.make_async_remote_copy(
            src_ref=lat.at[owner],
            dst_ref=lat.at[owner],
            send_sem=send_sem.at[LAT_ON],
            recv_sem=lat_recv.at[owner],
            device_id={"ctx": across},
            device_id_type=MESH,
        )

    lat_copy.wait()

    def lat_near(owner):
        @pl.loop(1, chips_half)
        def _(i):
            lat_out(owner, near_chip(i)).start()

    pieces = 4
    deep = width // pieces

    def half_out(src, j, way, target, piece):
        return pltpu.make_async_remote_copy(
            src_ref=src.at[j, pl.ds(piece * deep, deep)],
            dst_ref=halves.at[way * heads + j, rep, pl.ds(piece * deep, deep)],
            send_sem=send_sem.at[HALF_R + way],
            recv_sem=half_recv.at[way * heads + j, rep],
            device_id={"ctx": target},
            device_id_type=MESH,
        )

    def half_over(j, way, which):
        return pltpu.make_async_remote_copy(
            src_ref=halves.at[way * heads + j, which],
            dst_ref=halves.at[way * heads + j, which],
            send_sem=send_sem.at[HALF_X],
            recv_sem=half_recv.at[way * heads + j, which],
            device_id={"rep": 1 - rep},
            device_id_type=MESH,
        )

    early_r = order_r
    early_l = [j for j in order_l if j < early]

    def relay(chip):
        owner = chip * cores + core
        lat_on(owner).wait_recv()
        lat_on(owner).start()

    def parity(owner, j):
        if heads % 2 == 0:
            return j % 2
        return lax.rem(owner * heads + j, 2)

    def weights_out(first, last):
        for which, src in ((0, wk_hbm), (1, wv_hbm)):

            @pl.when(rep == which)
            def _():
                for i in range(first, last):
                    half_out(src, early_r[i // pieces], 0, beside, i % pieces).start()

            @pl.when(jnp.logical_and(rep == which, inner))
            def _():
                for i in range(first, min(last, early * pieces)):
                    for target in (mine("A"), mine("E")):
                        half_out(src, early_l[i // pieces], 1, target, i % pieces).start()

    lends = [("G", c, j) for j in order_a[1:3] for c in range(cores)]
    lends += [("H", c, j) for j in ship for c in range(cores)]

    def query_start(owner, j):
        odd = parity(owner, j)
        pair = owner * (heads // 2) + j // 2 if heads % 2 == 0 else (owner * heads + j) // 2
        return pl.multiple_of(pair * (2 * qk) + odd * nope, nope)

    def lend(i):
        name, which, j = lends[i]
        return pltpu.make_async_remote_copy(
            src_ref=q.at[:, pl.ds(query_start(chip_of(name, which), j), 2 * nope)],
            dst_ref=lent.at[i],
            send_sem=send_sem.at[LEND],
            recv_sem=lend_sem.at[0],
            device_id={"ctx": mine("C")},
            device_id_type=MESH,
        )

    def give_back(name, j, which):
        item = chip_of(name, which) * heads + j
        slot = lends.index((name, 0, j)) + which
        mixed_out[slot] = attended(lent[slot], chip_of(name, which), j)
        return pltpu.make_async_remote_copy(
            src_ref=mixed_out.at[slot],
            dst_ref=o.at[:, pl.ds(pl.multiple_of(item * nope, nope), nope)],
            send_sem=send_sem.at[LEND],
            recv_sem=lend_sem.at[1],
            device_id={"ctx": mine("A")},
            device_id_type=MESH,
        )

    def lend_out(first, last):
        @pl.when(corner)
        def _():
            for i in range(first, last):
                lend(i).start()

    if early:

        def lat_to(owner, names):
            for name in names:
                lat_out(owner, mine(name) // cores).start()

        def lat_take(names):
            for name in names:
                lat_on(mine(name)).wait_recv()
                lat_on(mine(name)).start()

        def lat_meet(names):
            for name in names:
                lat_on(chip_of(name, other_core)).wait_recv()

        pl.when(corner)(lambda: lat_to(me, "EDCB"))
        pl.when(inner)(lambda: lat_to(me, "GFBEAD"))
        lat_on(me).start()
        weights_out(0, pieces)
        q_copy.wait()
        lend_out(0, 4)

        @pl.when(inner)
        def _():
            lat_take("G")
            lat_to(mine("G"), "BAD")
            lat_take("F")
            lat_to(mine("F"), "A")

        weights_out(pieces, heads * pieces)

        @pl.when(corner)
        def _():
            lat_take("BCD")
            lat_meet("ABCD")

        @pl.when(inner)
        def _():
            lat_take("ABDE")
            lat_meet("ABCDEF")

    else:
        lat_near(me)

        @pl.loop(0, chips_half)
        def _(i):
            lat_out(me, far_chip(i)).start()

        lat_on(me).start()

        @pl.loop(1, chips_half)
        def _(i):
            relay(near_chip(i))

        @pl.loop(0, chips_half)
        def _(i):
            lat_on(near_chip(i) * cores + other_core).wait_recv()

    pltpu.make_async_copy(wkv, wkv, load_sem.at[2]).wait()

    def send(owner, j, stream, target):
        return pltpu.make_async_remote_copy(
            src_ref=kv.at[owner * heads + j],
            dst_ref=kv.at[owner * heads + j],
            send_sem=send_sem.at[stream],
            recv_sem=kv_recv.at[owner * heads + j],
            device_id={"ctx": target},
            device_id_type=MESH,
        )

    def go_right(owner, j):
        return send(owner, j, RIGHT, right)

    def go_left(owner, j):
        return send(owner, j, LEFT, left)

    def go_across(owner, j):
        return send(owner, j, ACROSS, across)

    def piece_of(side, quarters, is_first):
        size = quarters if is_first else 4 - quarters
        return (side if is_first else 1 - side) * (4 - size), size

    def half_hop(owner, j, piece, is_first, way, stream, target):
        begin, size = piece
        quarter = rows // 4
        ref = kv.at[owner * heads + j, :, pl.ds(pl.multiple_of(begin * quarter, quarter), size * quarter)]
        sem = part_recv.at[way, j] if is_first else kv_recv.at[owner * heads + j]
        return pltpu.make_async_remote_copy(
            src_ref=ref,
            dst_ref=ref,
            send_sem=send_sem.at[stream],
            recv_sem=sem,
            device_id={"ctx": target},
            device_id_type=MESH,
        )

    def project_part(j, piece):
        begin, size = piece
        some = lat[pl.ds(begin * (devices // 4), size * (devices // 4))]
        some = some.reshape(size * rows // 4, lat.shape[2])[:, :width]
        both = jnp.dot(some, wkv[j], preferred_element_type=jnp.float32)
        keys = both[:, :nope]
        if parity(me, j) == 1:
            keys = jnp.concatenate([keys[:, rope:], keys[:, :rope]], axis=1)
        at = pl.ds(pl.multiple_of(begin * (rows // 4), rows // 4), size * (rows // 4))
        kv[me * heads + j, 0, at] = keys.astype(jnp.bfloat16)
        kv[me * heads + j, 1, at] = both[:, nope:].astype(jnp.bfloat16)

    late_l = [j for j in order_l if j >= early]

    def late_out(is_first):
        @pl.when(corner)
        def _():
            piece = piece_of(top, 2, is_first)
            for j in late:
                project_part(j, piece)
            for j in late:
                half_hop(me, j, piece, is_first, 2, LEFT, mine("C")).start()

        @pl.when(inner)
        def _():
            piece = piece_of(top, 3, is_first)
            for j in late:
                project_part(j, piece)
            for j in late_l:
                half_hop(me, j, piece, is_first, 1, LEFT, mine("A")).start()
                half_hop(me, j, piece, is_first, 1, MID, mine("E")).start()

    def store(owner, j, keys, values):
        odd = parity(owner, j)
        turned = jnp.concatenate([keys[:, rope:], keys[:, :rope]], axis=1)
        if isinstance(odd, int):
            keys = turned if odd else keys
        else:
            keys = jnp.where(odd == 1, turned, keys)
        kv[owner * heads + j, 0] = keys.astype(jnp.bfloat16)
        kv[owner * heads + j, 1] = values.astype(jnp.bfloat16)

    def project(j):
        both = jnp.dot(
            lat[...].reshape(rows, lat.shape[2])[:, :width], wkv[j], preferred_element_type=jnp.float32
        )
        store(me, j, both[:, :nope], both[:, nope:])

    def project_arrived(owner, j, way):
        some = lat[...].reshape(rows, lat.shape[2])[:, :width]
        slot = way * heads + j
        keys = jnp.dot(some, halves[slot, 0], preferred_element_type=jnp.float32)
        values = jnp.dot(some, halves[slot, 1], preferred_element_type=jnp.float32)
        store(owner, j, keys, values)

    def hand_over(*slots):
        for way, place_in in slots:
            j = (early_r, early_l)[way][place_in]
            half_over(j, way, rep).wait_recv()
            half_over(j, way, rep).start()

    if early:
        late_out(True)
        hand_over((1, 0))

        @pl.when(corner)
        def _():
            lat_take("EGFH")
            lat_meet("EGFH")

        @pl.when(inner)
        def _():
            lat_take("H")
            lat_meet("GH")

        late_out(False)
    else:
        @pl.loop(0, chips_half)
        def _(i):
            relay(far_chip(i))

        @pl.loop(0, chips_half)
        def _(i):
            lat_on(far_chip(i) * cores + other_core).wait_recv()
        for j in late:
            project(j)
            go_right(me, j).start()
            go_left(me, j).start()

    for j in range(early):
        project(j)
    if early:

        @pl.when(corner)
        def _():
            for j in range(early):
                send(me, j, LEFT, mine("C")).start()

        lend_out(4, len(lends))
    for j in range(heads):
        go_across(me, j).start()

    rope_part = lat[...].reshape(rows, lat.shape[2])[:, width:]
    blank = jnp.zeros_like(rope_part)
    ropes[0] = jnp.concatenate([rope_part, blank], axis=1)
    ropes[1] = jnp.concatenate([blank, rope_part], axis=1)

    if not early:
        q_copy.wait()

    lane = lax.broadcasted_iota(jnp.int32, (rows, nope), 1)
    upper = lane >= rope

    def attended(queries, owner, j):
        odd = parity(owner, j)
        head = owner * heads + j
        keys = kv[head, 0]
        values = kv[head, 1]

        def even_keys():
            return jnp.concatenate([keys, ropes[0]], axis=1)

        def odd_keys():
            return jnp.concatenate(
                [jnp.where(upper, keys, jnp.zeros_like(keys)), jnp.where(upper, ropes[1], keys)], axis=1
            )

        if isinstance(odd, int):
            keys_full = odd_keys() if odd else even_keys()
        else:
            keys_full = jnp.where(odd == 1, odd_keys(), even_keys())
        scores = lax.dot_general(
            queries, keys_full, (((1,), (1,)), ((), ())), preferred_element_type=jnp.float32
        )
        row_max = jnp.max(scores, axis=1, keepdims=True)
        weights = jnp.exp2((scores - row_max) * scale)
        total = jnp.sum(weights, axis=1, keepdims=True)
        mixed = jnp.dot(weights.astype(jnp.bfloat16), values, preferred_element_type=jnp.float32)
        return (mixed * (1.0 / total)).astype(jnp.bfloat16)

    def attend(owner, j):
        at = pl.multiple_of((owner * heads + j) * nope, nope)
        o[:, pl.ds(at, nope)] = attended(q[:, pl.ds(query_start(owner, j), 2 * nope)], owner, j)

    attend(me, 0)
    if early:
        hand_over(*[(1, i) for i in range(1, early)], *[(0, i) for i in range(early)])
    for i in range(1, early):
        attend(me, i)
    for j in range(max(early, 1), heads):
        attend(me, j)

    def sent(stream, ref):
        pltpu.make_async_remote_copy(
            src_ref=ref,
            dst_ref=ref,
            send_sem=send_sem.at[stream],
            recv_sem=send_sem.at[stream],
            device_id={"ctx": across},
            device_id_type=MESH,
        ).wait_send()

    def around():
        def others(s):
            return (device_at(place - s, other_core), device_at(place + s, other_core))

        def attend_others(s, pos):
            pair = list(zip(others(s), (order_r, order_l)))
            for owner, js in pair:
                go_across(owner, js[pos]).wait_recv()
            return [(owner, js[pos]) for owner, js in pair]

        def ring_step(s, first, last):
            from_left = device_at(place - s, core)
            from_right = device_at(place + s, core)
            for pos in range(heads):
                jr, jl = order_r[pos], order_l[pos]
                for j, way, owner, go in ((jr, 0, from_left, go_right), (jl, 1, from_right, go_left)):
                    go(owner, j).wait_recv()
                    if not last or pos < (half_right if way == 0 else heads - half_right):
                        go(owner, j).start()
                    go_across(owner, j).start()
                todo = [(from_left, jr), (from_right, jl)]
                if first:
                    go_across(across, pos).wait_recv()
                    todo.append((across, pos))
                if pos > 0:
                    todo += attend_others(s, pos - 1)
                elif not first:
                    todo += attend_others(s - 1, heads - 1)
                for owner, j in todo:
                    attend(owner, j)

        ring_step(1, True, half == 2)
        if half > 3:

            @pl.loop(2, half - 1)
            def _(s):
                ring_step(s, False, False)

        if half > 2:
            ring_step(half - 1, False, True)

        far = device_at(place + half, core)
        far_other = device_at(place + half, other_core)
        todo = attend_others(half - 1, heads - 1)
        for pos in range(half_right):
            arrivals = [(order_r[pos], go_right)]
            if pos < heads - half_right:
                arrivals.append((order_l[pos], go_left))
            for j, go in arrivals:
                go(far, j).wait_recv()
                go_across(far, j).start()
                todo.append((far, j))
            for owner, j in todo:
                attend(owner, j)
            for j, _ in arrivals:
                go_across(far_other, j).wait_recv()
            for j, _ in arrivals:
                attend(far_other, j)
            todo = []

        sent(RIGHT, kv.at[pl.ds(0, (half - 1) * heads + half_right)])
        sent(LEFT, kv.at[pl.ds(0, half * heads - half_right)])
        sent(ACROSS, kv.at[pl.ds(0, chips * heads)])

    def arrived(name, j, way):
        owner = mine(name)
        direct = {0: "B" if name == "B" else "D", 1: "C" if name == "C" else "E", 2: "A"}
        if way is None or name != direct[way]:
            go_across(owner, j).wait_recv()
        elif way == 0 or (way == 1 and j < early):
            half_over(j, way, 1 - rep).wait_recv()
            project_arrived(owner, j, way)
        elif j >= early:
            side = owner // (devices // 2)
            quarters = 3 if way == 1 else 2
            half_hop(owner, j, piece_of(side, quarters, True), True, way, RIGHT, across).wait_recv()
            half_hop(owner, j, piece_of(side, quarters, False), False, way, RIGHT, across).wait_recv()
        else:
            go_across(owner, j).wait_recv()

    def later_hands(k):
        if k in (0, 2):
            hand_over((0, early + k // 2))

    def follow(name, j):
        owner = chip_of(name, other_core)
        go_across(owner, j).wait_recv()
        return owner, j

    def at_corner():
        events = [[("C", j, 1)] for j in order_l]
        for jz, jy in zip(order_l, order_r):
            events.append([("E", jz, None), ("D", jz, None), ("B", jy, 0)])
        for k in range(heads):
            events.append([("G", j, None) for j in keep[k : k + 1]] + [("F", order_l[k], None)])
        events.append([("H", order_a[3], None)])
        lag = []
        for k, now in enumerate(events):
            for name, j, way in now:
                arrived(name, j, way)
                if name in "CE" or (name == "G" and j == order_a[3]):
                    send(mine(name), j, RIGHT, beside).start()
                go_across(mine(name), j).start()
            later_hands(k)
            todo = [(mine(name), j) for name, j, _ in now]
            if k < heads:
                go_across(across, k).wait_recv()
                todo.append((across, k))
            todo += [follow(name, j) for name, j in lag]
            for owner, j in todo:
                attend(owner, j)
            lag = [(name, j) for name, j, _ in now]
        for name, j in lag:
            attend(*follow(name, j))
        pltpu.make_async_copy(mixed_out, mixed_out, lend_sem.at[1]).wait()
        sent(RIGHT, kv.at[pl.ds(0, 2 * heads + 1)])
        sent(LAT_OUT, lat.at[pl.ds(0, 4)])
        sent(LEFT, kv.at[pl.ds(0, heads)])
        sent(ACROSS, kv.at[pl.ds(0, 6 * heads + len(keep) + 1)])
        sent(LEND, lent)

    def at_inner():
        events = []
        for k in range(heads):
            events.append([("E", order_l[k], 1), ("A", order_a[k], 2)])
        events[heads - 1].append(("F", order_l[0], None))
        for k in range(heads):
            events.append([("B", order_a[k], None), ("G", order_a[k], None), ("D", order_r[k], 0)])
        for k in range(heads):
            events.append([("H", order_a[k], None)])
            if k > 0:
                events[-1].append(("F", order_l[k], None))
            if k == heads - 2:
                events.append([])
        lag = []

        for k, now in enumerate(events):
            for name, j, way in now:
                arrived(name, j, way)
                if name == "A":
                    send(mine("A"), j, MID, mine("E")).start()
                    send(mine("A"), j, RIGHT, beside).start()
                elif name == "B":
                    send(mine("B"), j, MID, mine("E")).start()
                elif name == "E":
                    send(mine("E"), j, LEFT, mine("A")).start()
                    if j == order_l[0]:
                        send(mine("E"), j, RIGHT, beside).start()
                elif name == "G" and j in keep:
                    send(mine("G"), j, LEFT, mine("A")).start()
                go_across(mine(name), j).start()
            for name, j, _ in now:
                if name == "H" and j in ship:
                    give_back(name, j, core).start()
            later_hands(k)
            if k == heads - 1:
                for j in order_l[1:]:
                    send(mine("E"), j, RIGHT, beside).start()
            todo = [(mine(name), j) for name, j, _ in now]
            if k < heads:
                go_across(across, k).wait_recv()
                todo.append((across, k))
            todo += [follow(name, j) for name, j in lag]
            back = []
            if ("G", order_a[1]) in lag:
                pltpu.make_async_copy(lent, lent, lend_sem.at[0]).wait()
            for name, j in lag:
                if (name, 0, j) in lends:
                    back += [give_back(name, j, which) for which in ((core, other_core) if name == "G" else (other_core,))]
            for copy in back:
                copy.start()
            for owner, j in todo:
                attend(owner, j)
            lag = [(name, j) for name, j, _ in now]
        for name, j in lag:
            attend(*follow(name, j))
        sent(RIGHT, kv.at[pl.ds(0, 2 * heads)])
        sent(LAT_OUT, lat.at[pl.ds(0, 10)])
        sent(LEFT, kv.at[pl.ds(0, heads - early + heads + len(keep))])
        sent(MID, kv.at[pl.ds(0, heads - early + 2 * heads)])
        sent(ACROSS, kv.at[pl.ds(0, 8 * heads)])
        sent(HALF_L, halves.at[pl.ds(0, 2 * early), 0])
        sent(LEND, mixed_out)

    if early:
        pl.when(corner)(at_corner)
        pl.when(inner)(at_inner)
        sent(HALF_R, halves.at[pl.ds(0, heads), 0])
        sent(HALF_X, halves.at[pl.ds(0, heads + early), 0])
    else:
        around()
        sent(LAT_OUT, lat.at[pl.ds(0, chips - 1)])
    sent(LAT_ON, lat.at[pl.ds(0, chips)])


def on_device(grid_y, cores, early, queries, latents, w_key, w_value):
    devices = lax.axis_size("ctx")
    heads, width, nope = w_key.shape
    query_rows = queries.shape[0]
    block = latents.shape[0]
    rows = block * devices
    anywhere = pl.BlockSpec(memory_space=pl.ANY)
    dma = pltpu.SemaphoreType.DMA
    return pl.pallas_call(
        functools.partial(kernel, grid_y, cores, early),
        out_shape=jax.ShapeDtypeStruct((query_rows, devices * heads * nope), jnp.bfloat16),
        in_specs=[anywhere] * 4,
        out_specs=pl.BlockSpec(memory_space=pltpu.VMEM),
        scratch_shapes=[
            pltpu.VMEM(queries.shape, jnp.bfloat16),
            pltpu.VMEM((devices, block, latents.shape[1]), jnp.bfloat16),
            pltpu.VMEM((heads, width, 2 * nope), jnp.bfloat16),
            pltpu.VMEM((2, rows, nope), jnp.bfloat16),
            pltpu.VMEM((devices * heads, 2, rows, nope), jnp.bfloat16),
            pltpu.VMEM((heads + early if early else 1, 2, width, nope), jnp.bfloat16),
            dma((3,)),
            dma((devices,)),
            dma((devices * heads,)),
            dma((heads + early if early else 1, 2)),
            dma((10,)),
            dma((3, heads)),
            pltpu.VMEM((10 if early else 1, query_rows, 2 * nope), jnp.bfloat16),
            pltpu.VMEM((10 if early else 1, query_rows, nope), jnp.bfloat16),
            dma((2,)),
        ],
        compiler_params=pltpu.CompilerParams(
            collective_id=0, has_side_effects=True, vmem_limit_bytes=50 * 1024 * 1024
        ),
    )(*(pltpu.with_memory_space_constraint(a, pltpu.HBM) for a in (queries, latents, w_key, w_value)))


def layout_of(mesh):
    group = list(mesh.devices.reshape(-1, mesh.shape["ctx"])[0])
    places = [tuple(d.coords) for d in group]
    chips = sorted(set(places))
    cores = len(group) // len(chips)
    varied = [axis for axis in range(3) if len({c[axis] for c in chips}) > 1]
    grid_y = 1
    if len(varied) == 2:
        fast = len({c[varied[0]] for c in chips})
        grid_y = 2 if fast == 2 else 1
    return grid_y, cores


def solution(mesh):
    grid_y, cores = layout_of(mesh)
    chips = mesh.shape["ctx"] // cores
    early = 2 if mesh.shape["rep"] == 2 and grid_y == 2 and chips // grid_y == 4 and cores == 2 else 0
    return jax.shard_map(
        functools.partial(on_device, grid_y, cores, early),
        mesh=mesh,
        in_specs=(
            P(("rep", "ctx"), None),
            P(("rep", "ctx"), None),
            P("ctx", None, None),
            P("ctx", None, None),
        ),
        out_specs=P(("rep", "ctx"), None),
        check_vma=False,
    )
```

```python
import functools
import math

import jax
import jax.numpy as jnp
from jax import lax
from jax.experimental import pallas as pl
from jax.experimental.pallas import tpu as pltpu
from jax.sharding import PartitionSpec as P

MESH = pl.DeviceIdType.MESH


def kernel(
    grid_y,
    cores,
    early,
    q_hbm,
    lat_hbm,
    wk_hbm,
    wv_hbm,
    o,
    q,
    lat,
    wkv,
    ropes,
    kv,
    halves,
    load_sem,
    lat_recv,
    kv_recv,
    half_recv,
    send_sem,
    part_recv,
    lent,
    mixed_out,
    lend_sem,
):
    devices = lat.shape[0]
    heads = wkv.shape[0]
    rows = kv.shape[2]
    nope = kv.shape[3]
    width = wkv.shape[1]
    rope = lat.shape[2] - width
    qk = nope + rope
    chips = devices // cores
    grid_z = chips // grid_y
    half = chips // 2
    scale = math.log2(math.e) / math.sqrt(qk)

    half_right = (heads + 1) // 2
    late = list(range(early, heads))
    order_r = late + list(range(early))
    order_l = order_r[half_right:] + order_r[:half_right]
    if early:
        order_l = [early - 1] + late[::-1] + list(range(early - 1))
        order_r = list(range(heads))
    order_a = late + list(range(early))
    keep = order_a[:1] + order_a[3:]
    ship = order_a[:3]

    me = lax.axis_index("ctx")
    core = lax.rem(me, cores)
    my_chip = me // cores
    my_y = lax.rem(my_chip, grid_y)
    my_z = my_chip // grid_y
    place = (1 - my_y) * my_z + my_y * (2 * grid_z - 1 - my_z)

    def device_at(spot, which):
        spot = lax.rem(spot + 2 * chips, chips)
        y = spot // grid_z
        z = (1 - y) * spot + y * (2 * grid_z - 1 - spot)
        return (z * grid_y + y) * cores + which

    other_core = cores - 1 - core
    across = my_chip * cores + other_core
    right = device_at(place + 1, core)
    left = device_at(place - 1, core)
    rep = lax.axis_index("rep")
    top = my_z // (grid_z // 2)
    inward = 1 - 2 * top
    z_a = top * (grid_z - 1)
    z_g = (1 - top) * (grid_z - 1)
    corner = my_z == z_a
    inner = my_z != z_a

    def chip_of(name, which):
        z = {"A": z_a, "C": z_a + inward, "E": z_g - inward, "G": z_g}
        z |= {"B": z["A"], "D": z["C"], "F": z["E"], "H": z["G"]}
        y = my_y if name in "ACEG" else 1 - my_y
        return (z[name] * grid_y + y) * cores + which

    def mine(name):
        return chip_of(name, core)

    barrier = pltpu.get_barrier_semaphore()

    plane = grid_y * cores
    beside = (my_z * grid_y + 1 - my_y) * cores + core
    steps = [(0, 1, True), (-1, 1, my_z > 0), (1, 1, my_z < grid_z - 1)]
    steps += [(-1, 0, my_z > 0), (1, 0, my_z < grid_z - 1), (-2, 0, my_z > 1), (2, 0, my_z < grid_z - 2)]

    def greet(sem):
        for dz, dy, there in steps:
            to = (beside if dy else me) + dz * plane

            def tell():
                pl.semaphore_signal(sem, inc=1, device_id={"ctx": to}, device_id_type=MESH)

            if there is True:
                tell()
            else:
                pl.when(there)(tell)

    greeted = 1
    for _, _, there in steps[1:]:
        greeted = greeted + lax.convert_element_type(there, jnp.int32)
    if early:
        greet(barrier)
        pl.semaphore_signal(barrier, inc=1, device_id={"rep": 1 - rep}, device_id_type=MESH)
    else:

        @pl.loop(1, chips)
        def _(d):
            pl.semaphore_signal(
                barrier, inc=1, device_id={"ctx": device_at(place + d, core)}, device_id_type=MESH
            )

    pl.semaphore_signal(barrier, inc=1, device_id={"ctx": across}, device_id_type=MESH)

    q_copy = pltpu.make_async_copy(q_hbm, q, load_sem.at[0])
    lat_copy = pltpu.make_async_copy(lat_hbm, lat.at[me], load_sem.at[1])
    lat_copy.start()
    for j in range(heads):
        pltpu.make_async_copy(wk_hbm.at[j], wkv.at[j, :, pl.ds(0, nope)], load_sem.at[2]).start()
        pltpu.make_async_copy(wv_hbm.at[j], wkv.at[j, :, pl.ds(nope, nope)], load_sem.at[2]).start()
    q_copy.start()

    pl.semaphore_wait(barrier, greeted + 2 if early else chips)

    LAT_OUT, LAT_ON, RIGHT, LEFT, MID, ACROSS, HALF_R, HALF_L, HALF_X, LEND = range(10)

    near = me // (devices // 2)
    chips_half = chips // 2

    def near_chip(i):
        return near * chips_half + lax.rem(my_chip - near * chips_half + i, chips_half)

    def far_chip(i):
        return (1 - near) * chips_half + lax.rem(my_chip - near * chips_half + i, chips_half)

    def lat_out(owner, chip):
        return pltpu.make_async_remote_copy(
            src_ref=lat.at[owner],
            dst_ref=lat.at[owner],
            send_sem=send_sem.at[LAT_OUT],
            recv_sem=lat_recv.at[owner],
            device_id={"ctx": chip * cores + core},
            device_id_type=MESH,
        )

    def lat_on(owner):
        return pltpu.make_async_remote_copy(
            src_ref=lat.at[owner],
            dst_ref=lat.at[owner],
            send_sem=send_sem.at[LAT_ON],
            recv_sem=lat_recv.at[owner],
            device_id={"ctx": across},
            device_id_type=MESH,
        )

    lat_copy.wait()

    def lat_near(owner):
        @pl.loop(1, chips_half)
        def _(i):
            lat_out(owner, near_chip(i)).start()

    pieces = 4
    deep = width // pieces

    def half_out(src, j, way, target, piece):
        return pltpu.make_async_remote_copy(
            src_ref=src.at[j, pl.ds(piece * deep, deep)],
            dst_ref=halves.at[way * heads + j, rep, pl.ds(piece * deep, deep)],
            send_sem=send_sem.at[HALF_R + way],
            recv_sem=half_recv.at[way * heads + j, rep],
            device_id={"ctx": target},
            device_id_type=MESH,
        )

    def half_over(j, way, which):
        return pltpu.make_async_remote_copy(
            src_ref=halves.at[way * heads + j, which],
            dst_ref=halves.at[way * heads + j, which],
            send_sem=send_sem.at[HALF_X],
            recv_sem=half_recv.at[way * heads + j, which],
            device_id={"rep": 1 - rep},
            device_id_type=MESH,
        )

    early_r = order_r
    early_l = [j for j in order_l if j < early]

    def relay(chip):
        owner = chip * cores + core
        lat_on(owner).wait_recv()
        lat_on(owner).start()

    def parity(owner, j):
        if heads % 2 == 0:
            return j % 2
        return lax.rem(owner * heads + j, 2)

    def weights_out(first, last):
        for which, src in ((0, wk_hbm), (1, wv_hbm)):

            @pl.when(rep == which)
            def _():
                for i in range(first, last):
                    half_out(src, early_r[i // pieces], 0, beside, i % pieces).start()

            @pl.when(jnp.logical_and(rep == which, inner))
            def _():
                for i in range(first, min(last, early * pieces)):
                    for target in (mine("A"), mine("E")):
                        half_out(src, early_l[i // pieces], 1, target, i % pieces).start()

    lends = [("G", c, j) for j in order_a[1:3] for c in range(cores)]
    lends += [("H", c, j) for j in ship for c in range(cores)]

    def query_start(owner, j):
        odd = parity(owner, j)
        pair = owner * (heads // 2) + j // 2 if heads % 2 == 0 else (owner * heads + j) // 2
        return pl.multiple_of(pair * (2 * qk) + odd * nope, nope)

    def lend(i):
        name, which, j = lends[i]
        return pltpu.make_async_remote_copy(
            src_ref=q.at[:, pl.ds(query_start(chip_of(name, which), j), 2 * nope)],
            dst_ref=lent.at[i],
            send_sem=send_sem.at[LEND],
            recv_sem=lend_sem.at[0],
            device_id={"ctx": mine("C")},
            device_id_type=MESH,
        )

    def give_back(name, j, which):
        item = chip_of(name, which) * heads + j
        slot = lends.index((name, 0, j)) + which
        mixed_out[slot] = attended(lent[slot], chip_of(name, which), j)
        return pltpu.make_async_remote_copy(
            src_ref=mixed_out.at[slot],
            dst_ref=o.at[:, pl.ds(pl.multiple_of(item * nope, nope), nope)],
            send_sem=send_sem.at[LEND],
            recv_sem=lend_sem.at[1],
            device_id={"ctx": mine("A")},
            device_id_type=MESH,
        )

    def lend_out(first, last):
        @pl.when(corner)
        def _():
            for i in range(first, last):
                lend(i).start()

    if early:

        def lat_to(owner, names):
            for name in names:
                lat_out(owner, mine(name) // cores).start()

        def lat_take(names):
            for name in names:
                lat_on(mine(name)).wait_recv()
                lat_on(mine(name)).start()

        def lat_meet(names):
            for name in names:
                lat_on(chip_of(name, other_core)).wait_recv()

        pl.when(corner)(lambda: lat_to(me, "EDCB"))
        pl.when(inner)(lambda: lat_to(me, "GFBEAD"))
        lat_on(me).start()
        weights_out(0, pieces)
        q_copy.wait()
        lend_out(0, 4)

        @pl.when(inner)
        def _():
            lat_take("G")
            lat_to(mine("G"), "BAD")
            lat_take("F")
            lat_to(mine("F"), "A")

        weights_out(pieces, heads * pieces)

        @pl.when(corner)
        def _():
            lat_take("BCD")
            lat_meet("ABCD")

        @pl.when(inner)
        def _():
            lat_take("ABDE")
            lat_meet("ABCDEF")

    else:
        lat_near(me)

        @pl.loop(0, chips_half)
        def _(i):
            lat_out(me, far_chip(i)).start()

        lat_on(me).start()

        @pl.loop(1, chips_half)
        def _(i):
            relay(near_chip(i))

        @pl.loop(0, chips_half)
        def _(i):
            lat_on(near_chip(i) * cores + other_core).wait_recv()

    pltpu.make_async_copy(wkv, wkv, load_sem.at[2]).wait()

    def send(owner, j, stream, target):
        return pltpu.make_async_remote_copy(
            src_ref=kv.at[owner * heads + j],
            dst_ref=kv.at[owner * heads + j],
            send_sem=send_sem.at[stream],
            recv_sem=kv_recv.at[owner * heads + j],
            device_id={"ctx": target},
            device_id_type=MESH,
        )

    def go_right(owner, j):
        return send(owner, j, RIGHT, right)

    def go_left(owner, j):
        return send(owner, j, LEFT, left)

    def go_across(owner, j):
        return send(owner, j, ACROSS, across)

    def piece_of(side, quarters, is_first):
        size = quarters if is_first else 4 - quarters
        return (side if is_first else 1 - side) * (4 - size), size

    def half_hop(owner, j, piece, is_first, way, stream, target):
        begin, size = piece
        quarter = rows // 4
        ref = kv.at[owner * heads + j, :, pl.ds(pl.multiple_of(begin * quarter, quarter), size * quarter)]
        sem = part_recv.at[way - 1, j - early] if is_first else kv_recv.at[owner * heads + j]
        return pltpu.make_async_remote_copy(
            src_ref=ref,
            dst_ref=ref,
            send_sem=send_sem.at[stream],
            recv_sem=sem,
            device_id={"ctx": target},
            device_id_type=MESH,
        )

    def project_part(j, piece):
        begin, size = piece
        some = lat[pl.ds(begin * (devices // 4), size * (devices // 4))]
        some = some.reshape(size * rows // 4, lat.shape[2])[:, :width]
        both = jnp.dot(some, wkv[j], preferred_element_type=jnp.float32)
        keys = both[:, :nope]
        if parity(me, j) == 1:
            keys = jnp.concatenate([keys[:, rope:], keys[:, :rope]], axis=1)
        at = pl.ds(pl.multiple_of(begin * (rows // 4), rows // 4), size * (rows // 4))
        kv[me * heads + j, 0, at] = keys.astype(jnp.bfloat16)
        kv[me * heads + j, 1, at] = both[:, nope:].astype(jnp.bfloat16)

    late_l = [j for j in order_l if j >= early]

    def late_out(is_first):
        @pl.when(corner)
        def _():
            piece = piece_of(top, 2, is_first)
            for j in late:
                project_part(j, piece)
            for j in late:
                half_hop(me, j, piece, is_first, 2, LEFT, mine("C")).start()

        @pl.when(inner)
        def _():
            piece = piece_of(top, 3, is_first)
            for j in late:
                project_part(j, piece)
            for j in late_l:
                half_hop(me, j, piece, is_first, 1, LEFT, mine("A")).start()
                half_hop(me, j, piece, is_first, 1, MID, mine("E")).start()

    def store(owner, j, keys, values):
        odd = parity(owner, j)
        turned = jnp.concatenate([keys[:, rope:], keys[:, :rope]], axis=1)
        if isinstance(odd, int):
            keys = turned if odd else keys
        else:
            keys = jnp.where(odd == 1, turned, keys)
        kv[owner * heads + j, 0] = keys.astype(jnp.bfloat16)
        kv[owner * heads + j, 1] = values.astype(jnp.bfloat16)

    def project(j):
        both = jnp.dot(
            lat[...].reshape(rows, lat.shape[2])[:, :width], wkv[j], preferred_element_type=jnp.float32
        )
        store(me, j, both[:, :nope], both[:, nope:])

    def project_arrived(owner, j, way):
        some = lat[...].reshape(rows, lat.shape[2])[:, :width]
        slot = way * heads + j
        keys = jnp.dot(some, halves[slot, 0], preferred_element_type=jnp.float32)
        values = jnp.dot(some, halves[slot, 1], preferred_element_type=jnp.float32)
        store(owner, j, keys, values)

    def hand_over(*slots):
        for way, place_in in slots:
            j = (early_r, early_l)[way][place_in]
            half_over(j, way, rep).wait_recv()
            half_over(j, way, rep).start()

    if early:
        late_out(True)
        hand_over((1, 0))

        @pl.when(corner)
        def _():
            lat_take("EGFH")
            lat_meet("EGFH")

        @pl.when(inner)
        def _():
            lat_take("H")
            lat_meet("GH")

        late_out(False)
    else:
        @pl.loop(0, chips_half)
        def _(i):
            relay(far_chip(i))

        @pl.loop(0, chips_half)
        def _(i):
            lat_on(far_chip(i) * cores + other_core).wait_recv()
        for j in late:
            project(j)
            go_right(me, j).start()
            go_left(me, j).start()

    for j in range(early):
        project(j)
    if early:

        @pl.when(corner)
        def _():
            for j in range(early):
                send(me, j, LEFT, mine("C")).start()

        lend_out(4, len(lends))
    for j in range(heads):
        go_across(me, j).start()

    rope_part = lat[...].reshape(rows, lat.shape[2])[:, width:]
    blank = jnp.zeros_like(rope_part)
    ropes[0] = jnp.concatenate([rope_part, blank], axis=1)
    ropes[1] = jnp.concatenate([blank, rope_part], axis=1)

    if not early:
        q_copy.wait()

    lane = lax.broadcasted_iota(jnp.int32, (rows, nope), 1)
    upper = lane >= rope

    def attended(queries, owner, j):
        odd = parity(owner, j)
        head = owner * heads + j
        keys = kv[head, 0]
        values = kv[head, 1]

        def even_keys():
            return jnp.concatenate([keys, ropes[0]], axis=1)

        def odd_keys():
            return jnp.concatenate(
                [jnp.where(upper, keys, jnp.zeros_like(keys)), jnp.where(upper, ropes[1], keys)], axis=1
            )

        if isinstance(odd, int):
            keys_full = odd_keys() if odd else even_keys()
        else:
            keys_full = jnp.where(odd == 1, odd_keys(), even_keys())
        scores = lax.dot_general(
            queries, keys_full, (((1,), (1,)), ((), ())), preferred_element_type=jnp.float32
        )
        row_max = jnp.max(scores, axis=1, keepdims=True)
        weights = jnp.exp2((scores - row_max) * scale)
        total = jnp.sum(weights, axis=1, keepdims=True)
        mixed = jnp.dot(weights.astype(jnp.bfloat16), values, preferred_element_type=jnp.float32)
        return (mixed * (1.0 / total)).astype(jnp.bfloat16)

    def attend(owner, j):
        at = pl.multiple_of((owner * heads + j) * nope, nope)
        o[:, pl.ds(at, nope)] = attended(q[:, pl.ds(query_start(owner, j), 2 * nope)], owner, j)

    attend(me, 0)
    if early:
        hand_over(*[(1, i) for i in range(1, early)], *[(0, i) for i in range(early)])
    for i in range(1, early):
        attend(me, i)
    for j in range(max(early, 1), heads):
        attend(me, j)

    def sent(stream, ref):
        pltpu.make_async_remote_copy(
            src_ref=ref,
            dst_ref=ref,
            send_sem=send_sem.at[stream],
            recv_sem=send_sem.at[stream],
            device_id={"ctx": across},
            device_id_type=MESH,
        ).wait_send()

    def around():
        def others(s):
            return (device_at(place - s, other_core), device_at(place + s, other_core))

        def attend_others(s, pos):
            pair = list(zip(others(s), (order_r, order_l)))
            for owner, js in pair:
                go_across(owner, js[pos]).wait_recv()
            return [(owner, js[pos]) for owner, js in pair]

        def ring_step(s, first, last):
            from_left = device_at(place - s, core)
            from_right = device_at(place + s, core)
            for pos in range(heads):
                jr, jl = order_r[pos], order_l[pos]
                for j, way, owner, go in ((jr, 0, from_left, go_right), (jl, 1, from_right, go_left)):
                    go(owner, j).wait_recv()
                    if not last or pos < (half_right if way == 0 else heads - half_right):
                        go(owner, j).start()
                    go_across(owner, j).start()
                todo = [(from_left, jr), (from_right, jl)]
                if first:
                    go_across(across, pos).wait_recv()
                    todo.append((across, pos))
                if pos > 0:
                    todo += attend_others(s, pos - 1)
                elif not first:
                    todo += attend_others(s - 1, heads - 1)
                for owner, j in todo:
                    attend(owner, j)

        ring_step(1, True, half == 2)
        if half > 3:

            @pl.loop(2, half - 1)
            def _(s):
                ring_step(s, False, False)

        if half > 2:
            ring_step(half - 1, False, True)

        far = device_at(place + half, core)
        far_other = device_at(place + half, other_core)
        todo = attend_others(half - 1, heads - 1)
        for pos in range(half_right):
            arrivals = [(order_r[pos], go_right)]
            if pos < heads - half_right:
                arrivals.append((order_l[pos], go_left))
            for j, go in arrivals:
                go(far, j).wait_recv()
                go_across(far, j).start()
                todo.append((far, j))
            for owner, j in todo:
                attend(owner, j)
            for j, _ in arrivals:
                go_across(far_other, j).wait_recv()
            for j, _ in arrivals:
                attend(far_other, j)
            todo = []

        sent(RIGHT, kv.at[pl.ds(0, (half - 1) * heads + half_right)])
        sent(LEFT, kv.at[pl.ds(0, half * heads - half_right)])
        sent(ACROSS, kv.at[pl.ds(0, chips * heads)])

    def arrived(name, j, way):
        owner = mine(name)
        direct = {0: "B" if name == "B" else "D", 1: "C" if name == "C" else "E", 2: "A"}
        if way is None or name != direct[way]:
            go_across(owner, j).wait_recv()
        elif way == 0 or (way == 1 and j < early):
            half_over(j, way, 1 - rep).wait_recv()
            project_arrived(owner, j, way)
        elif j >= early:
            side = owner // (devices // 2)
            quarters = 3 if way == 1 else 2
            half_hop(owner, j, piece_of(side, quarters, True), True, way, RIGHT, across).wait_recv()
            half_hop(owner, j, piece_of(side, quarters, False), False, way, RIGHT, across).wait_recv()
        else:
            go_across(owner, j).wait_recv()

    def later_hands(k):
        if k in (0, 2):
            hand_over((0, early + k // 2))

    def follow(name, j):
        owner = chip_of(name, other_core)
        go_across(owner, j).wait_recv()
        return owner, j

    def at_corner():
        events = [[("C", j, 1)] for j in order_l]
        for jz, jy in zip(order_l, order_r):
            events.append([("E", jz, None), ("D", jz, None), ("B", jy, 0)])
        for k in range(heads):
            events.append([("G", j, None) for j in keep[k : k + 1]] + [("F", order_l[k], None)])
        events.append([("H", order_a[3], None)])
        lag = []
        for k, now in enumerate(events):
            for name, j, way in now:
                arrived(name, j, way)
                if name in "CE" or (name == "G" and j == order_a[3]):
                    send(mine(name), j, RIGHT, beside).start()
                go_across(mine(name), j).start()
            later_hands(k)
            todo = [(mine(name), j) for name, j, _ in now]
            if k < heads:
                go_across(across, k).wait_recv()
                todo.append((across, k))
            todo += [follow(name, j) for name, j in lag]
            for owner, j in todo:
                attend(owner, j)
            lag = [(name, j) for name, j, _ in now]
        for name, j in lag:
            attend(*follow(name, j))
        pltpu.make_async_copy(mixed_out, mixed_out, lend_sem.at[1]).wait()
        sent(RIGHT, kv.at[pl.ds(0, 2 * heads + 1)])
        sent(LAT_OUT, lat.at[pl.ds(0, 4)])
        sent(LEFT, kv.at[pl.ds(0, heads)])
        sent(ACROSS, kv.at[pl.ds(0, 6 * heads + len(keep) + 1)])
        sent(LEND, lent)

    def at_inner():
        events = []
        for k in range(heads):
            events.append([("E", order_l[k], 1), ("A", order_a[k], 2)])
        events[heads - 1].append(("F", order_l[0], None))
        for k in range(heads):
            events.append([("B", order_a[k], None), ("G", order_a[k], None), ("D", order_r[k], 0)])
        for k in range(heads):
            events.append([("H", order_a[k], None)])
            if k > 0:
                events[-1].append(("F", order_l[k], None))
            if k == heads - 2:
                events.append([])
        lag = []
        held = []
        for k, now in enumerate(events):
            for name, j, way in now:
                arrived(name, j, way)
                if name == "A":
                    send(mine("A"), j, MID, mine("E")).start()
                    send(mine("A"), j, RIGHT, beside).start()
                elif name == "B":
                    send(mine("B"), j, MID, mine("E")).start()
                elif name == "E":
                    send(mine("E"), j, LEFT, mine("A")).start()
                    if j == order_l[0]:
                        send(mine("E"), j, RIGHT, beside).start()
                elif name == "G" and j in keep:
                    send(mine("G"), j, LEFT, mine("A")).start()
                go_across(mine(name), j).start()
            for name, j, _ in now:
                if name == "H" and j in ship:
                    give_back(name, j, core).start()
            later_hands(k)
            if k == heads - 1:
                for j in order_l[1:]:
                    send(mine("E"), j, RIGHT, beside).start()
            todo = [(mine(name), j) for name, j, _ in now]
            if k < heads:
                go_across(across, k).wait_recv()
                todo.append((across, k))
            todo += [follow(name, j) for name, j in lag]
            back = []
            if ("G", order_a[1]) in lag:
                pltpu.make_async_copy(lent, lent, lend_sem.at[0]).wait()
            for name, j in lag:
                if (name, 0, j) in lends:
                    back += [give_back(name, j, which) for which in ((core, other_core) if name == "G" else (other_core,))]
            for copy in back:
                copy.start()
            held += todo
            if events[k + 1 : k + 2] != [[]]:
                for owner, j in held:
                    attend(owner, j)
                held = []
            lag = [(name, j) for name, j, _ in now]
        for name, j in lag:
            attend(*follow(name, j))
        sent(RIGHT, kv.at[pl.ds(0, 2 * heads)])
        sent(LAT_OUT, lat.at[pl.ds(0, 10)])
        sent(LEFT, kv.at[pl.ds(0, heads - early + heads + len(keep))])
        sent(MID, kv.at[pl.ds(0, heads - early + 2 * heads)])
        sent(ACROSS, kv.at[pl.ds(0, 8 * heads)])
        sent(HALF_L, halves.at[pl.ds(0, 2 * early), 0])
        sent(LEND, mixed_out)

    if early:
        pl.when(corner)(at_corner)
        pl.when(inner)(at_inner)
        sent(HALF_R, halves.at[pl.ds(0, heads), 0])
        sent(HALF_X, halves.at[pl.ds(0, heads + early), 0])
    else:
        around()
        sent(LAT_OUT, lat.at[pl.ds(0, chips - 1)])
    sent(LAT_ON, lat.at[pl.ds(0, chips)])


def on_device(grid_y, cores, early, queries, latents, w_key, w_value):
    devices = lax.axis_size("ctx")
    heads, width, nope = w_key.shape
    query_rows = queries.shape[0]
    block = latents.shape[0]
    rows = block * devices
    anywhere = pl.BlockSpec(memory_space=pl.ANY)
    dma = pltpu.SemaphoreType.DMA
    return pl.pallas_call(
        functools.partial(kernel, grid_y, cores, early),
        out_shape=jax.ShapeDtypeStruct((query_rows, devices * heads * nope), jnp.bfloat16),
        in_specs=[anywhere] * 4,
        out_specs=pl.BlockSpec(memory_space=pltpu.VMEM),
        scratch_shapes=[
            pltpu.VMEM(queries.shape, jnp.bfloat16),
            pltpu.VMEM((devices, block, latents.shape[1]), jnp.bfloat16),
            pltpu.VMEM((heads, width, 2 * nope), jnp.bfloat16),
            pltpu.VMEM((2, rows, nope), jnp.bfloat16),
            pltpu.VMEM((devices * heads, 2, rows, nope), jnp.bfloat16),
            pltpu.VMEM((heads + early if early else 1, 2, width, nope), jnp.bfloat16),
            dma((3,)),
            dma((devices,)),
            dma((devices * heads,)),
            dma((heads + early if early else 1, 2)),
            dma((10,)),
            dma((2, max(heads - early, 1))),
            pltpu.VMEM((10 if early else 1, query_rows, 2 * nope), jnp.bfloat16),
            pltpu.VMEM((10 if early else 1, query_rows, nope), jnp.bfloat16),
            dma((2,)),
        ],
        compiler_params=pltpu.CompilerParams(
            collective_id=0, has_side_effects=True, vmem_limit_bytes=50 * 1024 * 1024
        ),
    )(*(pltpu.with_memory_space_constraint(a, pltpu.HBM) for a in (queries, latents, w_key, w_value)))


def layout_of(mesh):
    group = list(mesh.devices.reshape(-1, mesh.shape["ctx"])[0])
    places = [tuple(d.coords) for d in group]
    chips = sorted(set(places))
    cores = len(group) // len(chips)
    varied = [axis for axis in range(3) if len({c[axis] for c in chips}) > 1]
    grid_y = 1
    if len(varied) == 2:
        fast = len({c[varied[0]] for c in chips})
        grid_y = 2 if fast == 2 else 1
    return grid_y, cores


def solution(mesh):
    grid_y, cores = layout_of(mesh)
    chips = mesh.shape["ctx"] // cores
    early = 2 if mesh.shape["rep"] == 2 and grid_y == 2 and chips // grid_y == 4 and cores == 2 else 0
    return jax.shard_map(
        functools.partial(on_device, grid_y, cores, early),
        mesh=mesh,
        in_specs=(
            P(("rep", "ctx"), None),
            P(("rep", "ctx"), None),
            P("ctx", None, None),
            P("ctx", None, None),
        ),
        out_specs=P(("rep", "ctx"), None),
        check_vma=False,
    )
```

```python
import functools
import math

import jax
import jax.numpy as jnp
from jax import lax
from jax.experimental import pallas as pl
from jax.experimental.pallas import tpu as pltpu
from jax.sharding import PartitionSpec as P

MESH = pl.DeviceIdType.MESH


def kernel(
    grid_y,
    cores,
    early,
    q_hbm,
    lat_hbm,
    wk_hbm,
    wv_hbm,
    o,
    q,
    lat,
    wkv,
    ropes,
    kv,
    halves,
    load_sem,
    lat_recv,
    kv_recv,
    half_recv,
    send_sem,
    part_recv,
    lent,
    mixed_out,
    lend_sem,
):
    devices = lat.shape[0]
    heads = wkv.shape[0]
    rows = kv.shape[2]
    nope = kv.shape[3]
    width = wkv.shape[1]
    rope = lat.shape[2] - width
    qk = nope + rope
    chips = devices // cores
    grid_z = chips // grid_y
    half = chips // 2
    scale = math.log2(math.e) / math.sqrt(qk)

    half_right = (heads + 1) // 2
    late = list(range(early, heads))
    order_r = late + list(range(early))
    order_l = order_r[half_right:] + order_r[:half_right]
    if early:
        order_l = [early - 1] + late[::-1] + list(range(early - 1))
        order_r = list(range(heads))
    order_a = late + list(range(early))
    keep = order_a[:1] + order_a[3:]
    ship = order_a[:3]

    me = lax.axis_index("ctx")
    core = lax.rem(me, cores)
    my_chip = me // cores
    my_y = lax.rem(my_chip, grid_y)
    my_z = my_chip // grid_y
    place = (1 - my_y) * my_z + my_y * (2 * grid_z - 1 - my_z)

    def device_at(spot, which):
        spot = lax.rem(spot + 2 * chips, chips)
        y = spot // grid_z
        z = (1 - y) * spot + y * (2 * grid_z - 1 - spot)
        return (z * grid_y + y) * cores + which

    other_core = cores - 1 - core
    across = my_chip * cores + other_core
    right = device_at(place + 1, core)
    left = device_at(place - 1, core)
    rep = lax.axis_index("rep")
    top = my_z // (grid_z // 2)
    inward = 1 - 2 * top
    z_a = top * (grid_z - 1)
    z_g = (1 - top) * (grid_z - 1)
    corner = my_z == z_a
    inner = my_z != z_a

    def chip_of(name, which):
        z = {"A": z_a, "C": z_a + inward, "E": z_g - inward, "G": z_g}
        z |= {"B": z["A"], "D": z["C"], "F": z["E"], "H": z["G"]}
        y = my_y if name in "ACEG" else 1 - my_y
        return (z[name] * grid_y + y) * cores + which

    def mine(name):
        return chip_of(name, core)

    barrier = pltpu.get_barrier_semaphore()

    plane = grid_y * cores
    beside = (my_z * grid_y + 1 - my_y) * cores + core
    steps = [(0, 1, True), (-1, 1, my_z > 0), (1, 1, my_z < grid_z - 1)]
    steps += [(-1, 0, my_z > 0), (1, 0, my_z < grid_z - 1), (-2, 0, my_z > 1), (2, 0, my_z < grid_z - 2)]

    def greet(sem):
        for dz, dy, there in steps:
            to = (beside if dy else me) + dz * plane

            def tell():
                pl.semaphore_signal(sem, inc=1, device_id={"ctx": to}, device_id_type=MESH)

            if there is True:
                tell()
            else:
                pl.when(there)(tell)

    greeted = 1
    for _, _, there in steps[1:]:
        greeted = greeted + lax.convert_element_type(there, jnp.int32)
    if early:
        greet(barrier)
        pl.semaphore_signal(barrier, inc=1, device_id={"rep": 1 - rep}, device_id_type=MESH)
    else:

        @pl.loop(1, chips)
        def _(d):
            pl.semaphore_signal(
                barrier, inc=1, device_id={"ctx": device_at(place + d, core)}, device_id_type=MESH
            )

    pl.semaphore_signal(barrier, inc=1, device_id={"ctx": across}, device_id_type=MESH)

    q_copy = pltpu.make_async_copy(q_hbm, q, load_sem.at[0])
    lat_copy = pltpu.make_async_copy(lat_hbm, lat.at[me], load_sem.at[1])
    lat_copy.start()
    for j in range(heads):
        pltpu.make_async_copy(wk_hbm.at[j], wkv.at[j, :, pl.ds(0, nope)], load_sem.at[2]).start()
        pltpu.make_async_copy(wv_hbm.at[j], wkv.at[j, :, pl.ds(nope, nope)], load_sem.at[2]).start()
    q_copy.start()

    pl.semaphore_wait(barrier, greeted + 2 if early else chips)

    LAT_OUT, LAT_ON, RIGHT, LEFT, MID, ACROSS, HALF_R, HALF_L, HALF_X, LEND = range(10)

    near = me // (devices // 2)
    chips_half = chips // 2

    def near_chip(i):
        return near * chips_half + lax.rem(my_chip - near * chips_half + i, chips_half)

    def far_chip(i):
        return (1 - near) * chips_half + lax.rem(my_chip - near * chips_half + i, chips_half)

    def lat_out(owner, chip):
        return pltpu.make_async_remote_copy(
            src_ref=lat.at[owner],
            dst_ref=lat.at[owner],
            send_sem=send_sem.at[LAT_OUT],
            recv_sem=lat_recv.at[owner],
            device_id={"ctx": chip * cores + core},
            device_id_type=MESH,
        )

    def lat_on(owner):
        return pltpu.make_async_remote_copy(
            src_ref=lat.at[owner],
            dst_ref=lat.at[owner],
            send_sem=send_sem.at[LAT_ON],
            recv_sem=lat_recv.at[owner],
            device_id={"ctx": across},
            device_id_type=MESH,
        )

    lat_copy.wait()

    def lat_near(owner):
        @pl.loop(1, chips_half)
        def _(i):
            lat_out(owner, near_chip(i)).start()

    pieces = 4
    deep = width // pieces

    def half_out(src, j, way, target, piece):
        return pltpu.make_async_remote_copy(
            src_ref=src.at[j, pl.ds(piece * deep, deep)],
            dst_ref=halves.at[way * heads + j, rep, pl.ds(piece * deep, deep)],
            send_sem=send_sem.at[HALF_R + way],
            recv_sem=half_recv.at[way * heads + j, rep],
            device_id={"ctx": target},
            device_id_type=MESH,
        )

    def half_over(j, way, which):
        return pltpu.make_async_remote_copy(
            src_ref=halves.at[way * heads + j, which],
            dst_ref=halves.at[way * heads + j, which],
            send_sem=send_sem.at[HALF_X],
            recv_sem=half_recv.at[way * heads + j, which],
            device_id={"rep": 1 - rep},
            device_id_type=MESH,
        )

    early_r = order_r
    early_l = [j for j in order_l if j < early]

    def relay(chip):
        owner = chip * cores + core
        lat_on(owner).wait_recv()
        lat_on(owner).start()

    def parity(owner, j):
        if heads % 2 == 0:
            return j % 2
        return lax.rem(owner * heads + j, 2)

    def weights_out(first, last):
        for which, src in ((0, wk_hbm), (1, wv_hbm)):

            @pl.when(rep == which)
            def _():
                for i in range(first, last):
                    half_out(src, early_r[i // pieces], 0, beside, i % pieces).start()

            @pl.when(jnp.logical_and(rep == which, inner))
            def _():
                for i in range(first, min(last, early * pieces)):
                    for target in (mine("A"), mine("E")):
                        half_out(src, early_l[i // pieces], 1, target, i % pieces).start()

    lends = [("G", c, j) for j in order_a[1:3] for c in range(cores)]
    lends += [("H", c, j) for j in ship for c in range(cores)]

    def query_start(owner, j):
        odd = parity(owner, j)
        pair = owner * (heads // 2) + j // 2 if heads % 2 == 0 else (owner * heads + j) // 2
        return pl.multiple_of(pair * (2 * qk) + odd * nope, nope)

    def lend(i):
        name, which, j = lends[i]
        return pltpu.make_async_remote_copy(
            src_ref=q.at[:, pl.ds(query_start(chip_of(name, which), j), 2 * nope)],
            dst_ref=lent.at[i],
            send_sem=send_sem.at[LEND],
            recv_sem=lend_sem.at[0 if i < 4 else 2],
            device_id={"ctx": mine("C")},
            device_id_type=MESH,
        )

    def give_back(name, j, which):
        item = chip_of(name, which) * heads + j
        slot = lends.index((name, 0, j)) + which
        mixed_out[slot] = attended(lent[slot], chip_of(name, which), j)
        return pltpu.make_async_remote_copy(
            src_ref=mixed_out.at[slot],
            dst_ref=o.at[:, pl.ds(pl.multiple_of(item * nope, nope), nope)],
            send_sem=send_sem.at[LEND],
            recv_sem=lend_sem.at[1],
            device_id={"ctx": mine("A")},
            device_id_type=MESH,
        )

    def lend_out(first, last):
        @pl.when(corner)
        def _():
            for i in range(first, last):
                lend(i).start()

    if early:

        def lat_to(owner, names):
            for name in names:
                lat_out(owner, mine(name) // cores).start()

        def lat_take(names):
            for name in names:
                lat_on(mine(name)).wait_recv()
                lat_on(mine(name)).start()

        def lat_meet(names):
            for name in names:
                lat_on(chip_of(name, other_core)).wait_recv()

        pl.when(corner)(lambda: lat_to(me, "EDCB"))
        pl.when(inner)(lambda: lat_to(me, "GFBEAD"))
        lat_on(me).start()
        weights_out(0, pieces)
        q_copy.wait()
        lend_out(0, 4)

        @pl.when(inner)
        def _():
            lat_take("G")
            lat_to(mine("G"), "BAD")
            lat_take("F")
            lat_to(mine("F"), "A")

        weights_out(pieces, heads * pieces)

        @pl.when(corner)
        def _():
            lat_take("BCD")
            lat_meet("ABCD")

        @pl.when(inner)
        def _():
            lat_take("ABDE")
            lat_meet("ABCDEF")

    else:
        lat_near(me)

        @pl.loop(0, chips_half)
        def _(i):
            lat_out(me, far_chip(i)).start()

        lat_on(me).start()

        @pl.loop(1, chips_half)
        def _(i):
            relay(near_chip(i))

        @pl.loop(0, chips_half)
        def _(i):
            lat_on(near_chip(i) * cores + other_core).wait_recv()

    pltpu.make_async_copy(wkv, wkv, load_sem.at[2]).wait()

    def send(owner, j, stream, target):
        return pltpu.make_async_remote_copy(
            src_ref=kv.at[owner * heads + j],
            dst_ref=kv.at[owner * heads + j],
            send_sem=send_sem.at[stream],
            recv_sem=kv_recv.at[owner * heads + j],
            device_id={"ctx": target},
            device_id_type=MESH,
        )

    def go_right(owner, j):
        return send(owner, j, RIGHT, right)

    def go_left(owner, j):
        return send(owner, j, LEFT, left)

    def go_across(owner, j):
        return send(owner, j, ACROSS, across)

    def piece_of(side, quarters, is_first):
        size = quarters if is_first else 4 - quarters
        return (side if is_first else 1 - side) * (4 - size), size

    def half_hop(owner, j, piece, is_first, way, stream, target):
        begin, size = piece
        quarter = rows // 4
        ref = kv.at[owner * heads + j, :, pl.ds(pl.multiple_of(begin * quarter, quarter), size * quarter)]
        sem = part_recv.at[way - 1, j - early] if is_first else kv_recv.at[owner * heads + j]
        return pltpu.make_async_remote_copy(
            src_ref=ref,
            dst_ref=ref,
            send_sem=send_sem.at[stream],
            recv_sem=sem,
            device_id={"ctx": target},
            device_id_type=MESH,
        )

    def project_part(j, piece):
        begin, size = piece
        some = lat[pl.ds(begin * (devices // 4), size * (devices // 4))]
        some = some.reshape(size * rows // 4, lat.shape[2])[:, :width]
        both = jnp.dot(some, wkv[j], preferred_element_type=jnp.float32)
        keys = both[:, :nope]
        if parity(me, j) == 1:
            keys = jnp.concatenate([keys[:, rope:], keys[:, :rope]], axis=1)
        at = pl.ds(pl.multiple_of(begin * (rows // 4), rows // 4), size * (rows // 4))
        kv[me * heads + j, 0, at] = keys.astype(jnp.bfloat16)
        kv[me * heads + j, 1, at] = both[:, nope:].astype(jnp.bfloat16)

    late_l = [j for j in order_l if j >= early]

    def late_out(is_first):
        @pl.when(corner)
        def _():
            piece = piece_of(top, 2, is_first)
            for j in late:
                project_part(j, piece)
            for j in late:
                half_hop(me, j, piece, is_first, 2, LEFT, mine("C")).start()

        @pl.when(inner)
        def _():
            piece = piece_of(top, 3, is_first)
            for j in late:
                project_part(j, piece)
            for j in late_l:
                half_hop(me, j, piece, is_first, 1, LEFT, mine("A")).start()
                half_hop(me, j, piece, is_first, 1, MID, mine("E")).start()

    def store(owner, j, keys, values):
        odd = parity(owner, j)
        turned = jnp.concatenate([keys[:, rope:], keys[:, :rope]], axis=1)
        if isinstance(odd, int):
            keys = turned if odd else keys
        else:
            keys = jnp.where(odd == 1, turned, keys)
        kv[owner * heads + j, 0] = keys.astype(jnp.bfloat16)
        kv[owner * heads + j, 1] = values.astype(jnp.bfloat16)

    def project(j):
        both = jnp.dot(
            lat[...].reshape(rows, lat.shape[2])[:, :width], wkv[j], preferred_element_type=jnp.float32
        )
        store(me, j, both[:, :nope], both[:, nope:])

    def project_arrived(owner, j, way):
        some = lat[...].reshape(rows, lat.shape[2])[:, :width]
        slot = way * heads + j
        keys = jnp.dot(some, halves[slot, 0], preferred_element_type=jnp.float32)
        values = jnp.dot(some, halves[slot, 1], preferred_element_type=jnp.float32)
        store(owner, j, keys, values)

    def hand_over(*slots):
        for way, place_in in slots:
            j = (early_r, early_l)[way][place_in]
            half_over(j, way, rep).wait_recv()
            half_over(j, way, rep).start()

    if early:
        late_out(True)
        hand_over((1, 0))

        @pl.when(corner)
        def _():
            lat_take("EGFH")
            lat_meet("EGFH")

        @pl.when(inner)
        def _():
            lat_take("H")
            lat_meet("GH")

        late_out(False)
    else:
        @pl.loop(0, chips_half)
        def _(i):
            relay(far_chip(i))

        @pl.loop(0, chips_half)
        def _(i):
            lat_on(far_chip(i) * cores + other_core).wait_recv()
        for j in late:
            project(j)
            go_right(me, j).start()
            go_left(me, j).start()

    for j in range(early):
        project(j)
    if early:

        @pl.when(corner)
        def _():
            for j in range(early):
                send(me, j, LEFT, mine("C")).start()

        lend_out(4, len(lends))
    for j in range(heads):
        go_across(me, j).start()

    rope_part = lat[...].reshape(rows, lat.shape[2])[:, width:]
    blank = jnp.zeros_like(rope_part)
    ropes[0] = jnp.concatenate([rope_part, blank], axis=1)
    ropes[1] = jnp.concatenate([blank, rope_part], axis=1)

    if not early:
        q_copy.wait()

    lane = lax.broadcasted_iota(jnp.int32, (rows, nope), 1)
    upper = lane >= rope

    def attended(queries, owner, j):
        odd = parity(owner, j)
        head = owner * heads + j
        keys = kv[head, 0]
        values = kv[head, 1]

        def even_keys():
            return jnp.concatenate([keys, ropes[0]], axis=1)

        def odd_keys():
            return jnp.concatenate(
                [jnp.where(upper, keys, jnp.zeros_like(keys)), jnp.where(upper, ropes[1], keys)], axis=1
            )

        if isinstance(odd, int):
            keys_full = odd_keys() if odd else even_keys()
        else:
            keys_full = jnp.where(odd == 1, odd_keys(), even_keys())
        scores = lax.dot_general(
            queries, keys_full, (((1,), (1,)), ((), ())), preferred_element_type=jnp.float32
        )
        row_max = jnp.max(scores, axis=1, keepdims=True)
        weights = jnp.exp2((scores - row_max) * scale)
        total = jnp.sum(weights, axis=1, keepdims=True)
        mixed = jnp.dot(weights.astype(jnp.bfloat16), values, preferred_element_type=jnp.float32)
        return (mixed * (1.0 / total)).astype(jnp.bfloat16)

    def attend(owner, j):
        at = pl.multiple_of((owner * heads + j) * nope, nope)
        o[:, pl.ds(at, nope)] = attended(q[:, pl.ds(query_start(owner, j), 2 * nope)], owner, j)

    attend(me, 0)
    if early:
        hand_over(*[(1, i) for i in range(1, early)], *[(0, i) for i in range(early)])
    for i in range(1, early):
        attend(me, i)
    for j in range(max(early, 1), heads):
        attend(me, j)

    def sent(stream, ref):
        pltpu.make_async_remote_copy(
            src_ref=ref,
            dst_ref=ref,
            send_sem=send_sem.at[stream],
            recv_sem=send_sem.at[stream],
            device_id={"ctx": across},
            device_id_type=MESH,
        ).wait_send()

    def around():
        def others(s):
            return (device_at(place - s, other_core), device_at(place + s, other_core))

        def attend_others(s, pos):
            pair = list(zip(others(s), (order_r, order_l)))
            for owner, js in pair:
                go_across(owner, js[pos]).wait_recv()
            return [(owner, js[pos]) for owner, js in pair]

        def ring_step(s, first, last):
            from_left = device_at(place - s, core)
            from_right = device_at(place + s, core)
            for pos in range(heads):
                jr, jl = order_r[pos], order_l[pos]
                for j, way, owner, go in ((jr, 0, from_left, go_right), (jl, 1, from_right, go_left)):
                    go(owner, j).wait_recv()
                    if not last or pos < (half_right if way == 0 else heads - half_right):
                        go(owner, j).start()
                    go_across(owner, j).start()
                todo = [(from_left, jr), (from_right, jl)]
                if first:
                    go_across(across, pos).wait_recv()
                    todo.append((across, pos))
                if pos > 0:
                    todo += attend_others(s, pos - 1)
                elif not first:
                    todo += attend_others(s - 1, heads - 1)
                for owner, j in todo:
                    attend(owner, j)

        ring_step(1, True, half == 2)
        if half > 3:

            @pl.loop(2, half - 1)
            def _(s):
                ring_step(s, False, False)

        if half > 2:
            ring_step(half - 1, False, True)

        far = device_at(place + half, core)
        far_other = device_at(place + half, other_core)
        todo = attend_others(half - 1, heads - 1)
        for pos in range(half_right):
            arrivals = [(order_r[pos], go_right)]
            if pos < heads - half_right:
                arrivals.append((order_l[pos], go_left))
            for j, go in arrivals:
                go(far, j).wait_recv()
                go_across(far, j).start()
                todo.append((far, j))
            for owner, j in todo:
                attend(owner, j)
            for j, _ in arrivals:
                go_across(far_other, j).wait_recv()
            for j, _ in arrivals:
                attend(far_other, j)
            todo = []

        sent(RIGHT, kv.at[pl.ds(0, (half - 1) * heads + half_right)])
        sent(LEFT, kv.at[pl.ds(0, half * heads - half_right)])
        sent(ACROSS, kv.at[pl.ds(0, chips * heads)])

    def arrived(name, j, way):
        owner = mine(name)
        direct = {0: "B" if name == "B" else "D", 1: "C" if name == "C" else "E", 2: "A"}
        if way is None or name != direct[way]:
            go_across(owner, j).wait_recv()
        elif way == 0 or (way == 1 and j < early):
            half_over(j, way, 1 - rep).wait_recv()
            project_arrived(owner, j, way)
        elif j >= early:
            side = owner // (devices // 2)
            quarters = 3 if way == 1 else 2
            half_hop(owner, j, piece_of(side, quarters, True), True, way, RIGHT, across).wait_recv()
            half_hop(owner, j, piece_of(side, quarters, False), False, way, RIGHT, across).wait_recv()
        else:
            go_across(owner, j).wait_recv()

    def later_hands(k):
        if k in (0, 2):
            hand_over((0, early + k // 2))

    def follow(name, j):
        owner = chip_of(name, other_core)
        go_across(owner, j).wait_recv()
        return owner, j

    def at_corner():
        events = [[("C", j, 1)] for j in order_l]
        for jz, jy in zip(order_l, order_r):
            events.append([("E", jz, None), ("D", jz, None), ("B", jy, 0)])
        for k in range(heads):
            events.append([("G", j, None) for j in keep[k : k + 1]] + [("F", order_l[k], None)])
        events.append([("H", order_a[3], None)])
        lag = []
        for k, now in enumerate(events):
            for name, j, way in now:
                arrived(name, j, way)
                if name in "CE" or (name == "G" and j == order_a[3]):
                    send(mine(name), j, RIGHT, beside).start()
                go_across(mine(name), j).start()
            later_hands(k)
            todo = [(mine(name), j) for name, j, _ in now]
            if k < heads:
                go_across(across, k).wait_recv()
                todo.append((across, k))
            todo += [follow(name, j) for name, j in lag]
            for owner, j in todo:
                attend(owner, j)
            lag = [(name, j) for name, j, _ in now]
        for name, j in lag:
            attend(*follow(name, j))
        pltpu.make_async_copy(mixed_out, mixed_out, lend_sem.at[1]).wait()
        sent(RIGHT, kv.at[pl.ds(0, 2 * heads + 1)])
        sent(LAT_OUT, lat.at[pl.ds(0, 4)])
        sent(LEFT, kv.at[pl.ds(0, heads)])
        sent(ACROSS, kv.at[pl.ds(0, 6 * heads + len(keep) + 1)])
        sent(LEND, lent)

    def at_inner():
        events = []
        for k in range(heads):
            events.append([("E", order_l[k], 1), ("A", order_a[k], 2)])
        events[heads - 1].append(("F", order_l[0], None))
        for k in range(heads):
            events.append([("B", order_a[k], None), ("G", order_a[k], None), ("D", order_r[k], 0)])
        for k in range(heads):
            events.append([("H", order_a[k], None)])
            if k > 0:
                events[-1].append(("F", order_l[k], None))
            if k == heads - 2:
                events.append([])
        lag = []
        held = []
        for k, now in enumerate(events):
            for name, j, way in now:
                arrived(name, j, way)
                if name == "A":
                    send(mine("A"), j, MID, mine("E")).start()
                    send(mine("A"), j, RIGHT, beside).start()
                elif name == "B":
                    send(mine("B"), j, MID, mine("E")).start()
                elif name == "E":
                    send(mine("E"), j, LEFT, mine("A")).start()
                    if j == order_l[0]:
                        send(mine("E"), j, RIGHT, beside).start()
                elif name == "G" and j in keep:
                    send(mine("G"), j, LEFT, mine("A")).start()
                go_across(mine(name), j).start()
            for name, j, _ in now:
                if name == "H" and j == ship[0]:
                    rest = lent.at[pl.ds(4, len(lends) - 4)]
                    pltpu.make_async_copy(rest, rest, lend_sem.at[2]).wait()
                if name == "H" and j in ship:
                    give_back(name, j, core).start()
            later_hands(k)
            if k == heads - 1:
                for j in order_l[1:]:
                    send(mine("E"), j, RIGHT, beside).start()
            todo = [(mine(name), j) for name, j, _ in now]
            if k < heads:
                go_across(across, k).wait_recv()
                todo.append((across, k))
            todo += [follow(name, j) for name, j in lag]
            back = []
            if ("G", order_a[1]) in lag:
                pltpu.make_async_copy(lent.at[pl.ds(0, 4)], lent.at[pl.ds(0, 4)], lend_sem.at[0]).wait()
            for name, j in lag:
                if (name, 0, j) in lends:
                    back += [give_back(name, j, which) for which in ((core, other_core) if name == "G" else (other_core,))]
            for copy in back:
                copy.start()
            held += todo
            if events[k + 1 : k + 2] != [[]]:
                for owner, j in held:
                    attend(owner, j)
                held = []
            lag = [(name, j) for name, j, _ in now]
        for name, j in lag:
            attend(*follow(name, j))
        sent(RIGHT, kv.at[pl.ds(0, 2 * heads)])
        sent(LAT_OUT, lat.at[pl.ds(0, 10)])
        sent(LEFT, kv.at[pl.ds(0, heads - early + heads + len(keep))])
        sent(MID, kv.at[pl.ds(0, heads - early + 2 * heads)])
        sent(ACROSS, kv.at[pl.ds(0, 8 * heads)])
        sent(HALF_L, halves.at[pl.ds(0, 2 * early), 0])
        sent(LEND, mixed_out)

    if early:
        pl.when(corner)(at_corner)
        pl.when(inner)(at_inner)
        sent(HALF_R, halves.at[pl.ds(0, heads), 0])
        sent(HALF_X, halves.at[pl.ds(0, heads + early), 0])
    else:
        around()
        sent(LAT_OUT, lat.at[pl.ds(0, chips - 1)])
    sent(LAT_ON, lat.at[pl.ds(0, chips)])


def on_device(grid_y, cores, early, queries, latents, w_key, w_value):
    devices = lax.axis_size("ctx")
    heads, width, nope = w_key.shape
    query_rows = queries.shape[0]
    block = latents.shape[0]
    rows = block * devices
    anywhere = pl.BlockSpec(memory_space=pl.ANY)
    dma = pltpu.SemaphoreType.DMA
    return pl.pallas_call(
        functools.partial(kernel, grid_y, cores, early),
        out_shape=jax.ShapeDtypeStruct((query_rows, devices * heads * nope), jnp.bfloat16),
        in_specs=[anywhere] * 4,
        out_specs=pl.BlockSpec(memory_space=pltpu.VMEM),
        scratch_shapes=[
            pltpu.VMEM(queries.shape, jnp.bfloat16),
            pltpu.VMEM((devices, block, latents.shape[1]), jnp.bfloat16),
            pltpu.VMEM((heads, width, 2 * nope), jnp.bfloat16),
            pltpu.VMEM((2, rows, nope), jnp.bfloat16),
            pltpu.VMEM((devices * heads, 2, rows, nope), jnp.bfloat16),
            pltpu.VMEM((heads + early if early else 1, 2, width, nope), jnp.bfloat16),
            dma((3,)),
            dma((devices,)),
            dma((devices * heads,)),
            dma((heads + early if early else 1, 2)),
            dma((10,)),
            dma((2, max(heads - early, 1))),
            pltpu.VMEM((10 if early else 1, query_rows, 2 * nope), jnp.bfloat16),
            pltpu.VMEM((10 if early else 1, query_rows, nope), jnp.bfloat16),
            dma((3,)),
        ],
        compiler_params=pltpu.CompilerParams(
            collective_id=0, has_side_effects=True, vmem_limit_bytes=50 * 1024 * 1024
        ),
    )(*(pltpu.with_memory_space_constraint(a, pltpu.HBM) for a in (queries, latents, w_key, w_value)))


def layout_of(mesh):
    group = list(mesh.devices.reshape(-1, mesh.shape["ctx"])[0])
    places = [tuple(d.coords) for d in group]
    chips = sorted(set(places))
    cores = len(group) // len(chips)
    varied = [axis for axis in range(3) if len({c[axis] for c in chips}) > 1]
    grid_y = 1
    if len(varied) == 2:
        fast = len({c[varied[0]] for c in chips})
        grid_y = 2 if fast == 2 else 1
    return grid_y, cores


def solution(mesh):
    grid_y, cores = layout_of(mesh)
    chips = mesh.shape["ctx"] // cores
    early = 2 if mesh.shape["rep"] == 2 and grid_y == 2 and chips // grid_y == 4 and cores == 2 else 0
    return jax.shard_map(
        functools.partial(on_device, grid_y, cores, early),
        mesh=mesh,
        in_specs=(
            P(("rep", "ctx"), None),
            P(("rep", "ctx"), None),
            P("ctx", None, None),
            P("ctx", None, None),
        ),
        out_specs=P(("rep", "ctx"), None),
        check_vma=False,
    )
```

```python
import functools
import math

import jax
import jax.numpy as jnp
from jax import lax
from jax.experimental import pallas as pl
from jax.experimental.pallas import tpu as pltpu
from jax.sharding import PartitionSpec as P

MESH = pl.DeviceIdType.MESH


def kernel(
    grid_y,
    cores,
    early,
    q_hbm,
    lat_hbm,
    wk_hbm,
    wv_hbm,
    o,
    q,
    lat,
    wkv,
    ropes,
    kv,
    halves,
    load_sem,
    lat_recv,
    kv_recv,
    half_recv,
    send_sem,
    part_recv,
    lent,
    mixed_out,
    lend_sem,
):
    devices = lat.shape[0]
    heads = wkv.shape[0]
    rows = kv.shape[2]
    nope = kv.shape[3]
    width = wkv.shape[1]
    rope = lat.shape[2] - width
    qk = nope + rope
    chips = devices // cores
    grid_z = chips // grid_y
    half = chips // 2
    scale = math.log2(math.e) / math.sqrt(qk)

    half_right = (heads + 1) // 2
    late = list(range(early, heads))
    order_r = late + list(range(early))
    order_l = order_r[half_right:] + order_r[:half_right]
    if early:
        order_l = [early - 1] + late[::-1] + list(range(early - 1))
        order_r = list(range(heads))
    order_a = late + list(range(early))
    keep = order_a[:1] + order_a[3:]
    ship = order_a[:3]

    me = lax.axis_index("ctx")
    core = lax.rem(me, cores)
    my_chip = me // cores
    my_y = lax.rem(my_chip, grid_y)
    my_z = my_chip // grid_y
    place = (1 - my_y) * my_z + my_y * (2 * grid_z - 1 - my_z)

    def device_at(spot, which):
        spot = lax.rem(spot + 2 * chips, chips)
        y = spot // grid_z
        z = (1 - y) * spot + y * (2 * grid_z - 1 - spot)
        return (z * grid_y + y) * cores + which

    other_core = cores - 1 - core
    across = my_chip * cores + other_core
    right = device_at(place + 1, core)
    left = device_at(place - 1, core)
    rep = lax.axis_index("rep")
    top = my_z // (grid_z // 2)
    inward = 1 - 2 * top
    z_a = top * (grid_z - 1)
    z_g = (1 - top) * (grid_z - 1)
    corner = my_z == z_a
    inner = my_z != z_a

    def chip_of(name, which):
        z = {"A": z_a, "C": z_a + inward, "E": z_g - inward, "G": z_g}
        z |= {"B": z["A"], "D": z["C"], "F": z["E"], "H": z["G"]}
        y = my_y if name in "ACEG" else 1 - my_y
        return (z[name] * grid_y + y) * cores + which

    def mine(name):
        return chip_of(name, core)

    barrier = pltpu.get_barrier_semaphore()

    plane = grid_y * cores
    beside = (my_z * grid_y + 1 - my_y) * cores + core
    steps = [(0, 1, True), (-1, 1, my_z > 0), (1, 1, my_z < grid_z - 1)]
    steps += [(-1, 0, my_z > 0), (1, 0, my_z < grid_z - 1), (-2, 0, my_z > 1), (2, 0, my_z < grid_z - 2)]

    def greet(sem):
        for dz, dy, there in steps[::-1]:
            to = (beside if dy else me) + dz * plane

            def tell():
                pl.semaphore_signal(sem, inc=1, device_id={"ctx": to}, device_id_type=MESH)

            if there is True:
                tell()
            else:
                pl.when(there)(tell)

    greeted = 1
    for _, _, there in steps[1:]:
        greeted = greeted + lax.convert_element_type(there, jnp.int32)
    if early:
        greet(barrier)
        pl.semaphore_signal(barrier, inc=1, device_id={"rep": 1 - rep}, device_id_type=MESH)
    else:

        @pl.loop(1, chips)
        def _(d):
            pl.semaphore_signal(
                barrier, inc=1, device_id={"ctx": device_at(place + d, core)}, device_id_type=MESH
            )

    pl.semaphore_signal(barrier, inc=1, device_id={"ctx": across}, device_id_type=MESH)

    q_copy = pltpu.make_async_copy(q_hbm, q, load_sem.at[0])
    lat_copy = pltpu.make_async_copy(lat_hbm, lat.at[me], load_sem.at[1])
    lat_copy.start()
    for j in range(heads):
        pltpu.make_async_copy(wk_hbm.at[j], wkv.at[j, :, pl.ds(0, nope)], load_sem.at[2]).start()
        pltpu.make_async_copy(wv_hbm.at[j], wkv.at[j, :, pl.ds(nope, nope)], load_sem.at[2]).start()
    q_copy.start()

    pl.semaphore_wait(barrier, greeted + 2 if early else chips)

    LAT_OUT, LAT_ON, RIGHT, LEFT, MID, ACROSS, HALF_R, HALF_L, HALF_X, LEND = range(10)

    near = me // (devices // 2)
    chips_half = chips // 2

    def near_chip(i):
        return near * chips_half + lax.rem(my_chip - near * chips_half + i, chips_half)

    def far_chip(i):
        return (1 - near) * chips_half + lax.rem(my_chip - near * chips_half + i, chips_half)

    def lat_out(owner, chip):
        return pltpu.make_async_remote_copy(
            src_ref=lat.at[owner],
            dst_ref=lat.at[owner],
            send_sem=send_sem.at[LAT_OUT],
            recv_sem=lat_recv.at[owner],
            device_id={"ctx": chip * cores + core},
            device_id_type=MESH,
        )

    def lat_on(owner):
        return pltpu.make_async_remote_copy(
            src_ref=lat.at[owner],
            dst_ref=lat.at[owner],
            send_sem=send_sem.at[LAT_ON],
            recv_sem=lat_recv.at[owner],
            device_id={"ctx": across},
            device_id_type=MESH,
        )

    lat_copy.wait()

    def lat_near(owner):
        @pl.loop(1, chips_half)
        def _(i):
            lat_out(owner, near_chip(i)).start()

    pieces = 4
    deep = width // pieces

    def half_out(src, j, way, target, piece):
        return pltpu.make_async_remote_copy(
            src_ref=src.at[j, pl.ds(piece * deep, deep)],
            dst_ref=halves.at[way * heads + j, rep, pl.ds(piece * deep, deep)],
            send_sem=send_sem.at[HALF_R + way],
            recv_sem=half_recv.at[way * heads + j, rep],
            device_id={"ctx": target},
            device_id_type=MESH,
        )

    def half_over(j, way, which):
        return pltpu.make_async_remote_copy(
            src_ref=halves.at[way * heads + j, which],
            dst_ref=halves.at[way * heads + j, which],
            send_sem=send_sem.at[HALF_X],
            recv_sem=half_recv.at[way * heads + j, which],
            device_id={"rep": 1 - rep},
            device_id_type=MESH,
        )

    early_r = order_r
    early_l = [j for j in order_l if j < early]

    def relay(chip):
        owner = chip * cores + core
        lat_on(owner).wait_recv()
        lat_on(owner).start()

    def parity(owner, j):
        if heads % 2 == 0:
            return j % 2
        return lax.rem(owner * heads + j, 2)

    def weights_out(first, last):
        for which, src in ((0, wk_hbm), (1, wv_hbm)):

            @pl.when(rep == which)
            def _():
                for i in range(first, last):
                    half_out(src, early_r[i // pieces], 0, beside, i % pieces).start()

            @pl.when(jnp.logical_and(rep == which, inner))
            def _():
                for i in range(first, min(last, early * pieces)):
                    for target in (mine("A"), mine("E")):
                        half_out(src, early_l[i // pieces], 1, target, i % pieces).start()

    lends = [("G", c, j) for j in order_a[1:3] for c in range(cores)]
    lends += [("H", c, j) for j in ship for c in range(cores)]

    def query_start(owner, j):
        odd = parity(owner, j)
        pair = owner * (heads // 2) + j // 2 if heads % 2 == 0 else (owner * heads + j) // 2
        return pl.multiple_of(pair * (2 * qk) + odd * nope, nope)

    def lend(i):
        name, which, j = lends[i]
        return pltpu.make_async_remote_copy(
            src_ref=q.at[:, pl.ds(query_start(chip_of(name, which), j), 2 * nope)],
            dst_ref=lent.at[i],
            send_sem=send_sem.at[LEND],
            recv_sem=lend_sem.at[0 if i < 4 else 2],
            device_id={"ctx": mine("C")},
            device_id_type=MESH,
        )

    def give_back(name, j, which):
        item = chip_of(name, which) * heads + j
        slot = lends.index((name, 0, j)) + which
        mixed_out[slot] = attended(lent[slot], chip_of(name, which), j)
        return pltpu.make_async_remote_copy(
            src_ref=mixed_out.at[slot],
            dst_ref=o.at[:, pl.ds(pl.multiple_of(item * nope, nope), nope)],
            send_sem=send_sem.at[LEND],
            recv_sem=lend_sem.at[1],
            device_id={"ctx": mine("A")},
            device_id_type=MESH,
        )

    def lend_out(first, last):
        @pl.when(corner)
        def _():
            for i in range(first, last):
                lend(i).start()

    if early:

        def lat_to(owner, names):
            for name in names:
                lat_out(owner, mine(name) // cores).start()

        def lat_take(names):
            for name in names:
                lat_on(mine(name)).wait_recv()
                lat_on(mine(name)).start()

        def lat_meet(names):
            for name in names:
                lat_on(chip_of(name, other_core)).wait_recv()

        pl.when(corner)(lambda: lat_to(me, "EDCB"))
        pl.when(inner)(lambda: lat_to(me, "GFBEAD"))
        lat_on(me).start()
        weights_out(0, pieces)
        q_copy.wait()
        lend_out(0, 4)

        @pl.when(inner)
        def _():
            lat_take("G")
            lat_to(mine("G"), "BAD")
            lat_take("F")
            lat_to(mine("F"), "A")

        weights_out(pieces, heads * pieces)

        @pl.when(corner)
        def _():
            lat_take("BCD")
            lat_meet("ABCD")

        @pl.when(inner)
        def _():
            lat_take("ABDE")
            lat_meet("ABCDEF")

    else:
        lat_near(me)

        @pl.loop(0, chips_half)
        def _(i):
            lat_out(me, far_chip(i)).start()

        lat_on(me).start()

        @pl.loop(1, chips_half)
        def _(i):
            relay(near_chip(i))

        @pl.loop(0, chips_half)
        def _(i):
            lat_on(near_chip(i) * cores + other_core).wait_recv()

    pltpu.make_async_copy(wkv, wkv, load_sem.at[2]).wait()

    def send(owner, j, stream, target):
        return pltpu.make_async_remote_copy(
            src_ref=kv.at[owner * heads + j],
            dst_ref=kv.at[owner * heads + j],
            send_sem=send_sem.at[stream],
            recv_sem=kv_recv.at[owner * heads + j],
            device_id={"ctx": target},
            device_id_type=MESH,
        )

    def go_right(owner, j):
        return send(owner, j, RIGHT, right)

    def go_left(owner, j):
        return send(owner, j, LEFT, left)

    def go_across(owner, j):
        return send(owner, j, ACROSS, across)

    def piece_of(side, quarters, is_first):
        size = quarters if is_first else 4 - quarters
        return (side if is_first else 1 - side) * (4 - size), size

    def half_hop(owner, j, piece, is_first, way, stream, target):
        begin, size = piece
        quarter = rows // 4
        ref = kv.at[owner * heads + j, :, pl.ds(pl.multiple_of(begin * quarter, quarter), size * quarter)]
        sem = part_recv.at[way - 1, j - early] if is_first else kv_recv.at[owner * heads + j]
        return pltpu.make_async_remote_copy(
            src_ref=ref,
            dst_ref=ref,
            send_sem=send_sem.at[stream],
            recv_sem=sem,
            device_id={"ctx": target},
            device_id_type=MESH,
        )

    def project_part(j, piece):
        begin, size = piece
        some = lat[pl.ds(begin * (devices // 4), size * (devices // 4))]
        some = some.reshape(size * rows // 4, lat.shape[2])[:, :width]
        both = jnp.dot(some, wkv[j], preferred_element_type=jnp.float32)
        keys = both[:, :nope]
        if parity(me, j) == 1:
            keys = jnp.concatenate([keys[:, rope:], keys[:, :rope]], axis=1)
        at = pl.ds(pl.multiple_of(begin * (rows // 4), rows // 4), size * (rows // 4))
        kv[me * heads + j, 0, at] = keys.astype(jnp.bfloat16)
        kv[me * heads + j, 1, at] = both[:, nope:].astype(jnp.bfloat16)

    late_l = [j for j in order_l if j >= early]

    def late_out(is_first):
        @pl.when(corner)
        def _():
            piece = piece_of(top, 2, is_first)
            for j in late:
                project_part(j, piece)
            for j in late:
                half_hop(me, j, piece, is_first, 2, LEFT, mine("C")).start()

        @pl.when(inner)
        def _():
            piece = piece_of(top, 3, is_first)
            for j in late:
                project_part(j, piece)
            for j in late_l:
                half_hop(me, j, piece, is_first, 1, LEFT, mine("A")).start()
                half_hop(me, j, piece, is_first, 1, MID, mine("E")).start()

    def store(owner, j, keys, values):
        odd = parity(owner, j)
        turned = jnp.concatenate([keys[:, rope:], keys[:, :rope]], axis=1)
        if isinstance(odd, int):
            keys = turned if odd else keys
        else:
            keys = jnp.where(odd == 1, turned, keys)
        kv[owner * heads + j, 0] = keys.astype(jnp.bfloat16)
        kv[owner * heads + j, 1] = values.astype(jnp.bfloat16)

    def project(j):
        both = jnp.dot(
            lat[...].reshape(rows, lat.shape[2])[:, :width], wkv[j], preferred_element_type=jnp.float32
        )
        store(me, j, both[:, :nope], both[:, nope:])

    def project_arrived(owner, j, way):
        some = lat[...].reshape(rows, lat.shape[2])[:, :width]
        slot = way * heads + j
        keys = jnp.dot(some, halves[slot, 0], preferred_element_type=jnp.float32)
        values = jnp.dot(some, halves[slot, 1], preferred_element_type=jnp.float32)
        store(owner, j, keys, values)

    def hand_over(*slots):
        for way, place_in in slots:
            j = (early_r, early_l)[way][place_in]
            half_over(j, way, rep).wait_recv()
            half_over(j, way, rep).start()

    if early:
        late_out(True)
        hand_over((1, 0))

        @pl.when(corner)
        def _():
            lat_take("EGFH")
            lat_meet("EGFH")

        @pl.when(inner)
        def _():
            lat_take("H")
            lat_meet("GH")

        late_out(False)
    else:
        @pl.loop(0, chips_half)
        def _(i):
            relay(far_chip(i))

        @pl.loop(0, chips_half)
        def _(i):
            lat_on(far_chip(i) * cores + other_core).wait_recv()
        for j in late:
            project(j)
            go_right(me, j).start()
            go_left(me, j).start()

    for j in range(early):
        project(j)
    if early:

        @pl.when(corner)
        def _():
            for j in range(early):
                send(me, j, LEFT, mine("C")).start()

        lend_out(4, len(lends))
    for j in range(heads):
        go_across(me, j).start()

    rope_part = lat[...].reshape(rows, lat.shape[2])[:, width:]
    blank = jnp.zeros_like(rope_part)
    ropes[0] = jnp.concatenate([rope_part, blank], axis=1)
    ropes[1] = jnp.concatenate([blank, rope_part], axis=1)

    if not early:
        q_copy.wait()

    lane = lax.broadcasted_iota(jnp.int32, (rows, nope), 1)
    upper = lane >= rope

    def attended(queries, owner, j):
        odd = parity(owner, j)
        head = owner * heads + j
        keys = kv[head, 0]
        values = kv[head, 1]

        def even_keys():
            return jnp.concatenate([keys, ropes[0]], axis=1)

        def odd_keys():
            return jnp.concatenate(
                [jnp.where(upper, keys, jnp.zeros_like(keys)), jnp.where(upper, ropes[1], keys)], axis=1
            )

        if isinstance(odd, int):
            keys_full = odd_keys() if odd else even_keys()
        else:
            keys_full = jnp.where(odd == 1, odd_keys(), even_keys())
        scores = lax.dot_general(
            queries, keys_full, (((1,), (1,)), ((), ())), preferred_element_type=jnp.float32
        )
        row_max = jnp.max(scores, axis=1, keepdims=True)
        weights = jnp.exp2((scores - row_max) * scale)
        total = jnp.sum(weights, axis=1, keepdims=True)
        mixed = jnp.dot(weights.astype(jnp.bfloat16), values, preferred_element_type=jnp.float32)
        return (mixed * (1.0 / total)).astype(jnp.bfloat16)

    def attend(owner, j):
        at = pl.multiple_of((owner * heads + j) * nope, nope)
        o[:, pl.ds(at, nope)] = attended(q[:, pl.ds(query_start(owner, j), 2 * nope)], owner, j)

    attend(me, 0)
    if early:
        hand_over(*[(1, i) for i in range(1, early)], *[(0, i) for i in range(early)])
    for i in range(1, early):
        attend(me, i)
    for j in range(max(early, 1), heads):
        attend(me, j)

    def sent(stream, ref):
        pltpu.make_async_remote_copy(
            src_ref=ref,
            dst_ref=ref,
            send_sem=send_sem.at[stream],
            recv_sem=send_sem.at[stream],
            device_id={"ctx": across},
            device_id_type=MESH,
        ).wait_send()

    def around():
        def others(s):
            return (device_at(place - s, other_core), device_at(place + s, other_core))

        def attend_others(s, pos):
            pair = list(zip(others(s), (order_r, order_l)))
            for owner, js in pair:
                go_across(owner, js[pos]).wait_recv()
            return [(owner, js[pos]) for owner, js in pair]

        def ring_step(s, first, last):
            from_left = device_at(place - s, core)
            from_right = device_at(place + s, core)
            for pos in range(heads):
                jr, jl = order_r[pos], order_l[pos]
                for j, way, owner, go in ((jr, 0, from_left, go_right), (jl, 1, from_right, go_left)):
                    go(owner, j).wait_recv()
                    if not last or pos < (half_right if way == 0 else heads - half_right):
                        go(owner, j).start()
                    go_across(owner, j).start()
                todo = [(from_left, jr), (from_right, jl)]
                if first:
                    go_across(across, pos).wait_recv()
                    todo.append((across, pos))
                if pos > 0:
                    todo += attend_others(s, pos - 1)
                elif not first:
                    todo += attend_others(s - 1, heads - 1)
                for owner, j in todo:
                    attend(owner, j)

        ring_step(1, True, half == 2)
        if half > 3:

            @pl.loop(2, half - 1)
            def _(s):
                ring_step(s, False, False)

        if half > 2:
            ring_step(half - 1, False, True)

        far = device_at(place + half, core)
        far_other = device_at(place + half, other_core)
        todo = attend_others(half - 1, heads - 1)
        for pos in range(half_right):
            arrivals = [(order_r[pos], go_right)]
            if pos < heads - half_right:
                arrivals.append((order_l[pos], go_left))
            for j, go in arrivals:
                go(far, j).wait_recv()
                go_across(far, j).start()
                todo.append((far, j))
            for owner, j in todo:
                attend(owner, j)
            for j, _ in arrivals:
                go_across(far_other, j).wait_recv()
            for j, _ in arrivals:
                attend(far_other, j)
            todo = []

        sent(RIGHT, kv.at[pl.ds(0, (half - 1) * heads + half_right)])
        sent(LEFT, kv.at[pl.ds(0, half * heads - half_right)])
        sent(ACROSS, kv.at[pl.ds(0, chips * heads)])

    def arrived(name, j, way):
        owner = mine(name)
        direct = {0: "B" if name == "B" else "D", 1: "C" if name == "C" else "E", 2: "A"}
        if way is None or name != direct[way]:
            go_across(owner, j).wait_recv()
        elif way == 0 or (way == 1 and j < early):
            half_over(j, way, 1 - rep).wait_recv()
            project_arrived(owner, j, way)
        elif j >= early:
            side = owner // (devices // 2)
            quarters = 3 if way == 1 else 2
            half_hop(owner, j, piece_of(side, quarters, True), True, way, RIGHT, across).wait_recv()
            half_hop(owner, j, piece_of(side, quarters, False), False, way, RIGHT, across).wait_recv()
        else:
            go_across(owner, j).wait_recv()

    def later_hands(k):
        if k in (0, 2):
            hand_over((0, early + k // 2))

    def follow(name, j):
        owner = chip_of(name, other_core)
        go_across(owner, j).wait_recv()
        return owner, j

    def at_corner():
        events = [[("C", j, 1)] for j in order_l]
        for jz, jy in zip(order_l, order_r):
            events.append([("E", jz, None), ("D", jz, None), ("B", jy, 0)])
        for k in range(heads):
            events.append([("G", j, None) for j in keep[k : k + 1]] + [("F", order_l[k], None)])
        events.append([("H", order_a[3], None)])
        lag = []
        for k, now in enumerate(events):
            for name, j, way in now:
                arrived(name, j, way)
                if name in "CE" or (name == "G" and j == order_a[3]):
                    send(mine(name), j, RIGHT, beside).start()
                go_across(mine(name), j).start()
            later_hands(k)
            todo = [(mine(name), j) for name, j, _ in now]
            if k < heads:
                go_across(across, k).wait_recv()
                todo.append((across, k))
            todo += [follow(name, j) for name, j in lag]
            for owner, j in todo:
                attend(owner, j)
            lag = [(name, j) for name, j, _ in now]
        for name, j in lag:
            attend(*follow(name, j))
        pltpu.make_async_copy(mixed_out, mixed_out, lend_sem.at[1]).wait()
        sent(RIGHT, kv.at[pl.ds(0, 2 * heads + 1)])
        sent(LAT_OUT, lat.at[pl.ds(0, 4)])
        sent(LEFT, kv.at[pl.ds(0, heads)])
        sent(ACROSS, kv.at[pl.ds(0, 6 * heads + len(keep) + 1)])
        sent(LEND, lent)

    def at_inner():
        events = []
        for k in range(heads):
            events.append([("E", order_l[k], 1), ("A", order_a[k], 2)])
        events[heads - 1].append(("F", order_l[0], None))
        for k in range(heads):
            events.append([("B", order_a[k], None), ("G", order_a[k], None), ("D", order_r[k], 0)])
        for k in range(heads):
            events.append([("H", order_a[k], None)])
            if k > 0:
                events[-1].append(("F", order_l[k], None))
            if k == heads - 2:
                events.append([])
        lag = []
        held = []
        for k, now in enumerate(events):
            for name, j, way in now:
                arrived(name, j, way)
                if name == "A":
                    send(mine("A"), j, MID, mine("E")).start()
                    send(mine("A"), j, RIGHT, beside).start()
                elif name == "B":
                    send(mine("B"), j, MID, mine("E")).start()
                elif name == "E":
                    send(mine("E"), j, LEFT, mine("A")).start()
                    if j == order_l[0]:
                        send(mine("E"), j, RIGHT, beside).start()
                elif name == "G" and j in keep:
                    send(mine("G"), j, LEFT, mine("A")).start()
                go_across(mine(name), j).start()
            for name, j, _ in now:
                if name == "H" and j == ship[0]:
                    rest = lent.at[pl.ds(4, len(lends) - 4)]
                    pltpu.make_async_copy(rest, rest, lend_sem.at[2]).wait()
                if name == "H" and j in ship:
                    give_back(name, j, core).start()
            later_hands(k)
            if k == heads - 1:
                for j in order_l[1:]:
                    send(mine("E"), j, RIGHT, beside).start()
            todo = [(mine(name), j) for name, j, _ in now]
            if k < heads:
                go_across(across, k).wait_recv()
                todo.append((across, k))
            todo += [follow(name, j) for name, j in lag]
            back = []
            if ("G", order_a[1]) in lag:
                pltpu.make_async_copy(lent.at[pl.ds(0, 4)], lent.at[pl.ds(0, 4)], lend_sem.at[0]).wait()
            for name, j in lag:
                if (name, 0, j) in lends:
                    back += [give_back(name, j, which) for which in ((core, other_core) if name == "G" else (other_core,))]
            for copy in back:
                copy.start()
            held += todo
            if events[k + 1 : k + 2] != [[]]:
                for owner, j in held:
                    attend(owner, j)
                held = []
            lag = [(name, j) for name, j, _ in now]
        for name, j in lag:
            attend(*follow(name, j))
        sent(RIGHT, kv.at[pl.ds(0, 2 * heads)])
        sent(LAT_OUT, lat.at[pl.ds(0, 10)])
        sent(LEFT, kv.at[pl.ds(0, heads - early + heads + len(keep))])
        sent(MID, kv.at[pl.ds(0, heads - early + 2 * heads)])
        sent(ACROSS, kv.at[pl.ds(0, 8 * heads)])
        sent(HALF_L, halves.at[pl.ds(0, 2 * early), 0])
        sent(LEND, mixed_out)

    if early:
        pl.when(corner)(at_corner)
        pl.when(inner)(at_inner)
        sent(HALF_R, halves.at[pl.ds(0, heads), 0])
        sent(HALF_X, halves.at[pl.ds(0, heads + early), 0])
    else:
        around()
        sent(LAT_OUT, lat.at[pl.ds(0, chips - 1)])
    sent(LAT_ON, lat.at[pl.ds(0, chips)])


def on_device(grid_y, cores, early, queries, latents, w_key, w_value):
    devices = lax.axis_size("ctx")
    heads, width, nope = w_key.shape
    query_rows = queries.shape[0]
    block = latents.shape[0]
    rows = block * devices
    anywhere = pl.BlockSpec(memory_space=pl.ANY)
    dma = pltpu.SemaphoreType.DMA
    return pl.pallas_call(
        functools.partial(kernel, grid_y, cores, early),
        out_shape=jax.ShapeDtypeStruct((query_rows, devices * heads * nope), jnp.bfloat16),
        in_specs=[anywhere] * 4,
        out_specs=pl.BlockSpec(memory_space=pltpu.VMEM),
        scratch_shapes=[
            pltpu.VMEM(queries.shape, jnp.bfloat16),
            pltpu.VMEM((devices, block, latents.shape[1]), jnp.bfloat16),
            pltpu.VMEM((heads, width, 2 * nope), jnp.bfloat16),
            pltpu.VMEM((2, rows, nope), jnp.bfloat16),
            pltpu.VMEM((devices * heads, 2, rows, nope), jnp.bfloat16),
            pltpu.VMEM((heads + early if early else 1, 2, width, nope), jnp.bfloat16),
            dma((3,)),
            dma((devices,)),
            dma((devices * heads,)),
            dma((heads + early if early else 1, 2)),
            dma((10,)),
            dma((2, max(heads - early, 1))),
            pltpu.VMEM((10 if early else 1, query_rows, 2 * nope), jnp.bfloat16),
            pltpu.VMEM((10 if early else 1, query_rows, nope), jnp.bfloat16),
            dma((3,)),
        ],
        compiler_params=pltpu.CompilerParams(
            collective_id=0, has_side_effects=True, vmem_limit_bytes=50 * 1024 * 1024
        ),
    )(*(pltpu.with_memory_space_constraint(a, pltpu.HBM) for a in (queries, latents, w_key, w_value)))


def layout_of(mesh):
    group = list(mesh.devices.reshape(-1, mesh.shape["ctx"])[0])
    places = [tuple(d.coords) for d in group]
    chips = sorted(set(places))
    cores = len(group) // len(chips)
    varied = [axis for axis in range(3) if len({c[axis] for c in chips}) > 1]
    grid_y = 1
    if len(varied) == 2:
        fast = len({c[varied[0]] for c in chips})
        grid_y = 2 if fast == 2 else 1
    return grid_y, cores


def solution(mesh):
    grid_y, cores = layout_of(mesh)
    chips = mesh.shape["ctx"] // cores
    early = 2 if mesh.shape["rep"] == 2 and grid_y == 2 and chips // grid_y == 4 and cores == 2 else 0
    return jax.shard_map(
        functools.partial(on_device, grid_y, cores, early),
        mesh=mesh,
        in_specs=(
            P(("rep", "ctx"), None),
            P(("rep", "ctx"), None),
            P("ctx", None, None),
            P("ctx", None, None),
        ),
        out_specs=P(("rep", "ctx"), None),
        check_vma=False,
    )
```
